256 devices in a mesh: ctx: 64 (over y, z, core), ch: 4 (over x).
Axes of the slice: x: 4, y: 4, z: 8, core: 2. Of those that a mesh axis runs over, the one named last changes fastest.
Arguments:
- gate_medium: bfloat16 [16384, 8192], P('ctx', 'ch'), may hold values from -6 to 6
- key_medium: bfloat16 [16384, 8192], P('ctx', 'ch'), may hold values from -6 to 6
- value_medium: bfloat16 [16384, 8192], P('ctx', 'ch'), may hold values from -16 to 16
- short_medium: float32 [3, 3, 8192], P(None, None, 'ch'), may hold values from -3.5 to 3.5
- filter_medium: float32 [128, 8192], P(None, 'ch'), may hold values from -2 to 2
- skip_medium: float32 [8192], P('ch'), may hold values from -4 to 4
- norm_gain: float32 [8192], P('ch'), may hold values from 0.5 to 1.5
- gate_long: bfloat16 [16384, 8192], P('ctx', 'ch'), may hold values from -6 to 6
- key_long: bfloat16 [16384, 8192], P('ctx', 'ch'), may hold values from -6 to 6
- short_long: float32 [3, 3, 8192], P(None, None, 'ch'), may hold values from -3.5 to 3.5
- decay_rates: float32 [16, 8192], P(None, 'ch'), may hold values from 6.1035156e-07 to 0.0625
- residues: float32 [16, 8192], P(None, 'ch'), may hold values from -1.5 to 1.5
- skip_long: float32 [8192], P('ch'), may hold values from -4 to 4
Outputs:
- mixed_medium: bfloat16 [16384, 8192], P('ctx', 'ch')
- mixed_long: bfloat16 [16384, 8192], P('ctx', 'ch')
The draws below stay inside these ranges and needn't reach their ends.
All inputs are finite; a program needn't handle non-finite values.
Results may differ from the reference program's by a relative error of at most 0.0095.
Values may be sent and summed in bfloat16 or wider, within the bound.
A program may use at most 64 MiB of HBM per device.

```python
import math
import jax
import jax.numpy as jnp
from jax import lax

D = 8192
TAPS_MR = 128
MODES = 16
TOKENS = 16384


def draw_value_medium(key, part):
    first, second = jax.random.split(key)
    base = jnp.clip(jax.random.normal(first, (TOKENS, D), jnp.float32), -4.0, 4.0)
    spread = jax.random.uniform(second, (TOKENS, 1), jnp.float32, -0.5, 0.5)
    return (base * jnp.power(10.0, spread)).astype(jnp.bfloat16)


def draw_filter_medium(key, part):
    first, second = jax.random.split(key)
    column = jnp.arange(D).astype(jnp.float32) / D
    level = jax.random.uniform(second, (1, D), jnp.float32)
    base = jnp.clip(jax.random.normal(first, (TAPS_MR, D), jnp.float32), -4.0, 4.0)
    rise = jnp.power(3.0, column - 0.5)
    return base * rise[None, :] * jnp.power(10.0, level - 0.5) / math.sqrt(TAPS_MR)


def draw_decay_rates(key, part):
    first = jax.random.fold_in(key, 0)
    lowest = math.log(0.01 / TOKENS)
    highest = math.log(0.0625)
    level = jax.random.uniform(first, (MODES, D), jnp.float32)
    logs = lowest + level * (highest - lowest)
    return jnp.clip(jnp.exp(logs), 0.01 / TOKENS, 0.0625)


def block_scale(key, dims, cuts, low, top_value):
    def one(axis_at, parts):
        heights = jax.random.uniform(jax.random.fold_in(jax.random.fold_in(key, 6), axis_at), (parts,), jnp.float32, low / len(cuts), top_value / len(cuts))
        return jnp.repeat(jnp.exp(heights), dims[axis_at] // parts).reshape((-1,) + (1,) * (len(dims) - axis_at - 1))

    factor_of = one(*cuts[0])
    for cut in cuts[1:]:
        factor_of = factor_of * one(*cut)
    return factor_of


def noise(rng, shape, scale, bound, cuts=(), held_as=jnp.bfloat16):
    factor_of = block_scale(rng, shape, cuts, -0.22, 0.18) if cuts else 1.0
    values = jax.random.normal(rng, shape, jnp.float32) * scale * factor_of
    return jnp.minimum(jnp.maximum(values, -bound), bound).astype(held_as)


def setup_inputs(seed: int = 0) -> dict:
    key_of = jax.random.split(jax.random.key(seed), 14)
    return {
        "gate_medium": noise(key_of[0], (TOKENS, D), 1.0, 6.0, ((0, 64), (1, 4))),
        "key_medium": noise(key_of[1], (TOKENS, D), 1.0, 6.0, ((0, 64), (1, 4))),
        "value_medium": draw_value_medium(jax.random.fold_in(key_of[13], 71), 0),
        "short_medium": noise(key_of[3], (3, 3, D), 3 ** -0.5, 3.5, ((2, 4),), jnp.float32),
        "filter_medium": draw_filter_medium(jax.random.fold_in(key_of[13], 71), 0),
        "skip_medium": noise(key_of[5], (D,), 1.0, 4.0, ((0, 4),), jnp.float32),
        "norm_gain": jnp.clip(1.0 + 0.1 * jax.random.normal(key_of[6], (D,), jnp.float32), 0.5, 1.5),
        "gate_long": noise(key_of[7], (TOKENS, D), 1.0, 6.0, ((0, 64), (1, 4))),
        "key_long": noise(key_of[8], (TOKENS, D), 1.0, 6.0, ((0, 64), (1, 4))),
        "short_long": noise(key_of[9], (3, 3, D), 3 ** -0.5, 3.5, ((2, 4),), jnp.float32),
        "decay_rates": draw_decay_rates(jax.random.fold_in(key_of[13], 71), 0),
        "residues": noise(key_of[11], (MODES, D), 0.25, 1.5, ((1, 4),), jnp.float32),
        "skip_long": noise(key_of[12], (D,), 1.0, 4.0, ((0, 4),), jnp.float32),
    }


def short_filter(extended, weights):
    return weights[0] * extended[2:] + weights[1] * extended[1:-1] + weights[2] * extended[:-2]

def front_pad(values, count):
    return jnp.pad(values, ((count, 0), (0, 0)))

def split_channels(values, groups):
    shaped = values.reshape(values.shape[:-1] + (groups, values.shape[-1] // groups))
    return jnp.moveaxis(shaped, -2, 0)

def merge_channels(values):
    moved = jnp.moveaxis(values, 0, -2)
    return moved.reshape(moved.shape[:-2] + (moved.shape[-2] * moved.shape[-1],))

def medium_operator(pieces):
    gate_medium, key_medium, value_medium, short_medium, filter_medium, skip_medium = pieces
    tap_count = filter_medium.shape[0]
    filtered_gate = short_filter(front_pad(gate_medium, 2), short_medium[0])
    filtered_key = short_filter(front_pad(key_medium, 2), short_medium[1])
    filtered_value = short_filter(front_pad(value_medium, 2), short_medium[2])
    product = (filtered_key * filtered_value).astype(jnp.bfloat16)
    padded = front_pad(product, tap_count - 1)

    def add_tap(offset, total):
        start = jnp.asarray(tap_count - 1 - offset).astype(jnp.int32)
        piece = lax.dynamic_slice_in_dim(padded, start, TOKENS, 0)
        weight = lax.dynamic_index_in_dim(filter_medium, jnp.asarray(offset).astype(jnp.int32), 0, keepdims=False)
        return total + weight * piece
    conv = lax.fori_loop(0, tap_count, add_tap, jnp.zeros(product.shape, jnp.float32))
    conv = conv + skip_medium * product
    return (filtered_gate * conv).astype(jnp.bfloat16)

def long_operator(pieces):
    gate_long, key_long, normed, short_long, decay_rates, residues, skip_long = pieces
    block_rows = 64
    block_count = TOKENS // block_rows
    width = gate_long.shape[1]
    filtered_gate = short_filter(front_pad(gate_long, 2), short_long[0])
    filtered_key = short_filter(front_pad(key_long, 2), short_long[1])
    filtered_value = short_filter(front_pad(normed, 2), short_long[2])
    product = (filtered_key * filtered_value).astype(jnp.bfloat16)
    positions = jnp.arange(block_rows).astype(jnp.float32)
    mode_weight = residues * jnp.sqrt(-jnp.expm1(-2.0 * decay_rates))
    rates_wide = decay_rates[:, None, :]
    to_end = jnp.exp(-rates_wide * (block_rows - 1.0 - positions)[None, :, None])
    from_start = mode_weight[:, None, :] * jnp.exp(-rates_wide * (positions + 1.0)[None, :, None])
    impulse = lax.optimization_barrier(jnp.sum(mode_weight[:, None, :] * jnp.exp(-rates_wide * positions[None, :, None]), axis=0))
    blocks = product.reshape(block_count, block_rows, width)
    padded = jnp.pad(blocks, ((0, 0), (block_rows - 1, 0), (0, 0)))

    def add_tap(offset, total):
        start = jnp.asarray(block_rows - 1 - offset).astype(jnp.int32)
        piece = lax.dynamic_slice_in_dim(padded, start, block_rows, 1)
        weight = lax.dynamic_index_in_dim(impulse, jnp.asarray(offset).astype(jnp.int32), 0, keepdims=False)
        return total + weight * piece
    inner = lax.fori_loop(0, block_rows, add_tap, jnp.zeros(blocks.shape, jnp.float32))
    ends = jnp.einsum('bsc,msc->bmc', blocks.astype(jnp.float32), to_end, precision=lax.Precision.HIGHEST)
    block_decay = jnp.exp(-decay_rates * block_rows)

    def advance(state, end):
        return (block_decay * state + end, state)
    final_state, starts = lax.scan(advance, jnp.zeros(decay_rates.shape, jnp.float32), ends)
    outer = jnp.einsum('bmc,msc->bsc', starts, from_start, precision=lax.Precision.HIGHEST)
    conv = (inner + outer).reshape(TOKENS, width) + skip_long * product
    return (filtered_gate * conv).astype(jnp.bfloat16)

def reference(gate_medium, key_medium, value_medium, short_medium, filter_medium, skip_medium, norm_gain, gate_long, key_long, short_long, decay_rates, residues, skip_long):
    groups = D // 1024 if D % 1024 == 0 else 1
    medium_parts = lax.map(medium_operator, (split_channels(gate_medium, groups), split_channels(key_medium, groups), split_channels(value_medium, groups), split_channels(short_medium, groups), split_channels(filter_medium, groups), split_channels(skip_medium, groups)))
    mixed_medium = merge_channels(medium_parts)
    mean_square = lax.optimization_barrier(jnp.mean(jnp.square(mixed_medium.astype(jnp.float32)), axis=1))
    normed = (mixed_medium * norm_gain * lax.rsqrt(mean_square + 1e-06)[:, None]).astype(jnp.bfloat16)
    long_parts = lax.map(long_operator, (split_channels(gate_long, groups), split_channels(key_long, groups), split_channels(normed, groups), split_channels(short_long, groups), split_channels(decay_rates, groups), split_channels(residues, groups), split_channels(skip_long, groups)))
    mixed_long = merge_channels(long_parts)
    return (mixed_medium, mixed_long)
```

```python
import jax
import jax.numpy as jnp
from jax import lax
from jax.sharding import PartitionSpec as P
from jax.experimental import pallas as pl
from jax.experimental.pallas import tpu as pltpu

TAPS = 128
SUB = 128
RB = 8


def medium_kernel(ext_ref, f_ref, skip_ref, gate_ref, out_ref, ss_ref, q_ref):
    rows = out_ref.shape[0]
    width = out_ref.shape[1]
    span = ext_ref.shape[0]

    @pl.when(pl.program_id(0) == 0)
    def _():
        ss_ref[...] = jnp.zeros_like(ss_ref)

    for h in range(width // SUB):
        lanes = pl.ds(h * SUB, SUB)
        ext = ext_ref[:, lanes].astype(jnp.float32)
        for b in range(8):
            q_ref[b, 8:, :] = ext[8 - b : span - b]

        def block(kb, carry):
            acc = [jnp.zeros((8, SUB), jnp.float32) for _ in range(RB)]
            start = pl.multiple_of(kb * (8 * RB) + 8, 8)
            for b in range(8):
                qv = q_ref[b, pl.ds(start, 8 * (RB + 15)), :]
                for a in range(16):
                    w = jnp.broadcast_to(f_ref[pl.ds(8 * a + b, 1), lanes], (8, SUB))
                    for kk in range(RB):
                        v = kk + 15 - a
                        acc[kk] = acc[kk] + w * qv[8 * v : 8 * v + 8]
            skip = jnp.broadcast_to(skip_ref[:, lanes], (8, SUB))
            for kk in range(RB):
                row = pl.multiple_of(kb * (8 * RB) + 8 * kk, 8)
                own = q_ref[0, pl.ds(row + TAPS, 8), :]
                conv = acc[kk] + skip * own
                mixed = (gate_ref[pl.ds(row, 8), lanes] * conv).astype(jnp.bfloat16)
                out_ref[pl.ds(row, 8), lanes] = mixed
                m = mixed.astype(jnp.float32)
                ss_ref[pl.ds(row, 8), :] += m * m
            return carry

        lax.fori_loop(0, rows // (8 * RB), block, 0)


def medium_call(ext, taps, skip, gate_feat, block=512, interpret=False):
    span, width = ext.shape
    rows = gate_feat.shape[0]
    grid = (width // block,)
    return pl.pallas_call(
        medium_kernel,
        grid=grid,
        in_specs=[
            pl.BlockSpec((span, block), lambda i: (0, i)),
            pl.BlockSpec((TAPS, block), lambda i: (0, i)),
            pl.BlockSpec((1, block), lambda i: (0, i)),
            pl.BlockSpec((rows, block), lambda i: (0, i)),
        ],
        out_specs=[
            pl.BlockSpec((rows, block), lambda i: (0, i)),
            pl.BlockSpec((rows, SUB), lambda i: (0, 0)),
        ],
        out_shape=[
            jax.ShapeDtypeStruct((rows, width), jnp.bfloat16),
            jax.ShapeDtypeStruct((rows, SUB), jnp.float32),
        ],
        scratch_shapes=[pltpu.VMEM((8, span, SUB), jnp.float32)],
        compiler_params=pltpu.CompilerParams(dimension_semantics=("arbitrary",)),
        interpret=interpret,
    )(ext, taps, skip, gate_feat)

D = 8192


def passed_along(value, axis, steps):
    count = lax.axis_size(axis)
    first, last = (max(0, -steps), min(count, count - steps))
    return lax.ppermute(value, axis, [(source, source + steps) for source in range(first, last)])


def short_filter(extended, weights):
    return weights[0] * extended[2:] + weights[1] * extended[1:-1] + weights[2] * extended[:-2]


def medium_conv(extended, taps, row_count):
    tap_count = taps.shape[0]
    total = jnp.zeros((row_count, taps.shape[1]), jnp.float32)
    for offset in range(tap_count):
        start = tap_count - 1 - offset
        total = total + taps[offset] * extended[start : start + row_count]
    return total


def body(
    gate_medium,
    key_medium,
    value_medium,
    short_medium,
    filter_medium,
    skip_medium,
    norm_gain,
    gate_long,
    key_long,
    short_long,
    decay_rates,
    residues,
    skip_long,
):
    row_count = gate_medium.shape[0]
    tap_count = filter_medium.shape[0]
    width_local = gate_medium.shape[1]
    late_product = (
        short_filter(key_medium, short_medium[1]) * short_filter(value_medium, short_medium[2])
    ).astype(jnp.bfloat16)
    rim_gate, rim_key, rim_value, rim_product = passed_along(
        (gate_medium[-2:], key_medium[-2:], value_medium[-2:], late_product[-(tap_count - 1) :]),
        "ctx",
        1,
    )
    head_key = short_filter(jnp.concatenate([rim_key, key_medium[:2]], 0), short_medium[1])
    head_value = short_filter(jnp.concatenate([rim_value, value_medium[:2]], 0), short_medium[2])
    head_product = (head_key * head_value).astype(jnp.bfloat16)
    product = jnp.concatenate([rim_product, head_product, late_product], 0)
    gate_feat = short_filter(jnp.concatenate([rim_gate, gate_medium], 0), short_medium[0])
    extended = jnp.concatenate([jnp.zeros((1, width_local), jnp.bfloat16), product], 0)
    mixed_medium, partial_squares = medium_call(
        extended, filter_medium, skip_medium[None, :], gate_feat
    )
    squares = jnp.sum(partial_squares, axis=1)
    total_squares = lax.psum(squares, "ch")
    inverse = lax.rsqrt(total_squares / D + 1e-06)
    normed = (mixed_medium * norm_gain * inverse[:, None]).astype(jnp.bfloat16)
    rim_gate_long, rim_key_long, rim_normed = passed_along(
        (gate_long[-2:], key_long[-2:], normed[-2:]), "ctx", 1
    )
    gate_feat_long = short_filter(jnp.concatenate([rim_gate_long, gate_long], 0), short_long[0])
    key_feat_long = short_filter(jnp.concatenate([rim_key_long, key_long], 0), short_long[1])
    value_feat_long = short_filter(jnp.concatenate([rim_normed, normed], 0), short_long[2])
    product_long = (key_feat_long * value_feat_long).astype(jnp.bfloat16)
    block_rows = 64
    block_count = row_count // block_rows
    positions = jnp.arange(block_rows).astype(jnp.float32)
    mode_weight = residues * jnp.sqrt(-jnp.expm1(-2.0 * decay_rates))
    rates_wide = decay_rates[:, None, :]
    to_end = jnp.exp(-rates_wide * (block_rows - 1.0 - positions)[None, :, None])
    from_start = mode_weight[:, None, :] * jnp.exp(-rates_wide * (positions + 1.0)[None, :, None])
    impulse = jnp.sum(
        mode_weight[:, None, :] * jnp.exp(-rates_wide * positions[None, :, None]), axis=0
    )
    blocks = product_long.reshape(block_count, block_rows, width_local)
    padded = jnp.pad(blocks, ((0, 0), (block_rows - 1, 0), (0, 0)))
    inner = jnp.zeros(blocks.shape, jnp.float32)
    for offset in range(block_rows):
        start = block_rows - 1 - offset
        inner = inner + impulse[offset] * padded[:, start : start + block_rows]
    ends = jnp.einsum(
        "bsc,msc->bmc", blocks.astype(jnp.float32), to_end, precision=lax.Precision.HIGHEST
    )
    block_decay = jnp.exp(-decay_rates * block_rows)

    def advance(state, end):
        return (block_decay * state + end, state)

    final_state, starts = lax.scan(advance, jnp.zeros(decay_rates.shape, jnp.float32), ends)
    position = lax.axis_index("ctx")
    piece = lax.all_gather(
        final_state[None].astype(jnp.bfloat16), "ctx", axis=0, tiled=True
    ).astype(jnp.float32)
    count = piece.shape[0]
    gaps = (position - 1 - jnp.arange(count, dtype=jnp.int32)).astype(jnp.float32)
    factors = jnp.where(
        gaps[:, None, None] >= 0.0,
        jnp.exp(-decay_rates[None] * row_count * jnp.maximum(gaps, 0.0)[:, None, None]),
        0.0,
    )
    incoming = jnp.zeros_like(final_state) + jnp.sum(factors * piece, axis=0)
    lead = jnp.exp(
        -decay_rates[None]
        * (block_rows * jnp.arange(block_count).astype(jnp.float32))[:, None, None]
    )
    states = starts + lead * incoming[None]
    outer = jnp.einsum("bmc,msc->bsc", states, from_start, precision=lax.Precision.HIGHEST)
    conv_long = (inner + outer).reshape(row_count, width_local) + skip_long * product_long
    mixed_long = (gate_feat_long * conv_long).astype(jnp.bfloat16)
    return (mixed_medium, mixed_long)


def solution(mesh):
    placed = (
        P("ctx", "ch"),
        P("ctx", "ch"),
        P("ctx", "ch"),
        P(None, None, "ch"),
        P(None, "ch"),
        P("ch"),
        P("ch"),
        P("ctx", "ch"),
        P("ctx", "ch"),
        P(None, None, "ch"),
        P(None, "ch"),
        P(None, "ch"),
        P("ch"),
    )
    return jax.shard_map(
        body,
        mesh=mesh,
        in_specs=placed,
        out_specs=(P("ctx", "ch"), P("ctx", "ch")),
        check_vma=False,
    )
```

```python
import jax
import jax.numpy as jnp
from jax import lax
from jax.sharding import PartitionSpec as P
from jax.experimental import pallas as pl
from jax.experimental.pallas import tpu as pltpu

TAPS = 128
SUB = 128
RB = 8


def medium_kernel(ext_ref, f_ref, skip_ref, gate_ref, out_ref, ss_ref, q_ref):
    rows = out_ref.shape[0]
    width = out_ref.shape[1]
    span = ext_ref.shape[0]

    @pl.when(pl.program_id(0) == 0)
    def _():
        ss_ref[...] = jnp.zeros_like(ss_ref)

    for h in range(width // SUB):
        lanes = pl.ds(h * SUB, SUB)
        ext = ext_ref[:, lanes].astype(jnp.float32)
        for b in range(8):
            q_ref[b, 8:, :] = ext[8 - b : span - b]

        def block(kb, carry):
            acc = [jnp.zeros((8, SUB), jnp.float32) for _ in range(RB)]
            start = pl.multiple_of(kb * (8 * RB) + 8, 8)
            for b in range(8):
                qv = q_ref[b, pl.ds(start, 8 * (RB + 15)), :]
                for a in range(16):
                    w = jnp.broadcast_to(f_ref[pl.ds(8 * a + b, 1), lanes], (8, SUB))
                    for kk in range(RB):
                        v = kk + 15 - a
                        acc[kk] = acc[kk] + w * qv[8 * v : 8 * v + 8]
            skip = jnp.broadcast_to(skip_ref[:, lanes], (8, SUB))
            for kk in range(RB):
                row = pl.multiple_of(kb * (8 * RB) + 8 * kk, 8)
                own = q_ref[0, pl.ds(row + TAPS, 8), :]
                conv = acc[kk] + skip * own
                mixed = (gate_ref[pl.ds(row, 8), lanes] * conv).astype(jnp.bfloat16)
                out_ref[pl.ds(row, 8), lanes] = mixed
                m = mixed.astype(jnp.float32)
                ss_ref[pl.ds(row, 8), :] += m * m
            return carry

        lax.fori_loop(0, rows // (8 * RB), block, 0)


def medium_call(ext, taps, skip, gate_feat, block=512, interpret=False):
    span, width = ext.shape
    rows = gate_feat.shape[0]
    grid = (width // block,)
    return pl.pallas_call(
        medium_kernel,
        grid=grid,
        in_specs=[
            pl.BlockSpec((span, block), lambda i: (0, i)),
            pl.BlockSpec((TAPS, block), lambda i: (0, i)),
            pl.BlockSpec((1, block), lambda i: (0, i)),
            pl.BlockSpec((rows, block), lambda i: (0, i)),
        ],
        out_specs=[
            pl.BlockSpec((rows, block), lambda i: (0, i)),
            pl.BlockSpec((rows, SUB), lambda i: (0, 0)),
        ],
        out_shape=[
            jax.ShapeDtypeStruct((rows, width), jnp.bfloat16),
            jax.ShapeDtypeStruct((rows, SUB), jnp.float32),
        ],
        scratch_shapes=[pltpu.VMEM((8, span, SUB), jnp.float32)],
        compiler_params=pltpu.CompilerParams(dimension_semantics=("arbitrary",)),
        interpret=interpret,
    )(ext, taps, skip, gate_feat)

D = 8192


LANE = 128
GROUP = 4
MODES_HALF = 8


def _rows_to_f32(p_ref, pf_ref):
    pf_ref[...] = p_ref[...].astype(jnp.float32)


def modal_end_kernel(p_ref, e_ref, out_ref, pf_ref):
    rows = p_ref.shape[0]
    _rows_to_f32(p_ref, pf_ref)
    lanes = [pl.ds(g * LANE, LANE) for g in range(GROUP)]
    e_lo = [e_ref[0:8, ln] for ln in lanes]
    e_hi = [e_ref[8:16, ln] for ln in lanes]

    def step(i, carry):
        lo, hi = carry
        row = pl.multiple_of(i * 8, 8)
        blocks = [pf_ref[pl.ds(row, 8), ln] for ln in lanes]
        for j in range(8):
            new_lo, new_hi = [], []
            for g in range(GROUP):
                pb = jnp.broadcast_to(blocks[g][j : j + 1], (8, LANE))
                new_lo.append(e_lo[g] * lo[g] + pb)
                new_hi.append(e_hi[g] * hi[g] + pb)
            lo, hi = new_lo, new_hi
        return lo, hi

    zero = [jnp.zeros((8, LANE), jnp.float32) for _ in range(GROUP)]
    lo, hi = lax.fori_loop(0, rows // 8, step, (zero, list(zero)))
    for g, ln in enumerate(lanes):
        out_ref[0:8, ln] = lo[g]
        out_ref[8:16, ln] = hi[g]


def modal_end_call(product, decay):
    rows, width = product.shape
    block = LANE * GROUP
    return pl.pallas_call(
        modal_end_kernel,
        grid=(width // block,),
        in_specs=[
            pl.BlockSpec((rows, block), lambda i: (0, i)),
            pl.BlockSpec((16, block), lambda i: (0, i)),
        ],
        out_specs=pl.BlockSpec((16, block), lambda i: (0, i)),
        out_shape=jax.ShapeDtypeStruct((16, width), jnp.float32),
        scratch_shapes=[pltpu.VMEM((rows, block), jnp.float32)],
    )(product, decay)


def modal_out_kernel(p_ref, e_ref, w_ref, s_ref, skip_ref, gate_ref, out_ref, pf_ref, z_ref):
    rows = p_ref.shape[0]
    _rows_to_f32(p_ref, pf_ref)
    lanes = [pl.ds(g * LANE, LANE) for g in range(GROUP)]
    e_lo = [e_ref[0:8, ln] for ln in lanes]
    e_hi = [e_ref[8:16, ln] for ln in lanes]
    w_lo = [w_ref[0:8, ln] for ln in lanes]
    w_hi = [w_ref[8:16, ln] for ln in lanes]

    def step(i, carry):
        lo, hi = carry
        row = pl.multiple_of(i * 8, 8)
        blocks = [pf_ref[pl.ds(row, 8), ln] for ln in lanes]
        for j in range(8):
            new_lo, new_hi = [], []
            for g in range(GROUP):
                pb = jnp.broadcast_to(blocks[g][j : j + 1], (8, LANE))
                a = e_lo[g] * lo[g] + pb
                b = e_hi[g] * hi[g] + pb
                z_ref[g, pl.ds(pl.multiple_of(i * 64 + 8 * j, 8), 8), :] = w_lo[g] * a + w_hi[g] * b
                new_lo.append(a)
                new_hi.append(b)
            lo, hi = new_lo, new_hi
        return lo, hi

    init_lo = [s_ref[0:8, ln] for ln in lanes]
    init_hi = [s_ref[8:16, ln] for ln in lanes]
    lax.fori_loop(0, rows // 8, step, (init_lo, init_hi))

    def reduce(i, carry):
        row = pl.multiple_of(i * 8, 8)
        for g, ln in enumerate(lanes):
            total = z_ref[g, pl.ds(i * 64, 8, stride=8), :]
            for j in range(1, 8):
                total = total + z_ref[g, pl.ds(i * 64 + j, 8, stride=8), :]
            own = pf_ref[pl.ds(row, 8), ln]
            skip = jnp.broadcast_to(skip_ref[:, ln], (8, LANE))
            conv = total + skip * own
            out_ref[pl.ds(row, 8), ln] = (gate_ref[pl.ds(row, 8), ln] * conv).astype(out_ref.dtype)
        return carry

    lax.fori_loop(0, rows // 8, reduce, 0)


def modal_out_call(product, decay, weight, start, skip, gate_feat):
    rows, width = product.shape
    block = LANE * GROUP
    return pl.pallas_call(
        modal_out_kernel,
        grid=(width // block,),
        in_specs=[
            pl.BlockSpec((rows, block), lambda i: (0, i)),
            pl.BlockSpec((16, block), lambda i: (0, i)),
            pl.BlockSpec((16, block), lambda i: (0, i)),
            pl.BlockSpec((16, block), lambda i: (0, i)),
            pl.BlockSpec((1, block), lambda i: (0, i)),
            pl.BlockSpec((rows, block), lambda i: (0, i)),
        ],
        out_specs=pl.BlockSpec((rows, block), lambda i: (0, i)),
        out_shape=jax.ShapeDtypeStruct((rows, width), jnp.bfloat16),
        scratch_shapes=[
            pltpu.VMEM((rows, block), jnp.float32),
            pltpu.VMEM((GROUP, rows * 8, LANE), jnp.float32),
        ],
    )(product, decay, weight, start, skip, gate_feat)


def passed_along(value, axis, steps):
    count = lax.axis_size(axis)
    first, last = (max(0, -steps), min(count, count - steps))
    return lax.ppermute(value, axis, [(source, source + steps) for source in range(first, last)])


def short_filter(extended, weights):
    return weights[0] * extended[2:] + weights[1] * extended[1:-1] + weights[2] * extended[:-2]


def medium_conv(extended, taps, row_count):
    tap_count = taps.shape[0]
    total = jnp.zeros((row_count, taps.shape[1]), jnp.float32)
    for offset in range(tap_count):
        start = tap_count - 1 - offset
        total = total + taps[offset] * extended[start : start + row_count]
    return total


def body(
    gate_medium,
    key_medium,
    value_medium,
    short_medium,
    filter_medium,
    skip_medium,
    norm_gain,
    gate_long,
    key_long,
    short_long,
    decay_rates,
    residues,
    skip_long,
):
    row_count = gate_medium.shape[0]
    tap_count = filter_medium.shape[0]
    width_local = gate_medium.shape[1]
    late_product = (
        short_filter(key_medium, short_medium[1]) * short_filter(value_medium, short_medium[2])
    ).astype(jnp.bfloat16)
    rim_gate, rim_key, rim_value, rim_product = passed_along(
        (gate_medium[-2:], key_medium[-2:], value_medium[-2:], late_product[-(tap_count - 1) :]),
        "ctx",
        1,
    )
    head_key = short_filter(jnp.concatenate([rim_key, key_medium[:2]], 0), short_medium[1])
    head_value = short_filter(jnp.concatenate([rim_value, value_medium[:2]], 0), short_medium[2])
    head_product = (head_key * head_value).astype(jnp.bfloat16)
    product = jnp.concatenate([rim_product, head_product, late_product], 0)
    gate_feat = short_filter(jnp.concatenate([rim_gate, gate_medium], 0), short_medium[0])
    extended = jnp.concatenate([jnp.zeros((1, width_local), jnp.bfloat16), product], 0)
    mixed_medium, partial_squares = medium_call(
        extended, filter_medium, skip_medium[None, :], gate_feat
    )
    squares = jnp.sum(partial_squares, axis=1)
    total_squares = lax.psum(squares, "ch")
    inverse = lax.rsqrt(total_squares / D + 1e-06)
    normed = (mixed_medium * norm_gain * inverse[:, None]).astype(jnp.bfloat16)
    rim_gate_long, rim_key_long, rim_normed = passed_along(
        (gate_long[-2:], key_long[-2:], normed[-2:]), "ctx", 1
    )
    gate_feat_long = short_filter(jnp.concatenate([rim_gate_long, gate_long], 0), short_long[0])
    key_feat_long = short_filter(jnp.concatenate([rim_key_long, key_long], 0), short_long[1])
    value_feat_long = short_filter(jnp.concatenate([rim_normed, normed], 0), short_long[2])
    product_long = (key_feat_long * value_feat_long).astype(jnp.bfloat16)
    mode_weight = residues * jnp.sqrt(-jnp.expm1(-2.0 * decay_rates))
    step_decay = jnp.exp(-decay_rates)
    final_state = modal_end_call(product_long, step_decay)
    position = lax.axis_index("ctx")
    piece = lax.all_gather(
        final_state[None].astype(jnp.bfloat16), "ctx", axis=0, tiled=True
    ).astype(jnp.float32)
    count = piece.shape[0]
    gaps = (position - 1 - jnp.arange(count, dtype=jnp.int32)).astype(jnp.float32)
    factors = jnp.where(
        gaps[:, None, None] >= 0.0,
        jnp.exp(-decay_rates[None] * row_count * jnp.maximum(gaps, 0.0)[:, None, None]),
        0.0,
    )
    incoming = jnp.sum(factors * piece, axis=0)
    mixed_long = modal_out_call(
        product_long, step_decay, mode_weight, incoming, skip_long[None, :], gate_feat_long
    )
    return (mixed_medium, mixed_long)


def solution(mesh):
    placed = (
        P("ctx", "ch"),
        P("ctx", "ch"),
        P("ctx", "ch"),
        P(None, None, "ch"),
        P(None, "ch"),
        P("ch"),
        P("ch"),
        P("ctx", "ch"),
        P("ctx", "ch"),
        P(None, None, "ch"),
        P(None, "ch"),
        P(None, "ch"),
        P("ch"),
    )
    return jax.shard_map(
        body,
        mesh=mesh,
        in_specs=placed,
        out_specs=(P("ctx", "ch"), P("ctx", "ch")),
        check_vma=False,
    )
```

```python
import jax
import jax.numpy as jnp
from jax import lax
from jax.sharding import PartitionSpec as P
from jax.experimental import pallas as pl
from jax.experimental.pallas import tpu as pltpu

TAPS = 128
SUB = 128
RB = 8


def medium_kernel(ext_ref, f_ref, skip_ref, gate_ref, out_ref, ss_ref, q_ref):
    rows = out_ref.shape[0]
    width = out_ref.shape[1]
    span = ext_ref.shape[0]

    @pl.when(pl.program_id(0) == 0)
    def _():
        ss_ref[...] = jnp.zeros_like(ss_ref)

    for h in range(width // SUB):
        lanes = pl.ds(h * SUB, SUB)
        ext = ext_ref[:, lanes].astype(jnp.float32)
        for b in range(8):
            q_ref[b, 8:, :] = ext[8 - b : span - b]

        def block(kb, carry):
            acc = [jnp.zeros((8, SUB), jnp.float32) for _ in range(RB)]
            start = pl.multiple_of(kb * (8 * RB) + 8, 8)
            for b in range(8):
                qv = q_ref[b, pl.ds(start, 8 * (RB + 15)), :]
                for a in range(16):
                    w = jnp.broadcast_to(f_ref[pl.ds(8 * a + b, 1), lanes], (8, SUB))
                    for kk in range(RB):
                        v = kk + 15 - a
                        acc[kk] = acc[kk] + w * qv[8 * v : 8 * v + 8]
            skip = jnp.broadcast_to(skip_ref[:, lanes], (8, SUB))
            for kk in range(RB):
                row = pl.multiple_of(kb * (8 * RB) + 8 * kk, 8)
                own = q_ref[0, pl.ds(row + TAPS, 8), :]
                conv = acc[kk] + skip * own
                mixed = (gate_ref[pl.ds(row, 8), lanes] * conv).astype(jnp.bfloat16)
                out_ref[pl.ds(row, 8), lanes] = mixed
                m = mixed.astype(jnp.float32)
                ss_ref[pl.ds(row, 8), :] += m * m
            return carry

        lax.fori_loop(0, rows // (8 * RB), block, 0)


def medium_call(ext, taps, skip, gate_feat, block=512, interpret=False):
    span, width = ext.shape
    rows = gate_feat.shape[0]
    grid = (width // block,)
    return pl.pallas_call(
        medium_kernel,
        grid=grid,
        in_specs=[
            pl.BlockSpec((span, block), lambda i: (0, i)),
            pl.BlockSpec((TAPS, block), lambda i: (0, i)),
            pl.BlockSpec((1, block), lambda i: (0, i)),
            pl.BlockSpec((rows, block), lambda i: (0, i)),
        ],
        out_specs=[
            pl.BlockSpec((rows, block), lambda i: (0, i)),
            pl.BlockSpec((rows, SUB), lambda i: (0, 0)),
        ],
        out_shape=[
            jax.ShapeDtypeStruct((rows, width), jnp.bfloat16),
            jax.ShapeDtypeStruct((rows, SUB), jnp.float32),
        ],
        scratch_shapes=[pltpu.VMEM((8, span, SUB), jnp.float32)],
        compiler_params=pltpu.CompilerParams(dimension_semantics=("arbitrary",)),
        interpret=interpret,
    )(ext, taps, skip, gate_feat)

D = 8192


LANE = 128
GROUP = 4
MODES_HALF = 8


def _rows_to_f32(p_ref, pf_ref):
    pf_ref[...] = p_ref[...].astype(jnp.float32)


def modal_end_kernel(p_ref, e_ref, out_ref, pf_ref):
    rows = p_ref.shape[0]
    _rows_to_f32(p_ref, pf_ref)
    lanes = [pl.ds(g * LANE, LANE) for g in range(GROUP)]
    e_lo = [e_ref[0:8, ln] for ln in lanes]
    e_hi = [e_ref[8:16, ln] for ln in lanes]

    def step(i, carry):
        lo, hi = carry
        row = pl.multiple_of(i * 8, 8)
        blocks = [pf_ref[pl.ds(row, 8), ln] for ln in lanes]
        for j in range(8):
            new_lo, new_hi = [], []
            for g in range(GROUP):
                pb = jnp.broadcast_to(blocks[g][j : j + 1], (8, LANE))
                new_lo.append(e_lo[g] * lo[g] + pb)
                new_hi.append(e_hi[g] * hi[g] + pb)
            lo, hi = new_lo, new_hi
        return lo, hi

    zero = [jnp.zeros((8, LANE), jnp.float32) for _ in range(GROUP)]
    lo, hi = lax.fori_loop(0, rows // 8, step, (zero, list(zero)))
    for g, ln in enumerate(lanes):
        out_ref[0:8, ln] = lo[g]
        out_ref[8:16, ln] = hi[g]


def modal_end_call(product, decay):
    rows, width = product.shape
    block = LANE * GROUP
    return pl.pallas_call(
        modal_end_kernel,
        grid=(width // block,),
        in_specs=[
            pl.BlockSpec((rows, block), lambda i: (0, i)),
            pl.BlockSpec((16, block), lambda i: (0, i)),
        ],
        out_specs=pl.BlockSpec((16, block), lambda i: (0, i)),
        out_shape=jax.ShapeDtypeStruct((16, width), jnp.float32),
        scratch_shapes=[pltpu.VMEM((rows, block), jnp.float32)],
    )(product, decay)


def modal_out_kernel(p_ref, e_ref, w_ref, s_ref, skip_ref, gate_ref, out_ref, pf_ref, z_ref):
    rows = p_ref.shape[0]
    _rows_to_f32(p_ref, pf_ref)
    lanes = [pl.ds(g * LANE, LANE) for g in range(GROUP)]
    e_lo = [e_ref[0:8, ln] for ln in lanes]
    e_hi = [e_ref[8:16, ln] for ln in lanes]
    w_lo = [w_ref[0:8, ln] for ln in lanes]
    w_hi = [w_ref[8:16, ln] for ln in lanes]

    def step(i, carry):
        lo, hi = carry
        row = pl.multiple_of(i * 8, 8)
        blocks = [pf_ref[pl.ds(row, 8), ln] for ln in lanes]
        for j in range(8):
            new_lo, new_hi = [], []
            for g in range(GROUP):
                pb = jnp.broadcast_to(blocks[g][j : j + 1], (8, LANE))
                a = e_lo[g] * lo[g] + pb
                b = e_hi[g] * hi[g] + pb
                z_ref[g, pl.ds(pl.multiple_of(i * 64 + 8 * j, 8), 8), :] = w_lo[g] * a + w_hi[g] * b
                new_lo.append(a)
                new_hi.append(b)
            lo, hi = new_lo, new_hi
        return lo, hi

    init_lo = [s_ref[0:8, ln] for ln in lanes]
    init_hi = [s_ref[8:16, ln] for ln in lanes]
    lax.fori_loop(0, rows // 8, step, (init_lo, init_hi))

    def reduce(i, carry):
        row = pl.multiple_of(i * 8, 8)
        for g, ln in enumerate(lanes):
            total = z_ref[g, pl.ds(i * 64, 8, stride=8), :]
            for j in range(1, 8):
                total = total + z_ref[g, pl.ds(i * 64 + j, 8, stride=8), :]
            own = pf_ref[pl.ds(row, 8), ln]
            skip = jnp.broadcast_to(skip_ref[:, ln], (8, LANE))
            conv = total + skip * own
            out_ref[pl.ds(row, 8), ln] = (gate_ref[pl.ds(row, 8), ln] * conv).astype(out_ref.dtype)
        return carry

    lax.fori_loop(0, rows // 8, reduce, 0)


def modal_out_call(product, decay, weight, start, skip, gate_feat):
    rows, width = product.shape
    block = LANE * GROUP
    return pl.pallas_call(
        modal_out_kernel,
        grid=(width // block,),
        in_specs=[
            pl.BlockSpec((rows, block), lambda i: (0, i)),
            pl.BlockSpec((16, block), lambda i: (0, i)),
            pl.BlockSpec((16, block), lambda i: (0, i)),
            pl.BlockSpec((16, block), lambda i: (0, i)),
            pl.BlockSpec((1, block), lambda i: (0, i)),
            pl.BlockSpec((rows, block), lambda i: (0, i)),
        ],
        out_specs=pl.BlockSpec((rows, block), lambda i: (0, i)),
        out_shape=jax.ShapeDtypeStruct((rows, width), jnp.bfloat16),
        scratch_shapes=[
            pltpu.VMEM((rows, block), jnp.float32),
            pltpu.VMEM((GROUP, rows * 8, LANE), jnp.float32),
        ],
    )(product, decay, weight, start, skip, gate_feat)


def passed_along(value, axis, steps):
    count = lax.axis_size(axis)
    first, last = (max(0, -steps), min(count, count - steps))
    return lax.ppermute(value, axis, [(source, source + steps) for source in range(first, last)])


def short_filter(extended, weights):
    return weights[0] * extended[2:] + weights[1] * extended[1:-1] + weights[2] * extended[:-2]


def medium_conv(extended, taps, row_count):
    tap_count = taps.shape[0]
    total = jnp.zeros((row_count, taps.shape[1]), jnp.float32)
    for offset in range(tap_count):
        start = tap_count - 1 - offset
        total = total + taps[offset] * extended[start : start + row_count]
    return total


def body(
    gate_medium,
    key_medium,
    value_medium,
    short_medium,
    filter_medium,
    skip_medium,
    norm_gain,
    gate_long,
    key_long,
    short_long,
    decay_rates,
    residues,
    skip_long,
):
    row_count = gate_medium.shape[0]
    tap_count = filter_medium.shape[0]
    width_local = gate_medium.shape[1]
    late_product = (
        short_filter(key_medium, short_medium[1]) * short_filter(value_medium, short_medium[2])
    ).astype(jnp.bfloat16)
    rim_gate, rim_key, rim_value, rim_product = passed_along(
        (gate_medium[-2:], key_medium[-2:], value_medium[-2:], late_product[-(tap_count - 1) :]),
        "ctx",
        1,
    )
    head_key = short_filter(jnp.concatenate([rim_key, key_medium[:2]], 0), short_medium[1])
    head_value = short_filter(jnp.concatenate([rim_value, value_medium[:2]], 0), short_medium[2])
    head_product = (head_key * head_value).astype(jnp.bfloat16)
    product = jnp.concatenate([rim_product, head_product, late_product], 0)
    gate_feat = short_filter(jnp.concatenate([rim_gate, gate_medium], 0), short_medium[0])
    extended = jnp.concatenate([jnp.zeros((1, width_local), jnp.bfloat16), product], 0)
    mixed_medium, partial_squares = medium_call(
        extended, filter_medium, skip_medium[None, :], gate_feat
    )
    squares = jnp.sum(partial_squares, axis=1)
    ring = lax.axis_size("ch")
    total_squares = squares
    for shift in range(1, ring):
        total_squares = total_squares + lax.ppermute(
            squares, "ch", [(source, (source + shift) % ring) for source in range(ring)]
        )
    inverse = lax.rsqrt(total_squares / D + 1e-06)
    normed = (mixed_medium * norm_gain * inverse[:, None]).astype(jnp.bfloat16)
    rim_gate_long, rim_key_long, rim_normed = passed_along(
        (gate_long[-2:], key_long[-2:], normed[-2:]), "ctx", 1
    )
    gate_feat_long = short_filter(jnp.concatenate([rim_gate_long, gate_long], 0), short_long[0])
    key_feat_long = short_filter(jnp.concatenate([rim_key_long, key_long], 0), short_long[1])
    value_feat_long = short_filter(jnp.concatenate([rim_normed, normed], 0), short_long[2])
    product_long = (key_feat_long * value_feat_long).astype(jnp.bfloat16)
    mode_weight = residues * jnp.sqrt(-jnp.expm1(-2.0 * decay_rates))
    step_decay = jnp.exp(-decay_rates)
    final_state = modal_end_call(product_long, step_decay)
    incoming = passed_along(final_state, "ctx", 1)
    span = 1
    while span < lax.axis_size("ctx"):
        earlier = passed_along(incoming, "ctx", span)
        incoming = incoming + jnp.exp(-decay_rates * (row_count * span)) * earlier
        span *= 2
    mixed_long = modal_out_call(
        product_long, step_decay, mode_weight, incoming, skip_long[None, :], gate_feat_long
    )
    return (mixed_medium, mixed_long)


def solution(mesh):
    placed = (
        P("ctx", "ch"),
        P("ctx", "ch"),
        P("ctx", "ch"),
        P(None, None, "ch"),
        P(None, "ch"),
        P("ch"),
        P("ch"),
        P("ctx", "ch"),
        P("ctx", "ch"),
        P(None, None, "ch"),
        P(None, "ch"),
        P(None, "ch"),
        P("ch"),
    )
    return jax.shard_map(
        body,
        mesh=mesh,
        in_specs=placed,
        out_specs=(P("ctx", "ch"), P("ctx", "ch")),
        check_vma=False,
    )
```

```python
import functools
import jax
import jax.numpy as jnp
from jax import lax
from jax.sharding import PartitionSpec as P
from jax.experimental import pallas as pl
from jax.experimental.pallas import tpu as pltpu

TAPS = 128
SUB = 128
RB = 8


def medium_kernel(ext_ref, f_ref, skip_ref, gate_ref, out_ref, ss_ref, q_ref):
    rows = out_ref.shape[0]
    width = out_ref.shape[1]
    span = ext_ref.shape[0]

    @pl.when(pl.program_id(0) == 0)
    def _():
        ss_ref[...] = jnp.zeros_like(ss_ref)

    for h in range(width // SUB):
        lanes = pl.ds(h * SUB, SUB)
        ext = ext_ref[:, lanes].astype(jnp.float32)
        for b in range(8):
            q_ref[b, 8:, :] = ext[8 - b : span - b]

        def block(kb, carry):
            acc = [jnp.zeros((8, SUB), jnp.float32) for _ in range(RB)]
            start = pl.multiple_of(kb * (8 * RB) + 8, 8)
            for b in range(8):
                qv = q_ref[b, pl.ds(start, 8 * (RB + 15)), :]
                for a in range(16):
                    w = jnp.broadcast_to(f_ref[pl.ds(8 * a + b, 1), lanes], (8, SUB))
                    for kk in range(RB):
                        v = kk + 15 - a
                        acc[kk] = acc[kk] + w * qv[8 * v : 8 * v + 8]
            skip = jnp.broadcast_to(skip_ref[:, lanes], (8, SUB))
            for kk in range(RB):
                row = pl.multiple_of(kb * (8 * RB) + 8 * kk, 8)
                own = q_ref[0, pl.ds(row + TAPS, 8), :]
                conv = acc[kk] + skip * own
                mixed = (gate_ref[pl.ds(row, 8), lanes] * conv).astype(jnp.bfloat16)
                out_ref[pl.ds(row, 8), lanes] = mixed
                m = mixed.astype(jnp.float32)
                ss_ref[pl.ds(row, 8), :] += m * m
            return carry

        lax.fori_loop(0, rows // (8 * RB), block, 0)


def medium_call(ext, taps, skip, gate_feat, block=512, interpret=False):
    span, width = ext.shape
    rows = gate_feat.shape[0]
    grid = (width // block,)
    return pl.pallas_call(
        medium_kernel,
        grid=grid,
        in_specs=[
            pl.BlockSpec((span, block), lambda i: (0, i)),
            pl.BlockSpec((TAPS, block), lambda i: (0, i)),
            pl.BlockSpec((1, block), lambda i: (0, i)),
            pl.BlockSpec((rows, block), lambda i: (0, i)),
        ],
        out_specs=[
            pl.BlockSpec((rows, block), lambda i: (0, i)),
            pl.BlockSpec((rows, SUB), lambda i: (0, 0)),
        ],
        out_shape=[
            jax.ShapeDtypeStruct((rows, width), jnp.bfloat16),
            jax.ShapeDtypeStruct((rows, SUB), jnp.float32),
        ],
        scratch_shapes=[pltpu.VMEM((8, span, SUB), jnp.float32)],
        compiler_params=pltpu.CompilerParams(dimension_semantics=("arbitrary",)),
        interpret=interpret,
    )(ext, taps, skip, gate_feat)

D = 8192


LANE = 128
GROUP = 4
MODES_HALF = 8


def _rows_to_f32(p_ref, pf_ref):
    pf_ref[...] = p_ref[...].astype(jnp.float32)


def modal_end_kernel(p_ref, e_ref, out_ref, pf_ref):
    rows = p_ref.shape[0]
    _rows_to_f32(p_ref, pf_ref)
    lanes = [pl.ds(g * LANE, LANE) for g in range(GROUP)]
    e_lo = [e_ref[0:8, ln] for ln in lanes]
    e_hi = [e_ref[8:16, ln] for ln in lanes]

    def step(i, carry):
        lo, hi = carry
        row = pl.multiple_of(i * 8, 8)
        blocks = [pf_ref[pl.ds(row, 8), ln] for ln in lanes]
        for j in range(8):
            new_lo, new_hi = [], []
            for g in range(GROUP):
                pb = jnp.broadcast_to(blocks[g][j : j + 1], (8, LANE))
                new_lo.append(e_lo[g] * lo[g] + pb)
                new_hi.append(e_hi[g] * hi[g] + pb)
            lo, hi = new_lo, new_hi
        return lo, hi

    zero = [jnp.zeros((8, LANE), jnp.float32) for _ in range(GROUP)]
    lo, hi = lax.fori_loop(0, rows // 8, step, (zero, list(zero)))
    for g, ln in enumerate(lanes):
        out_ref[0:8, ln] = lo[g]
        out_ref[8:16, ln] = hi[g]


def modal_end_call(product, decay):
    rows, width = product.shape
    block = LANE * GROUP
    return pl.pallas_call(
        modal_end_kernel,
        grid=(width // block,),
        in_specs=[
            pl.BlockSpec((rows, block), lambda i: (0, i)),
            pl.BlockSpec((16, block), lambda i: (0, i)),
        ],
        out_specs=pl.BlockSpec((16, block), lambda i: (0, i)),
        out_shape=jax.ShapeDtypeStruct((16, width), jnp.float32),
        scratch_shapes=[pltpu.VMEM((rows, block), jnp.float32)],
    )(product, decay)


def modal_out_kernel(p_ref, e_ref, w_ref, s_ref, skip_ref, gate_ref, out_ref, pf_ref, z_ref):
    rows = p_ref.shape[0]
    _rows_to_f32(p_ref, pf_ref)
    lanes = [pl.ds(g * LANE, LANE) for g in range(GROUP)]
    e_lo = [e_ref[0:8, ln] for ln in lanes]
    e_hi = [e_ref[8:16, ln] for ln in lanes]
    w_lo = [w_ref[0:8, ln] for ln in lanes]
    w_hi = [w_ref[8:16, ln] for ln in lanes]

    def step(i, carry):
        lo, hi = carry
        row = pl.multiple_of(i * 8, 8)
        blocks = [pf_ref[pl.ds(row, 8), ln] for ln in lanes]
        for j in range(8):
            new_lo, new_hi = [], []
            for g in range(GROUP):
                pb = jnp.broadcast_to(blocks[g][j : j + 1], (8, LANE))
                a = e_lo[g] * lo[g] + pb
                b = e_hi[g] * hi[g] + pb
                z_ref[g, pl.ds(pl.multiple_of(i * 64 + 8 * j, 8), 8), :] = w_lo[g] * a + w_hi[g] * b
                new_lo.append(a)
                new_hi.append(b)
            lo, hi = new_lo, new_hi
        return lo, hi

    init_lo = [s_ref[0:8, ln] for ln in lanes]
    init_hi = [s_ref[8:16, ln] for ln in lanes]
    lax.fori_loop(0, rows // 8, step, (init_lo, init_hi))

    def reduce(i, carry):
        row = pl.multiple_of(i * 8, 8)
        for g, ln in enumerate(lanes):
            total = z_ref[g, pl.ds(i * 64, 8, stride=8), :]
            for j in range(1, 8):
                total = total + z_ref[g, pl.ds(i * 64 + j, 8, stride=8), :]
            own = pf_ref[pl.ds(row, 8), ln]
            skip = jnp.broadcast_to(skip_ref[:, ln], (8, LANE))
            conv = total + skip * own
            out_ref[pl.ds(row, 8), ln] = (gate_ref[pl.ds(row, 8), ln] * conv).astype(out_ref.dtype)
        return carry

    lax.fori_loop(0, rows // 8, reduce, 0)


def modal_out_call(product, decay, weight, start, skip, gate_feat):
    rows, width = product.shape
    block = LANE * GROUP
    return pl.pallas_call(
        modal_out_kernel,
        grid=(width // block,),
        in_specs=[
            pl.BlockSpec((rows, block), lambda i: (0, i)),
            pl.BlockSpec((16, block), lambda i: (0, i)),
            pl.BlockSpec((16, block), lambda i: (0, i)),
            pl.BlockSpec((16, block), lambda i: (0, i)),
            pl.BlockSpec((1, block), lambda i: (0, i)),
            pl.BlockSpec((rows, block), lambda i: (0, i)),
        ],
        out_specs=pl.BlockSpec((rows, block), lambda i: (0, i)),
        out_shape=jax.ShapeDtypeStruct((rows, width), jnp.bfloat16),
        scratch_shapes=[
            pltpu.VMEM((rows, block), jnp.float32),
            pltpu.VMEM((GROUP, rows * 8, LANE), jnp.float32),
        ],
    )(product, decay, weight, start, skip, gate_feat)


def scan_kernel(count, rows, f_ref, r_ref, out_ref, send_ref, recv_ref, send_sem, recv_sem):
    me = lax.axis_index("ctx")
    plan = [(1, False)]
    span = 1
    while span < count:
        plan.append((span, True))
        span *= 2
    out_ref[...] = jnp.zeros_like(out_ref)
    for k, (shift, combine) in enumerate(plan):
        if k == 0:
            source = f_ref
        else:
            send_ref[k] = out_ref[...]
            source = send_ref.at[k]
        copy = pltpu.make_async_remote_copy(
            src_ref=source,
            dst_ref=recv_ref.at[k],
            send_sem=send_sem.at[k],
            recv_sem=recv_sem.at[k],
            device_id={"ctx": me + shift},
            device_id_type=pl.DeviceIdType.MESH,
        )

        @pl.when(me + shift < count)
        def _():
            copy.start()

        @pl.when(me >= shift)
        def _():
            copy.wait_recv()
            if combine:
                factor = jnp.exp(r_ref[...] * (-1.0 * rows * shift))
                out_ref[...] = out_ref[...] + factor * recv_ref[k]
            else:
                out_ref[...] = recv_ref[k]

        @pl.when(me + shift < count)
        def _():
            copy.wait_send()


def scan_call(final_state, decay_rates, count, rows):
    steps = 1
    while (1 << (steps - 1)) < count:
        steps += 1
    shape = final_state.shape
    return pl.pallas_call(
        functools.partial(scan_kernel, count, rows),
        in_specs=[pl.BlockSpec(memory_space=pltpu.VMEM)] * 2,
        out_specs=pl.BlockSpec(memory_space=pltpu.VMEM),
        out_shape=jax.ShapeDtypeStruct(shape, jnp.float32),
        scratch_shapes=[
            pltpu.VMEM((steps,) + shape, jnp.float32),
            pltpu.VMEM((steps,) + shape, jnp.float32),
            pltpu.SemaphoreType.DMA((steps,)),
            pltpu.SemaphoreType.DMA((steps,)),
        ],
        compiler_params=pltpu.CompilerParams(has_side_effects=True),
    )(final_state, decay_rates)


def passed_along(value, axis, steps):
    count = lax.axis_size(axis)
    first, last = (max(0, -steps), min(count, count - steps))
    return lax.ppermute(value, axis, [(source, source + steps) for source in range(first, last)])


def short_filter(extended, weights):
    return weights[0] * extended[2:] + weights[1] * extended[1:-1] + weights[2] * extended[:-2]


def medium_conv(extended, taps, row_count):
    tap_count = taps.shape[0]
    total = jnp.zeros((row_count, taps.shape[1]), jnp.float32)
    for offset in range(tap_count):
        start = tap_count - 1 - offset
        total = total + taps[offset] * extended[start : start + row_count]
    return total


def body(
    gate_medium,
    key_medium,
    value_medium,
    short_medium,
    filter_medium,
    skip_medium,
    norm_gain,
    gate_long,
    key_long,
    short_long,
    decay_rates,
    residues,
    skip_long,
):
    row_count = gate_medium.shape[0]
    tap_count = filter_medium.shape[0]
    width_local = gate_medium.shape[1]
    late_product = (
        short_filter(key_medium, short_medium[1]) * short_filter(value_medium, short_medium[2])
    ).astype(jnp.bfloat16)
    rim_gate, rim_key, rim_value, rim_product = passed_along(
        (gate_medium[-2:], key_medium[-2:], value_medium[-2:], late_product[-(tap_count - 1) :]),
        "ctx",
        1,
    )
    head_key = short_filter(jnp.concatenate([rim_key, key_medium[:2]], 0), short_medium[1])
    head_value = short_filter(jnp.concatenate([rim_value, value_medium[:2]], 0), short_medium[2])
    head_product = (head_key * head_value).astype(jnp.bfloat16)
    product = jnp.concatenate([rim_product, head_product, late_product], 0)
    gate_feat = short_filter(jnp.concatenate([rim_gate, gate_medium], 0), short_medium[0])
    extended = jnp.concatenate([jnp.zeros((1, width_local), jnp.bfloat16), product], 0)
    mixed_medium, partial_squares = medium_call(
        extended, filter_medium, skip_medium[None, :], gate_feat
    )
    squares = jnp.sum(partial_squares, axis=1)
    ring = lax.axis_size("ch")
    total_squares = squares
    for shift in range(1, ring):
        total_squares = total_squares + lax.ppermute(
            squares, "ch", [(source, (source + shift) % ring) for source in range(ring)]
        )
    inverse = lax.rsqrt(total_squares / D + 1e-06)
    normed = (mixed_medium * norm_gain * inverse[:, None]).astype(jnp.bfloat16)
    rim_gate_long, rim_key_long, rim_normed = passed_along(
        (gate_long[-2:], key_long[-2:], normed[-2:]), "ctx", 1
    )
    gate_feat_long = short_filter(jnp.concatenate([rim_gate_long, gate_long], 0), short_long[0])
    key_feat_long = short_filter(jnp.concatenate([rim_key_long, key_long], 0), short_long[1])
    value_feat_long = short_filter(jnp.concatenate([rim_normed, normed], 0), short_long[2])
    product_long = (key_feat_long * value_feat_long).astype(jnp.bfloat16)
    mode_weight = residues * jnp.sqrt(-jnp.expm1(-2.0 * decay_rates))
    step_decay = jnp.exp(-decay_rates)
    final_state = modal_end_call(product_long, step_decay)
    incoming = scan_call(final_state, decay_rates, lax.axis_size("ctx"), row_count)
    mixed_long = modal_out_call(
        product_long, step_decay, mode_weight, incoming, skip_long[None, :], gate_feat_long
    )
    return (mixed_medium, mixed_long)


def solution(mesh):
    placed = (
        P("ctx", "ch"),
        P("ctx", "ch"),
        P("ctx", "ch"),
        P(None, None, "ch"),
        P(None, "ch"),
        P("ch"),
        P("ch"),
        P("ctx", "ch"),
        P("ctx", "ch"),
        P(None, None, "ch"),
        P(None, "ch"),
        P(None, "ch"),
        P("ch"),
    )
    return jax.shard_map(
        body,
        mesh=mesh,
        in_specs=placed,
        out_specs=(P("ctx", "ch"), P("ctx", "ch")),
        check_vma=False,
    )
```

```python
import functools
import jax
import jax.numpy as jnp
from jax import lax
from jax.sharding import PartitionSpec as P
from jax.experimental import pallas as pl
from jax.experimental.pallas import tpu as pltpu

TAPS = 128
SUB = 128
RB = 8


def medium_kernel(ext_ref, f_ref, skip_ref, gate_ref, out_ref, ss_ref, q_ref):
    rows = out_ref.shape[0]
    width = out_ref.shape[1]
    span = ext_ref.shape[0]

    @pl.when(pl.program_id(0) == 0)
    def _():
        ss_ref[...] = jnp.zeros_like(ss_ref)

    for h in range(width // SUB):
        lanes = pl.ds(h * SUB, SUB)
        ext = ext_ref[:, lanes].astype(jnp.float32)
        for b in range(8):
            q_ref[b, 8:, :] = ext[8 - b : span - b]

        def block(kb, carry):
            acc = [jnp.zeros((8, SUB), jnp.float32) for _ in range(RB)]
            start = pl.multiple_of(kb * (8 * RB) + 8, 8)
            for b in range(8):
                qv = q_ref[b, pl.ds(start, 8 * (RB + 15)), :]
                for a in range(16):
                    w = jnp.broadcast_to(f_ref[pl.ds(8 * a + b, 1), lanes], (8, SUB))
                    for kk in range(RB):
                        v = kk + 15 - a
                        acc[kk] = acc[kk] + w * qv[8 * v : 8 * v + 8]
            skip = jnp.broadcast_to(skip_ref[:, lanes], (8, SUB))
            for kk in range(RB):
                row = pl.multiple_of(kb * (8 * RB) + 8 * kk, 8)
                own = q_ref[0, pl.ds(row + TAPS, 8), :]
                conv = acc[kk] + skip * own
                mixed = (gate_ref[pl.ds(row, 8), lanes] * conv).astype(jnp.bfloat16)
                out_ref[pl.ds(row, 8), lanes] = mixed
                m = mixed.astype(jnp.float32)
                ss_ref[pl.ds(row, 8), :] += m * m
            return carry

        lax.fori_loop(0, rows // (8 * RB), block, 0)


def medium_call(ext, taps, skip, gate_feat, block=512, interpret=False):
    span, width = ext.shape
    rows = gate_feat.shape[0]
    grid = (width // block,)
    return pl.pallas_call(
        medium_kernel,
        grid=grid,
        in_specs=[
            pl.BlockSpec((span, block), lambda i: (0, i)),
            pl.BlockSpec((TAPS, block), lambda i: (0, i)),
            pl.BlockSpec((1, block), lambda i: (0, i)),
            pl.BlockSpec((rows, block), lambda i: (0, i)),
        ],
        out_specs=[
            pl.BlockSpec((rows, block), lambda i: (0, i)),
            pl.BlockSpec((rows, SUB), lambda i: (0, 0)),
        ],
        out_shape=[
            jax.ShapeDtypeStruct((rows, width), jnp.bfloat16),
            jax.ShapeDtypeStruct((rows, SUB), jnp.float32),
        ],
        scratch_shapes=[pltpu.VMEM((8, span, SUB), jnp.float32)],
        compiler_params=pltpu.CompilerParams(dimension_semantics=("arbitrary",)),
        interpret=interpret,
    )(ext, taps, skip, gate_feat)

D = 8192


LANE = 128
GROUP = 4
MODES_HALF = 8


def _rows_to_f32(p_ref, pf_ref):
    pf_ref[...] = p_ref[...].astype(jnp.float32)


def modal_end_kernel(p_ref, e_ref, out_ref, pf_ref):
    rows = p_ref.shape[0]
    _rows_to_f32(p_ref, pf_ref)
    lanes = [pl.ds(g * LANE, LANE) for g in range(GROUP)]
    e_lo = [e_ref[0:8, ln] for ln in lanes]
    e_hi = [e_ref[8:16, ln] for ln in lanes]

    def step(i, carry):
        lo, hi = carry
        row = pl.multiple_of(i * 8, 8)
        blocks = [pf_ref[pl.ds(row, 8), ln] for ln in lanes]
        for j in range(8):
            new_lo, new_hi = [], []
            for g in range(GROUP):
                pb = jnp.broadcast_to(blocks[g][j : j + 1], (8, LANE))
                new_lo.append(e_lo[g] * lo[g] + pb)
                new_hi.append(e_hi[g] * hi[g] + pb)
            lo, hi = new_lo, new_hi
        return lo, hi

    zero = [jnp.zeros((8, LANE), jnp.float32) for _ in range(GROUP)]
    lo, hi = lax.fori_loop(0, rows // 8, step, (zero, list(zero)))
    for g, ln in enumerate(lanes):
        out_ref[0:8, ln] = lo[g]
        out_ref[8:16, ln] = hi[g]


def modal_end_call(product, decay):
    rows, width = product.shape
    block = LANE * GROUP
    return pl.pallas_call(
        modal_end_kernel,
        grid=(width // block,),
        in_specs=[
            pl.BlockSpec((rows, block), lambda i: (0, i)),
            pl.BlockSpec((16, block), lambda i: (0, i)),
        ],
        out_specs=pl.BlockSpec((16, block), lambda i: (0, i)),
        out_shape=jax.ShapeDtypeStruct((16, width), jnp.float32),
        scratch_shapes=[pltpu.VMEM((rows, block), jnp.float32)],
    )(product, decay)


def modal_out_kernel(p_ref, e_ref, w_ref, s_ref, skip_ref, gate_ref, out_ref, pf_ref, z_ref):
    rows = p_ref.shape[0]
    _rows_to_f32(p_ref, pf_ref)
    lanes = [pl.ds(g * LANE, LANE) for g in range(GROUP)]
    e_lo = [e_ref[0:8, ln] for ln in lanes]
    e_hi = [e_ref[8:16, ln] for ln in lanes]
    w_lo = [w_ref[0:8, ln] for ln in lanes]
    w_hi = [w_ref[8:16, ln] for ln in lanes]

    def step(i, carry):
        lo, hi = carry
        row = pl.multiple_of(i * 8, 8)
        blocks = [pf_ref[pl.ds(row, 8), ln] for ln in lanes]
        for j in range(8):
            new_lo, new_hi = [], []
            for g in range(GROUP):
                pb = jnp.broadcast_to(blocks[g][j : j + 1], (8, LANE))
                a = e_lo[g] * lo[g] + pb
                b = e_hi[g] * hi[g] + pb
                z_ref[g, pl.ds(pl.multiple_of(i * 64 + 8 * j, 8), 8), :] = w_lo[g] * a + w_hi[g] * b
                new_lo.append(a)
                new_hi.append(b)
            lo, hi = new_lo, new_hi
        return lo, hi

    init_lo = [s_ref[0:8, ln] for ln in lanes]
    init_hi = [s_ref[8:16, ln] for ln in lanes]
    lax.fori_loop(0, rows // 8, step, (init_lo, init_hi))

    def reduce(i, carry):
        row = pl.multiple_of(i * 8, 8)
        for g, ln in enumerate(lanes):
            total = z_ref[g, pl.ds(i * 64, 8, stride=8), :]
            for j in range(1, 8):
                total = total + z_ref[g, pl.ds(i * 64 + j, 8, stride=8), :]
            own = pf_ref[pl.ds(row, 8), ln]
            skip = jnp.broadcast_to(skip_ref[:, ln], (8, LANE))
            conv = total + skip * own
            out_ref[pl.ds(row, 8), ln] = (gate_ref[pl.ds(row, 8), ln] * conv).astype(out_ref.dtype)
        return carry

    lax.fori_loop(0, rows // 8, reduce, 0)


def modal_out_call(product, decay, weight, start, skip, gate_feat):
    rows, width = product.shape
    block = LANE * GROUP
    return pl.pallas_call(
        modal_out_kernel,
        grid=(width // block,),
        in_specs=[
            pl.BlockSpec((rows, block), lambda i: (0, i)),
            pl.BlockSpec((16, block), lambda i: (0, i)),
            pl.BlockSpec((16, block), lambda i: (0, i)),
            pl.BlockSpec((16, block), lambda i: (0, i)),
            pl.BlockSpec((1, block), lambda i: (0, i)),
            pl.BlockSpec((rows, block), lambda i: (0, i)),
        ],
        out_specs=pl.BlockSpec((rows, block), lambda i: (0, i)),
        out_shape=jax.ShapeDtypeStruct((rows, width), jnp.bfloat16),
        scratch_shapes=[
            pltpu.VMEM((rows, block), jnp.float32),
            pltpu.VMEM((GROUP, rows * 8, LANE), jnp.float32),
        ],
    )(product, decay, weight, start, skip, gate_feat)


def scan_kernel(count, rows, f_ref, r_ref, out_ref, send_ref, recv_ref, send_sem, recv_sem):
    me = lax.axis_index("ctx")
    plan = []
    span = 1
    while span * 4 < count:
        plan.append([(span * i, span * i) for i in range(1, 4)])
        span *= 4
    plan.append([(1 + span * i, span * i) for i in range(count // span)])
    out_ref[...] = f_ref[...]
    for k, sends in enumerate(plan):
        send_ref[k] = out_ref[...]
        last = k == len(plan) - 1
        if last:
            out_ref[...] = jnp.zeros_like(out_ref)
        copies = []
        for i, (shift, power) in enumerate(sends):
            copy = pltpu.make_async_remote_copy(
                src_ref=send_ref.at[k],
                dst_ref=recv_ref.at[k, i],
                send_sem=send_sem.at[k, i],
                recv_sem=recv_sem.at[k, i],
                device_id={"ctx": me + shift},
                device_id_type=pl.DeviceIdType.MESH,
            )
            copies.append((shift, power, copy))

            @pl.when(me + shift < count)
            def _():
                copy.start()

        for i, (shift, power, copy) in enumerate(copies):

            @pl.when(me >= shift)
            def _():
                copy.wait_recv()
                if power == 0:
                    out_ref[...] = out_ref[...] + recv_ref[k, i]
                else:
                    factor = jnp.exp(r_ref[...] * (-1.0 * rows * power))
                    out_ref[...] = out_ref[...] + factor * recv_ref[k, i]

        for shift, power, copy in copies:

            @pl.when(me + shift < count)
            def _():
                copy.wait_send()


def scan_call(final_state, decay_rates, count, rows):
    shape = final_state.shape
    return pl.pallas_call(
        functools.partial(scan_kernel, count, rows),
        in_specs=[pl.BlockSpec(memory_space=pltpu.VMEM)] * 2,
        out_specs=pl.BlockSpec(memory_space=pltpu.VMEM),
        out_shape=jax.ShapeDtypeStruct(shape, jnp.float32),
        scratch_shapes=[
            pltpu.VMEM((3,) + shape, jnp.float32),
            pltpu.VMEM((3, 4) + shape, jnp.float32),
            pltpu.SemaphoreType.DMA((3, 4)),
            pltpu.SemaphoreType.DMA((3, 4)),
        ],
        compiler_params=pltpu.CompilerParams(has_side_effects=True),
    )(final_state, decay_rates)


def passed_along(value, axis, steps):
    count = lax.axis_size(axis)
    first, last = (max(0, -steps), min(count, count - steps))
    return lax.ppermute(value, axis, [(source, source + steps) for source in range(first, last)])


def short_filter(extended, weights):
    return weights[0] * extended[2:] + weights[1] * extended[1:-1] + weights[2] * extended[:-2]


def medium_conv(extended, taps, row_count):
    tap_count = taps.shape[0]
    total = jnp.zeros((row_count, taps.shape[1]), jnp.float32)
    for offset in range(tap_count):
        start = tap_count - 1 - offset
        total = total + taps[offset] * extended[start : start + row_count]
    return total


def body(
    gate_medium,
    key_medium,
    value_medium,
    short_medium,
    filter_medium,
    skip_medium,
    norm_gain,
    gate_long,
    key_long,
    short_long,
    decay_rates,
    residues,
    skip_long,
):
    row_count = gate_medium.shape[0]
    tap_count = filter_medium.shape[0]
    width_local = gate_medium.shape[1]
    late_product = (
        short_filter(key_medium, short_medium[1]) * short_filter(value_medium, short_medium[2])
    ).astype(jnp.bfloat16)
    rim_gate, rim_key, rim_value, rim_product = passed_along(
        (gate_medium[-2:], key_medium[-2:], value_medium[-2:], late_product[-(tap_count - 1) :]),
        "ctx",
        1,
    )
    head_key = short_filter(jnp.concatenate([rim_key, key_medium[:2]], 0), short_medium[1])
    head_value = short_filter(jnp.concatenate([rim_value, value_medium[:2]], 0), short_medium[2])
    head_product = (head_key * head_value).astype(jnp.bfloat16)
    product = jnp.concatenate([rim_product, head_product, late_product], 0)
    gate_feat = short_filter(jnp.concatenate([rim_gate, gate_medium], 0), short_medium[0])
    extended = jnp.concatenate([jnp.zeros((1, width_local), jnp.bfloat16), product], 0)
    mixed_medium, partial_squares = medium_call(
        extended, filter_medium, skip_medium[None, :], gate_feat
    )
    squares = jnp.sum(partial_squares, axis=1)
    ring = lax.axis_size("ch")
    total_squares = squares
    for shift in range(1, ring):
        total_squares = total_squares + lax.ppermute(
            squares, "ch", [(source, (source + shift) % ring) for source in range(ring)]
        )
    inverse = lax.rsqrt(total_squares / D + 1e-06)
    normed = (mixed_medium * norm_gain * inverse[:, None]).astype(jnp.bfloat16)
    rim_gate_long, rim_key_long, rim_normed = passed_along(
        (gate_long[-2:], key_long[-2:], normed[-2:]), "ctx", 1
    )
    gate_feat_long = short_filter(jnp.concatenate([rim_gate_long, gate_long], 0), short_long[0])
    key_feat_long = short_filter(jnp.concatenate([rim_key_long, key_long], 0), short_long[1])
    value_feat_long = short_filter(jnp.concatenate([rim_normed, normed], 0), short_long[2])
    product_long = (key_feat_long * value_feat_long).astype(jnp.bfloat16)
    mode_weight = residues * jnp.sqrt(-jnp.expm1(-2.0 * decay_rates))
    step_decay = jnp.exp(-decay_rates)
    final_state = modal_end_call(product_long, step_decay)
    incoming = scan_call(final_state, decay_rates, lax.axis_size("ctx"), row_count)
    mixed_long = modal_out_call(
        product_long, step_decay, mode_weight, incoming, skip_long[None, :], gate_feat_long
    )
    return (mixed_medium, mixed_long)


def solution(mesh):
    placed = (
        P("ctx", "ch"),
        P("ctx", "ch"),
        P("ctx", "ch"),
        P(None, None, "ch"),
        P(None, "ch"),
        P("ch"),
        P("ch"),
        P("ctx", "ch"),
        P("ctx", "ch"),
        P(None, None, "ch"),
        P(None, "ch"),
        P(None, "ch"),
        P("ch"),
    )
    return jax.shard_map(
        body,
        mesh=mesh,
        in_specs=placed,
        out_specs=(P("ctx", "ch"), P("ctx", "ch")),
        check_vma=False,
    )
```

```python
import functools
import jax
import jax.numpy as jnp
from jax import lax
from jax.sharding import PartitionSpec as P
from jax.experimental import pallas as pl
from jax.experimental.pallas import tpu as pltpu

TAPS = 128
SUB = 128
RB = 8


def medium_kernel(ext_ref, f_ref, skip_ref, gate_ref, out_ref, ss_ref, q_ref):
    rows = out_ref.shape[0]
    width = out_ref.shape[1]
    span = ext_ref.shape[0]

    @pl.when(pl.program_id(0) == 0)
    def _():
        ss_ref[...] = jnp.zeros_like(ss_ref)

    for h in range(width // SUB):
        lanes = pl.ds(h * SUB, SUB)
        ext = ext_ref[:, lanes].astype(jnp.float32)
        for b in range(8):
            q_ref[b, 8:, :] = ext[8 - b : span - b]

        def block(kb, carry):
            acc = [jnp.zeros((8, SUB), jnp.float32) for _ in range(RB)]
            start = pl.multiple_of(kb * (8 * RB) + 8, 8)
            for b in range(8):
                qv = q_ref[b, pl.ds(start, 8 * (RB + 15)), :]
                for a in range(16):
                    w = jnp.broadcast_to(f_ref[pl.ds(8 * a + b, 1), lanes], (8, SUB))
                    for kk in range(RB):
                        v = kk + 15 - a
                        acc[kk] = acc[kk] + w * qv[8 * v : 8 * v + 8]
            skip = jnp.broadcast_to(skip_ref[:, lanes], (8, SUB))
            for kk in range(RB):
                row = pl.multiple_of(kb * (8 * RB) + 8 * kk, 8)
                own = q_ref[0, pl.ds(row + TAPS, 8), :]
                conv = acc[kk] + skip * own
                mixed = (gate_ref[pl.ds(row, 8), lanes] * conv).astype(jnp.bfloat16)
                out_ref[pl.ds(row, 8), lanes] = mixed
                m = mixed.astype(jnp.float32)
                ss_ref[pl.ds(row, 8), :] += m * m
            return carry

        lax.fori_loop(0, rows // (8 * RB), block, 0)


def medium_call(ext, taps, skip, gate_feat, block=512, interpret=False):
    span, width = ext.shape
    rows = gate_feat.shape[0]
    grid = (width // block,)
    return pl.pallas_call(
        medium_kernel,
        grid=grid,
        in_specs=[
            pl.BlockSpec((span, block), lambda i: (0, i)),
            pl.BlockSpec((TAPS, block), lambda i: (0, i)),
            pl.BlockSpec((1, block), lambda i: (0, i)),
            pl.BlockSpec((rows, block), lambda i: (0, i)),
        ],
        out_specs=[
            pl.BlockSpec((rows, block), lambda i: (0, i)),
            pl.BlockSpec((rows, SUB), lambda i: (0, 0)),
        ],
        out_shape=[
            jax.ShapeDtypeStruct((rows, width), jnp.bfloat16),
            jax.ShapeDtypeStruct((rows, SUB), jnp.float32),
        ],
        scratch_shapes=[pltpu.VMEM((8, span, SUB), jnp.float32)],
        compiler_params=pltpu.CompilerParams(dimension_semantics=("arbitrary",)),
        interpret=interpret,
    )(ext, taps, skip, gate_feat)

D = 8192


LANE = 128
GROUP = 4
MODES_HALF = 8


def _rows_to_f32(p_ref, pf_ref):
    pf_ref[...] = p_ref[...].astype(jnp.float32)


def modal_end_kernel(p_ref, e_ref, out_ref, pf_ref):
    rows = p_ref.shape[0]
    _rows_to_f32(p_ref, pf_ref)
    lanes = [pl.ds(g * LANE, LANE) for g in range(GROUP)]
    e_lo = [e_ref[0:8, ln] for ln in lanes]
    e_hi = [e_ref[8:16, ln] for ln in lanes]

    def step(i, carry):
        lo, hi = carry
        row = pl.multiple_of(i * 8, 8)
        blocks = [pf_ref[pl.ds(row, 8), ln] for ln in lanes]
        for j in range(8):
            new_lo, new_hi = [], []
            for g in range(GROUP):
                pb = jnp.broadcast_to(blocks[g][j : j + 1], (8, LANE))
                new_lo.append(e_lo[g] * lo[g] + pb)
                new_hi.append(e_hi[g] * hi[g] + pb)
            lo, hi = new_lo, new_hi
        return lo, hi

    zero = [jnp.zeros((8, LANE), jnp.float32) for _ in range(GROUP)]
    lo, hi = lax.fori_loop(0, rows // 8, step, (zero, list(zero)))
    for g, ln in enumerate(lanes):
        out_ref[0:8, ln] = lo[g]
        out_ref[8:16, ln] = hi[g]


def modal_end_call(product, decay):
    rows, width = product.shape
    block = LANE * GROUP
    return pl.pallas_call(
        modal_end_kernel,
        grid=(width // block,),
        in_specs=[
            pl.BlockSpec((rows, block), lambda i: (0, i)),
            pl.BlockSpec((16, block), lambda i: (0, i)),
        ],
        out_specs=pl.BlockSpec((16, block), lambda i: (0, i)),
        out_shape=jax.ShapeDtypeStruct((16, width), jnp.float32),
        scratch_shapes=[pltpu.VMEM((rows, block), jnp.float32)],
    )(product, decay)


def modal_out_kernel(p_ref, e_ref, w_ref, s_ref, skip_ref, gate_ref, out_ref, pf_ref, z_ref):
    rows = p_ref.shape[0]
    _rows_to_f32(p_ref, pf_ref)
    lanes = [pl.ds(g * LANE, LANE) for g in range(GROUP)]
    e_lo = [e_ref[0:8, ln] for ln in lanes]
    e_hi = [e_ref[8:16, ln] for ln in lanes]
    w_lo = [w_ref[0:8, ln] for ln in lanes]
    w_hi = [w_ref[8:16, ln] for ln in lanes]

    def step(i, carry):
        lo, hi = carry
        row = pl.multiple_of(i * 8, 8)
        blocks = [pf_ref[pl.ds(row, 8), ln] for ln in lanes]
        for j in range(8):
            new_lo, new_hi = [], []
            for g in range(GROUP):
                pb = jnp.broadcast_to(blocks[g][j : j + 1], (8, LANE))
                a = e_lo[g] * lo[g] + pb
                b = e_hi[g] * hi[g] + pb
                z_ref[g, pl.ds(pl.multiple_of(i * 64 + 8 * j, 8), 8), :] = w_lo[g] * a + w_hi[g] * b
                new_lo.append(a)
                new_hi.append(b)
            lo, hi = new_lo, new_hi
        return lo, hi

    init_lo = [s_ref[0:8, ln] for ln in lanes]
    init_hi = [s_ref[8:16, ln] for ln in lanes]
    lax.fori_loop(0, rows // 8, step, (init_lo, init_hi))

    def reduce(i, carry):
        row = pl.multiple_of(i * 8, 8)
        for g, ln in enumerate(lanes):
            total = z_ref[g, pl.ds(i * 64, 8, stride=8), :]
            for j in range(1, 8):
                total = total + z_ref[g, pl.ds(i * 64 + j, 8, stride=8), :]
            own = pf_ref[pl.ds(row, 8), ln]
            skip = jnp.broadcast_to(skip_ref[:, ln], (8, LANE))
            conv = total + skip * own
            out_ref[pl.ds(row, 8), ln] = (gate_ref[pl.ds(row, 8), ln] * conv).astype(out_ref.dtype)
        return carry

    lax.fori_loop(0, rows // 8, reduce, 0)


def modal_out_call(product, decay, weight, start, skip, gate_feat):
    rows, width = product.shape
    block = LANE * GROUP
    return pl.pallas_call(
        modal_out_kernel,
        grid=(width // block,),
        in_specs=[
            pl.BlockSpec((rows, block), lambda i: (0, i)),
            pl.BlockSpec((16, block), lambda i: (0, i)),
            pl.BlockSpec((16, block), lambda i: (0, i)),
            pl.BlockSpec((16, block), lambda i: (0, i)),
            pl.BlockSpec((1, block), lambda i: (0, i)),
            pl.BlockSpec((rows, block), lambda i: (0, i)),
        ],
        out_specs=pl.BlockSpec((rows, block), lambda i: (0, i)),
        out_shape=jax.ShapeDtypeStruct((rows, width), jnp.bfloat16),
        scratch_shapes=[
            pltpu.VMEM((rows, block), jnp.float32),
            pltpu.VMEM((GROUP, rows * 8, LANE), jnp.float32),
        ],
    )(product, decay, weight, start, skip, gate_feat)


def scan_kernel(count, rows, f_ref, r_ref, out_ref, send_ref, recv_ref, send_sem, recv_sem):
    me = lax.axis_index("ctx")
    plan = []
    span = 1
    while span * 4 < count:
        plan.append([(span * i, span * i) for i in range(1, 4)])
        span *= 4
    plan.append([(1 + span * i, span * i) for i in range(count // span)])
    barrier = pltpu.get_barrier_semaphore()
    partners = sorted({shift for sends in plan for shift, _ in sends})
    for shift in partners:
        for other in (me + shift, me - shift):

            @pl.when(jnp.logical_and(other >= 0, other < count))
            def _():
                pl.semaphore_signal(
                    barrier, 1, device_id={"ctx": other}, device_id_type=pl.DeviceIdType.MESH
                )

    peers = 0
    for shift in partners:
        peers = peers + (1 - (me + shift) // count) + (me - shift + count) // count
    pl.semaphore_wait(barrier, peers)

    out_ref[...] = f_ref[...]
    for k, sends in enumerate(plan):
        send_ref[k] = out_ref[...]
        last = k == len(plan) - 1
        if last:
            out_ref[...] = jnp.zeros_like(out_ref)
        copies = []
        for i, (shift, power) in enumerate(sends):
            copy = pltpu.make_async_remote_copy(
                src_ref=send_ref.at[k],
                dst_ref=recv_ref.at[k, i],
                send_sem=send_sem.at[k, i],
                recv_sem=recv_sem.at[k, i],
                device_id={"ctx": me + shift},
                device_id_type=pl.DeviceIdType.MESH,
            )
            copies.append((shift, power, copy))

            @pl.when(me + shift < count)
            def _():
                copy.start()

        for i, (shift, power, copy) in enumerate(copies):

            @pl.when(me >= shift)
            def _():
                copy.wait_recv()
                if power == 0:
                    out_ref[...] = out_ref[...] + recv_ref[k, i]
                else:
                    factor = jnp.exp(r_ref[...] * (-1.0 * rows * power))
                    out_ref[...] = out_ref[...] + factor * recv_ref[k, i]

        for shift, power, copy in copies:

            @pl.when(me + shift < count)
            def _():
                copy.wait_send()


def scan_call(final_state, decay_rates, count, rows):
    shape = final_state.shape
    return pl.pallas_call(
        functools.partial(scan_kernel, count, rows),
        in_specs=[pl.BlockSpec(memory_space=pltpu.VMEM)] * 2,
        out_specs=pl.BlockSpec(memory_space=pltpu.VMEM),
        out_shape=jax.ShapeDtypeStruct(shape, jnp.float32),
        scratch_shapes=[
            pltpu.VMEM((3,) + shape, jnp.float32),
            pltpu.VMEM((3, 4) + shape, jnp.float32),
            pltpu.SemaphoreType.DMA((3, 4)),
            pltpu.SemaphoreType.DMA((3, 4)),
        ],
        compiler_params=pltpu.CompilerParams(collective_id=0, has_side_effects=True),
    )(final_state, decay_rates)


def passed_along(value, axis, steps):
    count = lax.axis_size(axis)
    first, last = (max(0, -steps), min(count, count - steps))
    return lax.ppermute(value, axis, [(source, source + steps) for source in range(first, last)])


def short_filter(extended, weights):
    return weights[0] * extended[2:] + weights[1] * extended[1:-1] + weights[2] * extended[:-2]


def medium_conv(extended, taps, row_count):
    tap_count = taps.shape[0]
    total = jnp.zeros((row_count, taps.shape[1]), jnp.float32)
    for offset in range(tap_count):
        start = tap_count - 1 - offset
        total = total + taps[offset] * extended[start : start + row_count]
    return total


def body(
    gate_medium,
    key_medium,
    value_medium,
    short_medium,
    filter_medium,
    skip_medium,
    norm_gain,
    gate_long,
    key_long,
    short_long,
    decay_rates,
    residues,
    skip_long,
):
    row_count = gate_medium.shape[0]
    tap_count = filter_medium.shape[0]
    width_local = gate_medium.shape[1]
    late_product = (
        short_filter(key_medium, short_medium[1]) * short_filter(value_medium, short_medium[2])
    ).astype(jnp.bfloat16)
    rim_gate, rim_key, rim_value, rim_product = passed_along(
        (gate_medium[-2:], key_medium[-2:], value_medium[-2:], late_product[-(tap_count - 1) :]),
        "ctx",
        1,
    )
    head_key = short_filter(jnp.concatenate([rim_key, key_medium[:2]], 0), short_medium[1])
    head_value = short_filter(jnp.concatenate([rim_value, value_medium[:2]], 0), short_medium[2])
    head_product = (head_key * head_value).astype(jnp.bfloat16)
    product = jnp.concatenate([rim_product, head_product, late_product], 0)
    gate_feat = short_filter(jnp.concatenate([rim_gate, gate_medium], 0), short_medium[0])
    extended = jnp.concatenate([jnp.zeros((1, width_local), jnp.bfloat16), product], 0)
    mixed_medium, partial_squares = medium_call(
        extended, filter_medium, skip_medium[None, :], gate_feat
    )
    squares = jnp.sum(partial_squares, axis=1)
    ring = lax.axis_size("ch")
    total_squares = squares
    for shift in range(1, ring):
        total_squares = total_squares + lax.ppermute(
            squares, "ch", [(source, (source + shift) % ring) for source in range(ring)]
        )
    inverse = lax.rsqrt(total_squares / D + 1e-06)
    normed = (mixed_medium * norm_gain * inverse[:, None]).astype(jnp.bfloat16)
    rim_gate_long, rim_key_long, rim_normed = passed_along(
        (gate_long[-2:], key_long[-2:], normed[-2:]), "ctx", 1
    )
    gate_feat_long = short_filter(jnp.concatenate([rim_gate_long, gate_long], 0), short_long[0])
    key_feat_long = short_filter(jnp.concatenate([rim_key_long, key_long], 0), short_long[1])
    value_feat_long = short_filter(jnp.concatenate([rim_normed, normed], 0), short_long[2])
    product_long = (key_feat_long * value_feat_long).astype(jnp.bfloat16)
    mode_weight = residues * jnp.sqrt(-jnp.expm1(-2.0 * decay_rates))
    step_decay = jnp.exp(-decay_rates)
    final_state = modal_end_call(product_long, step_decay)
    incoming = scan_call(final_state, decay_rates, lax.axis_size("ctx"), row_count)
    mixed_long = modal_out_call(
        product_long, step_decay, mode_weight, incoming, skip_long[None, :], gate_feat_long
    )
    return (mixed_medium, mixed_long)


def solution(mesh):
    placed = (
        P("ctx", "ch"),
        P("ctx", "ch"),
        P("ctx", "ch"),
        P(None, None, "ch"),
        P(None, "ch"),
        P("ch"),
        P("ch"),
        P("ctx", "ch"),
        P("ctx", "ch"),
        P(None, None, "ch"),
        P(None, "ch"),
        P(None, "ch"),
        P("ch"),
    )
    return jax.shard_map(
        body,
        mesh=mesh,
        in_specs=placed,
        out_specs=(P("ctx", "ch"), P("ctx", "ch")),
        check_vma=False,
    )
```

```python
import functools
import jax
import jax.numpy as jnp
from jax import lax
from jax.sharding import PartitionSpec as P
from jax.experimental import pallas as pl
from jax.experimental.pallas import tpu as pltpu

TAPS = 128
SUB = 128
RB = 8


def medium_kernel(ext_ref, f_ref, skip_ref, gate_ref, out_ref, ss_ref, q_ref):
    rows = out_ref.shape[0]
    width = out_ref.shape[1]
    span = ext_ref.shape[0]

    @pl.when(pl.program_id(0) == 0)
    def _():
        ss_ref[...] = jnp.zeros_like(ss_ref)

    for h in range(width // SUB):
        lanes = pl.ds(h * SUB, SUB)
        ext = ext_ref[:, lanes].astype(jnp.float32)
        for b in range(8):
            q_ref[b, 8:, :] = ext[8 - b : span - b]

        def block(kb, carry):
            acc = [jnp.zeros((8, SUB), jnp.float32) for _ in range(RB)]
            start = pl.multiple_of(kb * (8 * RB) + 8, 8)
            for b in range(8):
                qv = q_ref[b, pl.ds(start, 8 * (RB + 15)), :]
                for a in range(16):
                    w = jnp.broadcast_to(f_ref[pl.ds(8 * a + b, 1), lanes], (8, SUB))
                    for kk in range(RB):
                        v = kk + 15 - a
                        acc[kk] = acc[kk] + w * qv[8 * v : 8 * v + 8]
            skip = jnp.broadcast_to(skip_ref[:, lanes], (8, SUB))
            for kk in range(RB):
                row = pl.multiple_of(kb * (8 * RB) + 8 * kk, 8)
                own = q_ref[0, pl.ds(row + TAPS, 8), :]
                conv = acc[kk] + skip * own
                mixed = (gate_ref[pl.ds(row, 8), lanes] * conv).astype(jnp.bfloat16)
                out_ref[pl.ds(row, 8), lanes] = mixed
                m = mixed.astype(jnp.float32)
                ss_ref[pl.ds(row, 8), :] += m * m
            return carry

        lax.fori_loop(0, rows // (8 * RB), block, 0)


def medium_call(ext, taps, skip, gate_feat, block=512, interpret=False):
    span, width = ext.shape
    rows = gate_feat.shape[0]
    grid = (width // block,)
    return pl.pallas_call(
        medium_kernel,
        grid=grid,
        in_specs=[
            pl.BlockSpec((span, block), lambda i: (0, i)),
            pl.BlockSpec((TAPS, block), lambda i: (0, i)),
            pl.BlockSpec((1, block), lambda i: (0, i)),
            pl.BlockSpec((rows, block), lambda i: (0, i)),
        ],
        out_specs=[
            pl.BlockSpec((rows, block), lambda i: (0, i)),
            pl.BlockSpec((rows, SUB), lambda i: (0, 0)),
        ],
        out_shape=[
            jax.ShapeDtypeStruct((rows, width), jnp.bfloat16),
            jax.ShapeDtypeStruct((rows, SUB), jnp.float32),
        ],
        scratch_shapes=[pltpu.VMEM((8, span, SUB), jnp.float32)],
        compiler_params=pltpu.CompilerParams(dimension_semantics=("arbitrary",)),
        interpret=interpret,
    )(ext, taps, skip, gate_feat)

D = 8192


LANE = 128
GROUP = 4
MODES_HALF = 8


def _rows_to_f32(p_ref, pf_ref):
    pf_ref[...] = p_ref[...].astype(jnp.float32)


def modal_end_kernel(p_ref, e_ref, out_ref, pf_ref):
    rows = p_ref.shape[0]
    _rows_to_f32(p_ref, pf_ref)
    lanes = [pl.ds(g * LANE, LANE) for g in range(GROUP)]
    e_lo = [e_ref[0:8, ln] for ln in lanes]
    e_hi = [e_ref[8:16, ln] for ln in lanes]

    def step(i, carry):
        lo, hi = carry
        row = pl.multiple_of(i * 8, 8)
        blocks = [pf_ref[pl.ds(row, 8), ln] for ln in lanes]
        for j in range(8):
            new_lo, new_hi = [], []
            for g in range(GROUP):
                pb = jnp.broadcast_to(blocks[g][j : j + 1], (8, LANE))
                new_lo.append(e_lo[g] * lo[g] + pb)
                new_hi.append(e_hi[g] * hi[g] + pb)
            lo, hi = new_lo, new_hi
        return lo, hi

    zero = [jnp.zeros((8, LANE), jnp.float32) for _ in range(GROUP)]
    lo, hi = lax.fori_loop(0, rows // 8, step, (zero, list(zero)))
    for g, ln in enumerate(lanes):
        out_ref[0:8, ln] = lo[g]
        out_ref[8:16, ln] = hi[g]


def modal_end_call(product, decay):
    rows, width = product.shape
    block = LANE * GROUP
    return pl.pallas_call(
        modal_end_kernel,
        grid=(width // block,),
        in_specs=[
            pl.BlockSpec((rows, block), lambda i: (0, i)),
            pl.BlockSpec((16, block), lambda i: (0, i)),
        ],
        out_specs=pl.BlockSpec((16, block), lambda i: (0, i)),
        out_shape=jax.ShapeDtypeStruct((16, width), jnp.float32),
        scratch_shapes=[pltpu.VMEM((rows, block), jnp.float32)],
    )(product, decay)


def modal_out_kernel(p_ref, e_ref, w_ref, s_ref, skip_ref, gate_ref, out_ref, pf_ref, z_ref):
    rows = p_ref.shape[0]
    _rows_to_f32(p_ref, pf_ref)
    lanes = [pl.ds(g * LANE, LANE) for g in range(GROUP)]
    e_lo = [e_ref[0:8, ln] for ln in lanes]
    e_hi = [e_ref[8:16, ln] for ln in lanes]
    w_lo = [w_ref[0:8, ln] for ln in lanes]
    w_hi = [w_ref[8:16, ln] for ln in lanes]

    def step(i, carry):
        lo, hi = carry
        row = pl.multiple_of(i * 8, 8)
        blocks = [pf_ref[pl.ds(row, 8), ln] for ln in lanes]
        for j in range(8):
            new_lo, new_hi = [], []
            for g in range(GROUP):
                pb = jnp.broadcast_to(blocks[g][j : j + 1], (8, LANE))
                a = e_lo[g] * lo[g] + pb
                b = e_hi[g] * hi[g] + pb
                z_ref[g, pl.ds(pl.multiple_of(i * 64 + 8 * j, 8), 8), :] = w_lo[g] * a + w_hi[g] * b
                new_lo.append(a)
                new_hi.append(b)
            lo, hi = new_lo, new_hi
        return lo, hi

    init_lo = [s_ref[0:8, ln] for ln in lanes]
    init_hi = [s_ref[8:16, ln] for ln in lanes]
    lax.fori_loop(0, rows // 8, step, (init_lo, init_hi))

    def reduce(i, carry):
        row = pl.multiple_of(i * 8, 8)
        for g, ln in enumerate(lanes):
            total = z_ref[g, pl.ds(i * 64, 8, stride=8), :]
            for j in range(1, 8):
                total = total + z_ref[g, pl.ds(i * 64 + j, 8, stride=8), :]
            own = pf_ref[pl.ds(row, 8), ln]
            skip = jnp.broadcast_to(skip_ref[:, ln], (8, LANE))
            conv = total + skip * own
            out_ref[pl.ds(row, 8), ln] = (gate_ref[pl.ds(row, 8), ln] * conv).astype(out_ref.dtype)
        return carry

    lax.fori_loop(0, rows // 8, reduce, 0)


def modal_out_call(product, decay, weight, start, skip, gate_feat):
    rows, width = product.shape
    block = LANE * GROUP
    return pl.pallas_call(
        modal_out_kernel,
        grid=(width // block,),
        in_specs=[
            pl.BlockSpec((rows, block), lambda i: (0, i)),
            pl.BlockSpec((16, block), lambda i: (0, i)),
            pl.BlockSpec((16, block), lambda i: (0, i)),
            pl.BlockSpec((16, block), lambda i: (0, i)),
            pl.BlockSpec((1, block), lambda i: (0, i)),
            pl.BlockSpec((rows, block), lambda i: (0, i)),
        ],
        out_specs=pl.BlockSpec((rows, block), lambda i: (0, i)),
        out_shape=jax.ShapeDtypeStruct((rows, width), jnp.bfloat16),
        scratch_shapes=[
            pltpu.VMEM((rows, block), jnp.float32),
            pltpu.VMEM((GROUP, rows * 8, LANE), jnp.float32),
        ],
    )(product, decay, weight, start, skip, gate_feat)


def scan_kernel(count, rows, f_ref, r_ref, out_ref, send_ref, recv_ref, send_sem, recv_sem):
    me = lax.axis_index("ctx")
    plan = []
    span = 1
    while span * 4 < count:
        plan.append([(span * i, span * i) for i in range(1, 4)])
        span *= 4
    plan.append([(1 + span * i, span * i) for i in range(count // span)])
    barrier = pltpu.get_barrier_semaphore()
    partners = sorted({shift for sends in plan for shift, _ in sends})
    for shift in partners:
        for other in (me + shift, me - shift):

            @pl.when(jnp.logical_and(other >= 0, other < count))
            def _():
                pl.semaphore_signal(
                    barrier, 1, device_id={"ctx": other}, device_id_type=pl.DeviceIdType.MESH
                )

    peers = 0
    for shift in partners:
        peers = peers + (1 - (me + shift) // count) + (me - shift + count) // count
    pl.semaphore_wait(barrier, peers)

    out_ref[...] = f_ref[...]
    for k, sends in enumerate(plan):
        send_ref[k] = out_ref[...]
        last = k == len(plan) - 1
        if last:
            out_ref[...] = jnp.zeros_like(out_ref)
        copies = []
        for i, (shift, power) in enumerate(sends):
            copy = pltpu.make_async_remote_copy(
                src_ref=send_ref.at[k],
                dst_ref=recv_ref.at[k, i],
                send_sem=send_sem.at[k, i],
                recv_sem=recv_sem.at[k, i],
                device_id={"ctx": me + shift},
                device_id_type=pl.DeviceIdType.MESH,
            )
            copies.append((shift, power, copy))

            @pl.when(me + shift < count)
            def _():
                copy.start()

        for i, (shift, power, copy) in enumerate(copies):

            @pl.when(me >= shift)
            def _():
                copy.wait_recv()
                if power == 0:
                    out_ref[...] = out_ref[...] + recv_ref[k, i]
                else:
                    factor = jnp.exp(r_ref[...] * (-1.0 * rows * power))
                    out_ref[...] = out_ref[...] + factor * recv_ref[k, i]

        for shift, power, copy in copies:

            @pl.when(me + shift < count)
            def _():
                copy.wait_send()


def scan_call(final_state, decay_rates, count, rows):
    shape = final_state.shape
    return pl.pallas_call(
        functools.partial(scan_kernel, count, rows),
        in_specs=[pl.BlockSpec(memory_space=pltpu.VMEM)] * 2,
        out_specs=pl.BlockSpec(memory_space=pltpu.VMEM),
        out_shape=jax.ShapeDtypeStruct(shape, jnp.float32),
        scratch_shapes=[
            pltpu.VMEM((3,) + shape, jnp.float32),
            pltpu.VMEM((3, 4) + shape, jnp.float32),
            pltpu.SemaphoreType.DMA((3, 4)),
            pltpu.SemaphoreType.DMA((3, 4)),
        ],
        compiler_params=pltpu.CompilerParams(collective_id=0, has_side_effects=True),
    )(final_state, decay_rates)


def passed_along(value, axis, steps):
    count = lax.axis_size(axis)
    first, last = (max(0, -steps), min(count, count - steps))
    return lax.ppermute(value, axis, [(source, source + steps) for source in range(first, last)])


def short_filter(extended, weights):
    return weights[0] * extended[2:] + weights[1] * extended[1:-1] + weights[2] * extended[:-2]


def medium_conv(extended, taps, row_count):
    tap_count = taps.shape[0]
    total = jnp.zeros((row_count, taps.shape[1]), jnp.float32)
    for offset in range(tap_count):
        start = tap_count - 1 - offset
        total = total + taps[offset] * extended[start : start + row_count]
    return total


def body(
    gate_medium,
    key_medium,
    value_medium,
    short_medium,
    filter_medium,
    skip_medium,
    norm_gain,
    gate_long,
    key_long,
    short_long,
    decay_rates,
    residues,
    skip_long,
):
    row_count = gate_medium.shape[0]
    tap_count = filter_medium.shape[0]
    width_local = gate_medium.shape[1]
    late_product = (
        short_filter(key_medium, short_medium[1]) * short_filter(value_medium, short_medium[2])
    ).astype(jnp.bfloat16)
    halo = tap_count - 1
    rims = passed_along(
        jnp.concatenate(
            [
                late_product[-halo:],
                gate_medium[-2:],
                key_medium[-2:],
                value_medium[-2:],
                gate_long[-2:],
                key_long[-2:],
            ],
            0,
        ),
        "ctx",
        1,
    )
    rim_product = rims[:halo]
    rim_gate, rim_key, rim_value, rim_gate_long, rim_key_long = (
        rims[halo + 2 * i : halo + 2 * i + 2] for i in range(5)
    )
    head_key = short_filter(jnp.concatenate([rim_key, key_medium[:2]], 0), short_medium[1])
    head_value = short_filter(jnp.concatenate([rim_value, value_medium[:2]], 0), short_medium[2])
    head_product = (head_key * head_value).astype(jnp.bfloat16)
    product = jnp.concatenate([rim_product, head_product, late_product], 0)
    gate_feat = short_filter(jnp.concatenate([rim_gate, gate_medium], 0), short_medium[0])
    extended = jnp.concatenate([jnp.zeros((1, width_local), jnp.bfloat16), product], 0)
    mixed_medium, partial_squares = medium_call(
        extended, filter_medium, skip_medium[None, :], gate_feat
    )
    squares = jnp.sum(partial_squares, axis=1)
    ring = lax.axis_size("ch")
    total_squares = squares
    for shift in range(1, ring):
        total_squares = total_squares + lax.ppermute(
            squares, "ch", [(source, (source + shift) % ring) for source in range(ring)]
        )
    inverse = lax.rsqrt(total_squares / D + 1e-06)
    normed = (mixed_medium * norm_gain * inverse[:, None]).astype(jnp.bfloat16)
    rim_normed = passed_along(normed[-2:], "ctx", 1)
    gate_feat_long = short_filter(jnp.concatenate([rim_gate_long, gate_long], 0), short_long[0])
    key_feat_long = short_filter(jnp.concatenate([rim_key_long, key_long], 0), short_long[1])
    value_feat_long = short_filter(jnp.concatenate([rim_normed, normed], 0), short_long[2])
    product_long = (key_feat_long * value_feat_long).astype(jnp.bfloat16)
    mode_weight = residues * jnp.sqrt(-jnp.expm1(-2.0 * decay_rates))
    step_decay = jnp.exp(-decay_rates)
    final_state = modal_end_call(product_long, step_decay)
    incoming = scan_call(final_state, decay_rates, lax.axis_size("ctx"), row_count)
    mixed_long = modal_out_call(
        product_long, step_decay, mode_weight, incoming, skip_long[None, :], gate_feat_long
    )
    return (mixed_medium, mixed_long)


def solution(mesh):
    placed = (
        P("ctx", "ch"),
        P("ctx", "ch"),
        P("ctx", "ch"),
        P(None, None, "ch"),
        P(None, "ch"),
        P("ch"),
        P("ch"),
        P("ctx", "ch"),
        P("ctx", "ch"),
        P(None, None, "ch"),
        P(None, "ch"),
        P(None, "ch"),
        P("ch"),
    )
    return jax.shard_map(
        body,
        mesh=mesh,
        in_specs=placed,
        out_specs=(P("ctx", "ch"), P("ctx", "ch")),
        check_vma=False,
    )
```

```python
import functools
import jax
import jax.numpy as jnp
from jax import lax
from jax.sharding import PartitionSpec as P
from jax.experimental import pallas as pl
from jax.experimental.pallas import tpu as pltpu

TAPS = 128
SUB = 128
RB = 8


def medium_kernel(ext_ref, f_ref, skip_ref, gate_ref, out_ref, ss_ref, q_ref):
    rows = out_ref.shape[0]
    width = out_ref.shape[1]
    span = ext_ref.shape[0]

    @pl.when(pl.program_id(0) == 0)
    def _():
        ss_ref[...] = jnp.zeros_like(ss_ref)

    for h in range(width // SUB):
        lanes = pl.ds(h * SUB, SUB)
        ext = ext_ref[:, lanes].astype(jnp.float32)
        for b in range(8):
            q_ref[b, 8:, :] = ext[8 - b : span - b]

        def block(kb, carry):
            acc = [jnp.zeros((8, SUB), jnp.float32) for _ in range(RB)]
            start = pl.multiple_of(kb * (8 * RB) + 8, 8)
            for b in range(8):
                qv = q_ref[b, pl.ds(start, 8 * (RB + 15)), :]
                for a in range(16):
                    w = jnp.broadcast_to(f_ref[pl.ds(8 * a + b, 1), lanes], (8, SUB))
                    for kk in range(RB):
                        v = kk + 15 - a
                        acc[kk] = acc[kk] + w * qv[8 * v : 8 * v + 8]
            skip = jnp.broadcast_to(skip_ref[:, lanes], (8, SUB))
            for kk in range(RB):
                row = pl.multiple_of(kb * (8 * RB) + 8 * kk, 8)
                own = q_ref[0, pl.ds(row + TAPS, 8), :]
                conv = acc[kk] + skip * own
                mixed = (gate_ref[pl.ds(row, 8), lanes] * conv).astype(jnp.bfloat16)
                out_ref[pl.ds(row, 8), lanes] = mixed
                m = mixed.astype(jnp.float32)
                ss_ref[pl.ds(row, 8), :] += m * m
            return carry

        lax.fori_loop(0, rows // (8 * RB), block, 0)


def medium_call(ext, taps, skip, gate_feat, block=512, interpret=False):
    span, width = ext.shape
    rows = gate_feat.shape[0]
    grid = (width // block,)
    return pl.pallas_call(
        medium_kernel,
        grid=grid,
        in_specs=[
            pl.BlockSpec((span, block), lambda i: (0, i)),
            pl.BlockSpec((TAPS, block), lambda i: (0, i)),
            pl.BlockSpec((1, block), lambda i: (0, i)),
            pl.BlockSpec((rows, block), lambda i: (0, i)),
        ],
        out_specs=[
            pl.BlockSpec((rows, block), lambda i: (0, i)),
            pl.BlockSpec((rows, SUB), lambda i: (0, 0)),
        ],
        out_shape=[
            jax.ShapeDtypeStruct((rows, width), jnp.bfloat16),
            jax.ShapeDtypeStruct((rows, SUB), jnp.float32),
        ],
        scratch_shapes=[pltpu.VMEM((8, span, SUB), jnp.float32)],
        compiler_params=pltpu.CompilerParams(dimension_semantics=("arbitrary",)),
        interpret=interpret,
    )(ext, taps, skip, gate_feat)

D = 8192


LANE = 128
GROUP = 4
MODES_HALF = 8


def _rows_to_f32(p_ref, pf_ref):
    pf_ref[...] = p_ref[...].astype(jnp.float32)


def modal_end_kernel(p_ref, e_ref, out_ref, pf_ref):
    rows = p_ref.shape[0]
    _rows_to_f32(p_ref, pf_ref)
    lanes = [pl.ds(g * LANE, LANE) for g in range(GROUP)]
    e_lo = [e_ref[0:8, ln] for ln in lanes]
    e_hi = [e_ref[8:16, ln] for ln in lanes]

    def step(i, carry):
        lo, hi = carry
        row = pl.multiple_of(i * 8, 8)
        blocks = [pf_ref[pl.ds(row, 8), ln] for ln in lanes]
        for j in range(8):
            new_lo, new_hi = [], []
            for g in range(GROUP):
                pb = jnp.broadcast_to(blocks[g][j : j + 1], (8, LANE))
                new_lo.append(e_lo[g] * lo[g] + pb)
                new_hi.append(e_hi[g] * hi[g] + pb)
            lo, hi = new_lo, new_hi
        return lo, hi

    zero = [jnp.zeros((8, LANE), jnp.float32) for _ in range(GROUP)]
    lo, hi = lax.fori_loop(0, rows // 8, step, (zero, list(zero)))
    for g, ln in enumerate(lanes):
        out_ref[0:8, ln] = lo[g]
        out_ref[8:16, ln] = hi[g]


def modal_end_call(product, decay):
    rows, width = product.shape
    block = LANE * GROUP
    return pl.pallas_call(
        modal_end_kernel,
        grid=(width // block,),
        in_specs=[
            pl.BlockSpec((rows, block), lambda i: (0, i)),
            pl.BlockSpec((16, block), lambda i: (0, i)),
        ],
        out_specs=pl.BlockSpec((16, block), lambda i: (0, i)),
        out_shape=jax.ShapeDtypeStruct((16, width), jnp.float32),
        scratch_shapes=[pltpu.VMEM((rows, block), jnp.float32)],
    )(product, decay)


def modal_out_kernel(p_ref, e_ref, w_ref, s_ref, skip_ref, gate_ref, out_ref, pf_ref, z_ref):
    rows = p_ref.shape[0]
    _rows_to_f32(p_ref, pf_ref)
    lanes = [pl.ds(g * LANE, LANE) for g in range(GROUP)]
    e_lo = [e_ref[0:8, ln] for ln in lanes]
    e_hi = [e_ref[8:16, ln] for ln in lanes]
    w_lo = [w_ref[0:8, ln] for ln in lanes]
    w_hi = [w_ref[8:16, ln] for ln in lanes]

    def step(i, carry):
        lo, hi = carry
        row = pl.multiple_of(i * 8, 8)
        blocks = [pf_ref[pl.ds(row, 8), ln] for ln in lanes]
        for j in range(8):
            new_lo, new_hi = [], []
            for g in range(GROUP):
                pb = jnp.broadcast_to(blocks[g][j : j + 1], (8, LANE))
                a = e_lo[g] * lo[g] + pb
                b = e_hi[g] * hi[g] + pb
                z_ref[g, pl.ds(pl.multiple_of(i * 64 + 8 * j, 8), 8), :] = w_lo[g] * a + w_hi[g] * b
                new_lo.append(a)
                new_hi.append(b)
            lo, hi = new_lo, new_hi
        return lo, hi

    init_lo = [s_ref[0:8, ln] for ln in lanes]
    init_hi = [s_ref[8:16, ln] for ln in lanes]
    lax.fori_loop(0, rows // 8, step, (init_lo, init_hi))

    def reduce(i, carry):
        row = pl.multiple_of(i * 8, 8)
        for g, ln in enumerate(lanes):
            total = z_ref[g, pl.ds(i * 64, 8, stride=8), :]
            for j in range(1, 8):
                total = total + z_ref[g, pl.ds(i * 64 + j, 8, stride=8), :]
            own = pf_ref[pl.ds(row, 8), ln]
            skip = jnp.broadcast_to(skip_ref[:, ln], (8, LANE))
            conv = total + skip * own
            out_ref[pl.ds(row, 8), ln] = (gate_ref[pl.ds(row, 8), ln] * conv).astype(out_ref.dtype)
        return carry

    lax.fori_loop(0, rows // 8, reduce, 0)


def modal_out_call(product, decay, weight, start, skip, gate_feat):
    rows, width = product.shape
    block = LANE * GROUP
    return pl.pallas_call(
        modal_out_kernel,
        grid=(width // block,),
        in_specs=[
            pl.BlockSpec((rows, block), lambda i: (0, i)),
            pl.BlockSpec((16, block), lambda i: (0, i)),
            pl.BlockSpec((16, block), lambda i: (0, i)),
            pl.BlockSpec((16, block), lambda i: (0, i)),
            pl.BlockSpec((1, block), lambda i: (0, i)),
            pl.BlockSpec((rows, block), lambda i: (0, i)),
        ],
        out_specs=pl.BlockSpec((rows, block), lambda i: (0, i)),
        out_shape=jax.ShapeDtypeStruct((rows, width), jnp.bfloat16),
        scratch_shapes=[
            pltpu.VMEM((rows, block), jnp.float32),
            pltpu.VMEM((GROUP, rows * 8, LANE), jnp.float32),
        ],
    )(product, decay, weight, start, skip, gate_feat)


def scan_kernel(count, rows, f_ref, r_ref, out_ref, send_ref, recv_ref, send_sem, recv_sem):
    me = lax.axis_index("ctx")
    plan = []
    span = 1
    while span * 4 < count:
        plan.append([(span * i, span * i) for i in range(1, 4)])
        span *= 4
    plan.append([(1 + span * i, span * i) for i in range(count // span)])
    barrier = pltpu.get_barrier_semaphore()
    partners = sorted({shift for sends in plan for shift, _ in sends})
    for shift in partners:
        for other in (me + shift, me - shift):

            @pl.when(jnp.logical_and(other >= 0, other < count))
            def _():
                pl.semaphore_signal(
                    barrier, 1, device_id={"ctx": other}, device_id_type=pl.DeviceIdType.MESH
                )

    peers = 0
    for shift in partners:
        peers = peers + (1 - (me + shift) // count) + (me - shift + count) // count
    pl.semaphore_wait(barrier, peers)

    out_ref[...] = f_ref[...]
    for k, sends in enumerate(plan):
        send_ref[k] = out_ref[...].astype(send_ref.dtype)
        last = k == len(plan) - 1
        if last:
            out_ref[...] = jnp.zeros_like(out_ref)
        copies = []
        for i, (shift, power) in enumerate(sends):
            copy = pltpu.make_async_remote_copy(
                src_ref=send_ref.at[k],
                dst_ref=recv_ref.at[k, i],
                send_sem=send_sem.at[k, i],
                recv_sem=recv_sem.at[k, i],
                device_id={"ctx": me + shift},
                device_id_type=pl.DeviceIdType.MESH,
            )
            copies.append((shift, power, copy))

            @pl.when(me + shift < count)
            def _():
                copy.start()

        for i, (shift, power, copy) in enumerate(copies):

            @pl.when(me >= shift)
            def _():
                copy.wait_recv()
                if power == 0:
                    out_ref[...] = out_ref[...] + recv_ref[k, i].astype(jnp.float32)
                else:
                    factor = jnp.exp(r_ref[...] * (-1.0 * rows * power))
                    out_ref[...] = out_ref[...] + factor * recv_ref[k, i].astype(jnp.float32)

        for shift, power, copy in copies:

            @pl.when(me + shift < count)
            def _():
                copy.wait_send()


def scan_call(final_state, decay_rates, count, rows):
    shape = final_state.shape
    return pl.pallas_call(
        functools.partial(scan_kernel, count, rows),
        in_specs=[pl.BlockSpec(memory_space=pltpu.VMEM)] * 2,
        out_specs=pl.BlockSpec(memory_space=pltpu.VMEM),
        out_shape=jax.ShapeDtypeStruct(shape, jnp.float32),
        scratch_shapes=[
            pltpu.VMEM((3,) + shape, jnp.bfloat16),
            pltpu.VMEM((3, 4) + shape, jnp.bfloat16),
            pltpu.SemaphoreType.DMA((3, 4)),
            pltpu.SemaphoreType.DMA((3, 4)),
        ],
        compiler_params=pltpu.CompilerParams(collective_id=0, has_side_effects=True),
    )(final_state, decay_rates)


def passed_along(value, axis, steps):
    count = lax.axis_size(axis)
    first, last = (max(0, -steps), min(count, count - steps))
    return lax.ppermute(value, axis, [(source, source + steps) for source in range(first, last)])


def short_filter(extended, weights):
    return weights[0] * extended[2:] + weights[1] * extended[1:-1] + weights[2] * extended[:-2]


def medium_conv(extended, taps, row_count):
    tap_count = taps.shape[0]
    total = jnp.zeros((row_count, taps.shape[1]), jnp.float32)
    for offset in range(tap_count):
        start = tap_count - 1 - offset
        total = total + taps[offset] * extended[start : start + row_count]
    return total


def body(
    gate_medium,
    key_medium,
    value_medium,
    short_medium,
    filter_medium,
    skip_medium,
    norm_gain,
    gate_long,
    key_long,
    short_long,
    decay_rates,
    residues,
    skip_long,
):
    row_count = gate_medium.shape[0]
    tap_count = filter_medium.shape[0]
    width_local = gate_medium.shape[1]
    late_product = (
        short_filter(key_medium, short_medium[1]) * short_filter(value_medium, short_medium[2])
    ).astype(jnp.bfloat16)
    halo = tap_count - 1
    rims = passed_along(
        jnp.concatenate(
            [
                late_product[-halo:],
                gate_medium[-2:],
                key_medium[-2:],
                value_medium[-2:],
                gate_long[-2:],
                key_long[-2:],
            ],
            0,
        ),
        "ctx",
        1,
    )
    rim_product = rims[:halo]
    rim_gate, rim_key, rim_value, rim_gate_long, rim_key_long = (
        rims[halo + 2 * i : halo + 2 * i + 2] for i in range(5)
    )
    head_key = short_filter(jnp.concatenate([rim_key, key_medium[:2]], 0), short_medium[1])
    head_value = short_filter(jnp.concatenate([rim_value, value_medium[:2]], 0), short_medium[2])
    head_product = (head_key * head_value).astype(jnp.bfloat16)
    product = jnp.concatenate([rim_product, head_product, late_product], 0)
    gate_feat = short_filter(jnp.concatenate([rim_gate, gate_medium], 0), short_medium[0])
    extended = jnp.concatenate([jnp.zeros((1, width_local), jnp.bfloat16), product], 0)
    mixed_medium, partial_squares = medium_call(
        extended, filter_medium, skip_medium[None, :], gate_feat
    )
    squares = jnp.sum(partial_squares, axis=1)
    ring = lax.axis_size("ch")
    total_squares = squares
    for shift in range(1, ring):
        total_squares = total_squares + lax.ppermute(
            squares, "ch", [(source, (source + shift) % ring) for source in range(ring)]
        )
    inverse = lax.rsqrt(total_squares / D + 1e-06)
    normed = (mixed_medium * norm_gain * inverse[:, None]).astype(jnp.bfloat16)
    rim_normed = passed_along(normed[-2:], "ctx", 1)
    gate_feat_long = short_filter(jnp.concatenate([rim_gate_long, gate_long], 0), short_long[0])
    key_feat_long = short_filter(jnp.concatenate([rim_key_long, key_long], 0), short_long[1])
    value_feat_long = short_filter(jnp.concatenate([rim_normed, normed], 0), short_long[2])
    product_long = (key_feat_long * value_feat_long).astype(jnp.bfloat16)
    mode_weight = residues * jnp.sqrt(-jnp.expm1(-2.0 * decay_rates))
    step_decay = jnp.exp(-decay_rates)
    final_state = modal_end_call(product_long, step_decay)
    incoming = scan_call(final_state, decay_rates, lax.axis_size("ctx"), row_count)
    mixed_long = modal_out_call(
        product_long, step_decay, mode_weight, incoming, skip_long[None, :], gate_feat_long
    )
    return (mixed_medium, mixed_long)


def solution(mesh):
    placed = (
        P("ctx", "ch"),
        P("ctx", "ch"),
        P("ctx", "ch"),
        P(None, None, "ch"),
        P(None, "ch"),
        P("ch"),
        P("ch"),
        P("ctx", "ch"),
        P("ctx", "ch"),
        P(None, None, "ch"),
        P(None, "ch"),
        P(None, "ch"),
        P("ch"),
    )
    return jax.shard_map(
        body,
        mesh=mesh,
        in_specs=placed,
        out_specs=(P("ctx", "ch"), P("ctx", "ch")),
        check_vma=False,
    )
```

```python
import functools
import jax
import jax.numpy as jnp
from jax import lax
from jax.sharding import PartitionSpec as P
from jax.experimental import pallas as pl
from jax.experimental.pallas import tpu as pltpu

TAPS = 128
SUB = 128
RB = 8


def medium_kernel(ext_ref, f_ref, skip_ref, gate_ref, out_ref, ss_ref, q_ref):
    rows = out_ref.shape[0]
    width = out_ref.shape[1]
    span = ext_ref.shape[0]

    @pl.when(pl.program_id(0) == 0)
    def _():
        ss_ref[...] = jnp.zeros_like(ss_ref)

    for h in range(width // SUB):
        lanes = pl.ds(h * SUB, SUB)
        ext = ext_ref[:, lanes].astype(jnp.float32)
        for b in range(8):
            q_ref[b, 8:, :] = ext[8 - b : span - b]

        def block(kb, carry):
            acc = [jnp.zeros((8, SUB), jnp.float32) for _ in range(RB)]
            start = pl.multiple_of(kb * (8 * RB) + 8, 8)
            for b in range(8):
                qv = q_ref[b, pl.ds(start, 8 * (RB + 15)), :]
                for a in range(16):
                    w = jnp.broadcast_to(f_ref[pl.ds(8 * a + b, 1), lanes], (8, SUB))
                    for kk in range(RB):
                        v = kk + 15 - a
                        acc[kk] = acc[kk] + w * qv[8 * v : 8 * v + 8]
            skip = jnp.broadcast_to(skip_ref[:, lanes], (8, SUB))
            for kk in range(RB):
                row = pl.multiple_of(kb * (8 * RB) + 8 * kk, 8)
                own = q_ref[0, pl.ds(row + TAPS, 8), :]
                conv = acc[kk] + skip * own
                mixed = (gate_ref[pl.ds(row, 8), lanes] * conv).astype(jnp.bfloat16)
                out_ref[pl.ds(row, 8), lanes] = mixed
                m = mixed.astype(jnp.float32)
                ss_ref[pl.ds(row, 8), :] += m * m
            return carry

        lax.fori_loop(0, rows // (8 * RB), block, 0)


def medium_call(ext, taps, skip, gate_feat, block=512, interpret=False):
    span, width = ext.shape
    rows = gate_feat.shape[0]
    grid = (width // block,)
    return pl.pallas_call(
        medium_kernel,
        grid=grid,
        in_specs=[
            pl.BlockSpec((span, block), lambda i: (0, i)),
            pl.BlockSpec((TAPS, block), lambda i: (0, i)),
            pl.BlockSpec((1, block), lambda i: (0, i)),
            pl.BlockSpec((rows, block), lambda i: (0, i)),
        ],
        out_specs=[
            pl.BlockSpec((rows, block), lambda i: (0, i)),
            pl.BlockSpec((rows, SUB), lambda i: (0, 0)),
        ],
        out_shape=[
            jax.ShapeDtypeStruct((rows, width), jnp.bfloat16),
            jax.ShapeDtypeStruct((rows, SUB), jnp.float32),
        ],
        scratch_shapes=[pltpu.VMEM((8, span, SUB), jnp.float32)],
        compiler_params=pltpu.CompilerParams(dimension_semantics=("arbitrary",)),
        interpret=interpret,
    )(ext, taps, skip, gate_feat)

D = 8192


LANE = 128
GROUP = 4
MODES_HALF = 8


def _rows_to_f32(p_ref, pf_ref):
    pf_ref[...] = p_ref[...].astype(jnp.float32)


def modal_end_kernel(p_ref, e_ref, out_ref, pf_ref):
    rows = p_ref.shape[0]
    _rows_to_f32(p_ref, pf_ref)
    lanes = [pl.ds(g * LANE, LANE) for g in range(GROUP)]
    e_lo = [e_ref[0:8, ln] for ln in lanes]
    e_hi = [e_ref[8:16, ln] for ln in lanes]

    def step(i, carry):
        lo, hi = carry
        row = pl.multiple_of(i * 8, 8)
        blocks = [pf_ref[pl.ds(row, 8), ln] for ln in lanes]
        for j in range(8):
            new_lo, new_hi = [], []
            for g in range(GROUP):
                pb = jnp.broadcast_to(blocks[g][j : j + 1], (8, LANE))
                new_lo.append(e_lo[g] * lo[g] + pb)
                new_hi.append(e_hi[g] * hi[g] + pb)
            lo, hi = new_lo, new_hi
        return lo, hi

    zero = [jnp.zeros((8, LANE), jnp.float32) for _ in range(GROUP)]
    lo, hi = lax.fori_loop(0, rows // 8, step, (zero, list(zero)))
    for g, ln in enumerate(lanes):
        out_ref[0:8, ln] = lo[g]
        out_ref[8:16, ln] = hi[g]


def modal_end_call(product, decay):
    rows, width = product.shape
    block = LANE * GROUP
    return pl.pallas_call(
        modal_end_kernel,
        grid=(width // block,),
        in_specs=[
            pl.BlockSpec((rows, block), lambda i: (0, i)),
            pl.BlockSpec((16, block), lambda i: (0, i)),
        ],
        out_specs=pl.BlockSpec((16, block), lambda i: (0, i)),
        out_shape=jax.ShapeDtypeStruct((16, width), jnp.float32),
        scratch_shapes=[pltpu.VMEM((rows, block), jnp.float32)],
    )(product, decay)


def modal_out_kernel(p_ref, e_ref, w_ref, s_ref, skip_ref, gate_ref, out_ref, pf_ref, z_ref):
    rows = p_ref.shape[0]
    _rows_to_f32(p_ref, pf_ref)
    lanes = [pl.ds(g * LANE, LANE) for g in range(GROUP)]
    e_lo = [e_ref[0:8, ln] for ln in lanes]
    e_hi = [e_ref[8:16, ln] for ln in lanes]
    w_lo = [w_ref[0:8, ln] for ln in lanes]
    w_hi = [w_ref[8:16, ln] for ln in lanes]

    def step(i, carry):
        lo, hi = carry
        row = pl.multiple_of(i * 8, 8)
        blocks = [pf_ref[pl.ds(row, 8), ln] for ln in lanes]
        for j in range(8):
            new_lo, new_hi = [], []
            for g in range(GROUP):
                pb = jnp.broadcast_to(blocks[g][j : j + 1], (8, LANE))
                a = e_lo[g] * lo[g] + pb
                b = e_hi[g] * hi[g] + pb
                z_ref[g, pl.ds(pl.multiple_of(i * 64 + 8 * j, 8), 8), :] = w_lo[g] * a + w_hi[g] * b
                new_lo.append(a)
                new_hi.append(b)
            lo, hi = new_lo, new_hi
        return lo, hi

    init_lo = [s_ref[0:8, ln] for ln in lanes]
    init_hi = [s_ref[8:16, ln] for ln in lanes]
    lax.fori_loop(0, rows // 8, step, (init_lo, init_hi))

    def reduce(i, carry):
        row = pl.multiple_of(i * 8, 8)
        for g, ln in enumerate(lanes):
            total = z_ref[g, pl.ds(i * 64, 8, stride=8), :]
            for j in range(1, 8):
                total = total + z_ref[g, pl.ds(i * 64 + j, 8, stride=8), :]
            own = pf_ref[pl.ds(row, 8), ln]
            skip = jnp.broadcast_to(skip_ref[:, ln], (8, LANE))
            conv = total + skip * own
            out_ref[pl.ds(row, 8), ln] = (gate_ref[pl.ds(row, 8), ln] * conv).astype(out_ref.dtype)
        return carry

    lax.fori_loop(0, rows // 8, reduce, 0)


def modal_out_call(product, decay, weight, start, skip, gate_feat):
    rows, width = product.shape
    block = LANE * GROUP
    return pl.pallas_call(
        modal_out_kernel,
        grid=(width // block,),
        in_specs=[
            pl.BlockSpec((rows, block), lambda i: (0, i)),
            pl.BlockSpec((16, block), lambda i: (0, i)),
            pl.BlockSpec((16, block), lambda i: (0, i)),
            pl.BlockSpec((16, block), lambda i: (0, i)),
            pl.BlockSpec((1, block), lambda i: (0, i)),
            pl.BlockSpec((rows, block), lambda i: (0, i)),
        ],
        out_specs=pl.BlockSpec((rows, block), lambda i: (0, i)),
        out_shape=jax.ShapeDtypeStruct((rows, width), jnp.bfloat16),
        scratch_shapes=[
            pltpu.VMEM((rows, block), jnp.float32),
            pltpu.VMEM((GROUP, rows * 8, LANE), jnp.float32),
        ],
    )(product, decay, weight, start, skip, gate_feat)


PIECES = 4


def scan_kernel(count, rows, f_ref, r_ref, out_ref, send_ref, recv_ref, send_sem, recv_sem):
    me = lax.axis_index("ctx")
    piece = out_ref.shape[1] // PIECES
    plan = []
    span = 1
    while span * 4 < count:
        plan.append([(span * i, span * i) for i in range(1, 4)])
        span *= 4
    plan.append([(1 + span * i, span * i) for i in range(count // span)])
    barrier = pltpu.get_barrier_semaphore()
    partners = sorted({shift for sends in plan for shift, _ in sends})
    for shift in partners:
        for other in (me + shift, me - shift):

            @pl.when(jnp.logical_and(other >= 0, other < count))
            def _():
                pl.semaphore_signal(
                    barrier, 1, device_id={"ctx": other}, device_id_type=pl.DeviceIdType.MESH
                )

    peers = 0
    for shift in partners:
        peers = peers + (1 - (me + shift) // count) + (me - shift + count) // count
    pl.semaphore_wait(barrier, peers)

    out_ref[...] = f_ref[...]
    for k, sends in enumerate(plan):
        send_ref[k] = out_ref[...].astype(send_ref.dtype)
        last = k == len(plan) - 1
        if last:
            out_ref[...] = jnp.zeros_like(out_ref)
        copies = []
        for i, (shift, power) in enumerate(sends):
            parts = []
            for c in range(PIECES):
                lanes = pl.ds(c * piece, piece)
                parts.append(
                    pltpu.make_async_remote_copy(
                        src_ref=send_ref.at[k, :, lanes],
                        dst_ref=recv_ref.at[k, i, :, lanes],
                        send_sem=send_sem.at[k, i, c],
                        recv_sem=recv_sem.at[k, i, c],
                        device_id={"ctx": me + shift},
                        device_id_type=pl.DeviceIdType.MESH,
                    )
                )
            copies.append((shift, power, parts))

            @pl.when(me + shift < count)
            def _():
                for part in parts:
                    part.start()

        for i, (shift, power, parts) in enumerate(copies):

            @pl.when(me >= shift)
            def _():
                for part in parts:
                    part.wait_recv()
                if power == 0:
                    out_ref[...] = out_ref[...] + recv_ref[k, i].astype(jnp.float32)
                else:
                    factor = jnp.exp(r_ref[...] * (-1.0 * rows * power))
                    out_ref[...] = out_ref[...] + factor * recv_ref[k, i].astype(jnp.float32)

        for shift, power, parts in copies:

            @pl.when(me + shift < count)
            def _():
                for part in parts:
                    part.wait_send()


def scan_call(final_state, decay_rates, count, rows):
    shape = final_state.shape
    return pl.pallas_call(
        functools.partial(scan_kernel, count, rows),
        in_specs=[pl.BlockSpec(memory_space=pltpu.VMEM)] * 2,
        out_specs=pl.BlockSpec(memory_space=pltpu.VMEM),
        out_shape=jax.ShapeDtypeStruct(shape, jnp.float32),
        scratch_shapes=[
            pltpu.VMEM((3,) + shape, jnp.bfloat16),
            pltpu.VMEM((3, 4) + shape, jnp.bfloat16),
            pltpu.SemaphoreType.DMA((3, 4, PIECES)),
            pltpu.SemaphoreType.DMA((3, 4, PIECES)),
        ],
        compiler_params=pltpu.CompilerParams(collective_id=0, has_side_effects=True),
    )(final_state, decay_rates)


def passed_along(value, axis, steps):
    count = lax.axis_size(axis)
    first, last = (max(0, -steps), min(count, count - steps))
    return lax.ppermute(value, axis, [(source, source + steps) for source in range(first, last)])


def short_filter(extended, weights):
    return weights[0] * extended[2:] + weights[1] * extended[1:-1] + weights[2] * extended[:-2]


def medium_conv(extended, taps, row_count):
    tap_count = taps.shape[0]
    total = jnp.zeros((row_count, taps.shape[1]), jnp.float32)
    for offset in range(tap_count):
        start = tap_count - 1 - offset
        total = total + taps[offset] * extended[start : start + row_count]
    return total


def body(
    gate_medium,
    key_medium,
    value_medium,
    short_medium,
    filter_medium,
    skip_medium,
    norm_gain,
    gate_long,
    key_long,
    short_long,
    decay_rates,
    residues,
    skip_long,
):
    row_count = gate_medium.shape[0]
    tap_count = filter_medium.shape[0]
    width_local = gate_medium.shape[1]
    late_product = (
        short_filter(key_medium, short_medium[1]) * short_filter(value_medium, short_medium[2])
    ).astype(jnp.bfloat16)
    halo = tap_count - 1
    rims = passed_along(
        jnp.concatenate(
            [
                late_product[-halo:],
                gate_medium[-2:],
                key_medium[-2:],
                value_medium[-2:],
                gate_long[-2:],
                key_long[-2:],
            ],
            0,
        ),
        "ctx",
        1,
    )
    rim_product = rims[:halo]
    rim_gate, rim_key, rim_value, rim_gate_long, rim_key_long = (
        rims[halo + 2 * i : halo + 2 * i + 2] for i in range(5)
    )
    head_key = short_filter(jnp.concatenate([rim_key, key_medium[:2]], 0), short_medium[1])
    head_value = short_filter(jnp.concatenate([rim_value, value_medium[:2]], 0), short_medium[2])
    head_product = (head_key * head_value).astype(jnp.bfloat16)
    product = jnp.concatenate([rim_product, head_product, late_product], 0)
    gate_feat = short_filter(jnp.concatenate([rim_gate, gate_medium], 0), short_medium[0])
    extended = jnp.concatenate([jnp.zeros((1, width_local), jnp.bfloat16), product], 0)
    mixed_medium, partial_squares = medium_call(
        extended, filter_medium, skip_medium[None, :], gate_feat
    )
    squares = jnp.sum(partial_squares, axis=1)
    ring = lax.axis_size("ch")
    total_squares = squares
    for shift in range(1, ring):
        total_squares = total_squares + lax.ppermute(
            squares, "ch", [(source, (source + shift) % ring) for source in range(ring)]
        )
    inverse = lax.rsqrt(total_squares / D + 1e-06)
    normed = (mixed_medium * norm_gain * inverse[:, None]).astype(jnp.bfloat16)
    rim_normed = passed_along(normed[-2:], "ctx", 1)
    gate_feat_long = short_filter(jnp.concatenate([rim_gate_long, gate_long], 0), short_long[0])
    key_feat_long = short_filter(jnp.concatenate([rim_key_long, key_long], 0), short_long[1])
    value_feat_long = short_filter(jnp.concatenate([rim_normed, normed], 0), short_long[2])
    product_long = (key_feat_long * value_feat_long).astype(jnp.bfloat16)
    mode_weight = residues * jnp.sqrt(-jnp.expm1(-2.0 * decay_rates))
    step_decay = jnp.exp(-decay_rates)
    final_state = modal_end_call(product_long, step_decay)
    incoming = scan_call(final_state, decay_rates, lax.axis_size("ctx"), row_count)
    mixed_long = modal_out_call(
        product_long, step_decay, mode_weight, incoming, skip_long[None, :], gate_feat_long
    )
    return (mixed_medium, mixed_long)


def solution(mesh):
    placed = (
        P("ctx", "ch"),
        P("ctx", "ch"),
        P("ctx", "ch"),
        P(None, None, "ch"),
        P(None, "ch"),
        P("ch"),
        P("ch"),
        P("ctx", "ch"),
        P("ctx", "ch"),
        P(None, None, "ch"),
        P(None, "ch"),
        P(None, "ch"),
        P("ch"),
    )
    return jax.shard_map(
        body,
        mesh=mesh,
        in_specs=placed,
        out_specs=(P("ctx", "ch"), P("ctx", "ch")),
        check_vma=False,
    )
```

```python
import functools
import jax
import jax.numpy as jnp
from jax import lax
from jax.sharding import PartitionSpec as P
from jax.experimental import pallas as pl
from jax.experimental.pallas import tpu as pltpu

TAPS = 128
SUB = 128
RB = 8


def medium_kernel(ext_ref, f_ref, skip_ref, gate_ref, out_ref, ss_ref, q_ref):
    rows = out_ref.shape[0]
    width = out_ref.shape[1]
    span = ext_ref.shape[0]

    @pl.when(pl.program_id(0) == 0)
    def _():
        ss_ref[...] = jnp.zeros_like(ss_ref)

    for h in range(width // SUB):
        lanes = pl.ds(h * SUB, SUB)
        ext = ext_ref[:, lanes].astype(jnp.float32)
        for b in range(8):
            q_ref[b, 8:, :] = ext[8 - b : span - b]

        def block(kb, carry):
            acc = [jnp.zeros((8, SUB), jnp.float32) for _ in range(RB)]
            start = pl.multiple_of(kb * (8 * RB) + 8, 8)
            for b in range(8):
                qv = q_ref[b, pl.ds(start, 8 * (RB + 15)), :]
                for a in range(16):
                    w = jnp.broadcast_to(f_ref[pl.ds(8 * a + b, 1), lanes], (8, SUB))
                    for kk in range(RB):
                        v = kk + 15 - a
                        acc[kk] = acc[kk] + w * qv[8 * v : 8 * v + 8]
            skip = jnp.broadcast_to(skip_ref[:, lanes], (8, SUB))
            for kk in range(RB):
                row = pl.multiple_of(kb * (8 * RB) + 8 * kk, 8)
                own = q_ref[0, pl.ds(row + TAPS, 8), :]
                conv = acc[kk] + skip * own
                mixed = (gate_ref[pl.ds(row, 8), lanes] * conv).astype(jnp.bfloat16)
                out_ref[pl.ds(row, 8), lanes] = mixed
                m = mixed.astype(jnp.float32)
                ss_ref[pl.ds(row, 8), :] += m * m
            return carry

        lax.fori_loop(0, rows // (8 * RB), block, 0)


def medium_call(ext, taps, skip, gate_feat, block=512, interpret=False):
    span, width = ext.shape
    rows = gate_feat.shape[0]
    grid = (width // block,)
    return pl.pallas_call(
        medium_kernel,
        grid=grid,
        in_specs=[
            pl.BlockSpec((span, block), lambda i: (0, i)),
            pl.BlockSpec((TAPS, block), lambda i: (0, i)),
            pl.BlockSpec((1, block), lambda i: (0, i)),
            pl.BlockSpec((rows, block), lambda i: (0, i)),
        ],
        out_specs=[
            pl.BlockSpec((rows, block), lambda i: (0, i)),
            pl.BlockSpec((rows, SUB), lambda i: (0, 0)),
        ],
        out_shape=[
            jax.ShapeDtypeStruct((rows, width), jnp.bfloat16),
            jax.ShapeDtypeStruct((rows, SUB), jnp.float32),
        ],
        scratch_shapes=[pltpu.VMEM((8, span, SUB), jnp.float32)],
        compiler_params=pltpu.CompilerParams(dimension_semantics=("arbitrary",)),
        interpret=interpret,
    )(ext, taps, skip, gate_feat)

D = 8192


LANE = 128
GROUP = 4
MODES_HALF = 8


def _rows_to_f32(p_ref, pf_ref):
    pf_ref[...] = p_ref[...].astype(jnp.float32)


def modal_end_kernel(p_ref, e_ref, out_ref, pf_ref):
    rows = p_ref.shape[0]
    _rows_to_f32(p_ref, pf_ref)
    lanes = [pl.ds(g * LANE, LANE) for g in range(GROUP)]
    e_lo = [e_ref[0:8, ln] for ln in lanes]
    e_hi = [e_ref[8:16, ln] for ln in lanes]

    def step(i, carry):
        lo, hi = carry
        row = pl.multiple_of(i * 8, 8)
        blocks = [pf_ref[pl.ds(row, 8), ln] for ln in lanes]
        for j in range(8):
            new_lo, new_hi = [], []
            for g in range(GROUP):
                pb = jnp.broadcast_to(blocks[g][j : j + 1], (8, LANE))
                new_lo.append(e_lo[g] * lo[g] + pb)
                new_hi.append(e_hi[g] * hi[g] + pb)
            lo, hi = new_lo, new_hi
        return lo, hi

    zero = [jnp.zeros((8, LANE), jnp.float32) for _ in range(GROUP)]
    lo, hi = lax.fori_loop(0, rows // 8, step, (zero, list(zero)))
    for g, ln in enumerate(lanes):
        out_ref[0:8, ln] = lo[g]
        out_ref[8:16, ln] = hi[g]


def modal_end_call(product, decay):
    rows, width = product.shape
    block = LANE * GROUP
    return pl.pallas_call(
        modal_end_kernel,
        grid=(width // block,),
        in_specs=[
            pl.BlockSpec((rows, block), lambda i: (0, i)),
            pl.BlockSpec((16, block), lambda i: (0, i)),
        ],
        out_specs=pl.BlockSpec((16, block), lambda i: (0, i)),
        out_shape=jax.ShapeDtypeStruct((16, width), jnp.float32),
        scratch_shapes=[pltpu.VMEM((rows, block), jnp.float32)],
    )(product, decay)


def modal_out_kernel(p_ref, e_ref, w_ref, s_ref, skip_ref, gate_ref, out_ref, pf_ref, z_ref):
    rows = p_ref.shape[0]
    _rows_to_f32(p_ref, pf_ref)
    lanes = [pl.ds(g * LANE, LANE) for g in range(GROUP)]
    e_lo = [e_ref[0:8, ln] for ln in lanes]
    e_hi = [e_ref[8:16, ln] for ln in lanes]
    w_lo = [w_ref[0:8, ln] for ln in lanes]
    w_hi = [w_ref[8:16, ln] for ln in lanes]

    def step(i, carry):
        lo, hi = carry
        row = pl.multiple_of(i * 8, 8)
        blocks = [pf_ref[pl.ds(row, 8), ln] for ln in lanes]
        for j in range(8):
            new_lo, new_hi = [], []
            for g in range(GROUP):
                pb = jnp.broadcast_to(blocks[g][j : j + 1], (8, LANE))
                a = e_lo[g] * lo[g] + pb
                b = e_hi[g] * hi[g] + pb
                z_ref[g, pl.ds(pl.multiple_of(i * 64 + 8 * j, 8), 8), :] = w_lo[g] * a + w_hi[g] * b
                new_lo.append(a)
                new_hi.append(b)
            lo, hi = new_lo, new_hi
        return lo, hi

    init_lo = [s_ref[0:8, ln] for ln in lanes]
    init_hi = [s_ref[8:16, ln] for ln in lanes]
    lax.fori_loop(0, rows // 8, step, (init_lo, init_hi))

    def reduce(i, carry):
        row = pl.multiple_of(i * 8, 8)
        for g, ln in enumerate(lanes):
            total = z_ref[g, pl.ds(i * 64, 8, stride=8), :]
            for j in range(1, 8):
                total = total + z_ref[g, pl.ds(i * 64 + j, 8, stride=8), :]
            own = pf_ref[pl.ds(row, 8), ln]
            skip = jnp.broadcast_to(skip_ref[:, ln], (8, LANE))
            conv = total + skip * own
            out_ref[pl.ds(row, 8), ln] = (gate_ref[pl.ds(row, 8), ln] * conv).astype(out_ref.dtype)
        return carry

    lax.fori_loop(0, rows // 8, reduce, 0)


def modal_out_call(product, decay, weight, start, skip, gate_feat):
    rows, width = product.shape
    block = LANE * GROUP
    return pl.pallas_call(
        modal_out_kernel,
        grid=(width // block,),
        in_specs=[
            pl.BlockSpec((rows, block), lambda i: (0, i)),
            pl.BlockSpec((16, block), lambda i: (0, i)),
            pl.BlockSpec((16, block), lambda i: (0, i)),
            pl.BlockSpec((16, block), lambda i: (0, i)),
            pl.BlockSpec((1, block), lambda i: (0, i)),
            pl.BlockSpec((rows, block), lambda i: (0, i)),
        ],
        out_specs=pl.BlockSpec((rows, block), lambda i: (0, i)),
        out_shape=jax.ShapeDtypeStruct((rows, width), jnp.bfloat16),
        scratch_shapes=[
            pltpu.VMEM((rows, block), jnp.float32),
            pltpu.VMEM((GROUP, rows * 8, LANE), jnp.float32),
        ],
    )(product, decay, weight, start, skip, gate_feat)


def scan_kernel(count, rows, f_ref, r_ref, out_ref, send_ref, recv_ref, send_sem, recv_sem):
    me = lax.axis_index("ctx")
    plan = [[(1, 0)]]
    span = 1
    while span < count:
        plan.append([(span, span)])
        span *= 2
    barrier = pltpu.get_barrier_semaphore()
    partners = sorted({shift for sends in plan for shift, _ in sends})
    for shift in partners:
        for other in (me + shift, me - shift):

            @pl.when(jnp.logical_and(other >= 0, other < count))
            def _():
                pl.semaphore_signal(
                    barrier, 1, device_id={"ctx": other}, device_id_type=pl.DeviceIdType.MESH
                )

    peers = 0
    for shift in partners:
        peers = peers + (1 - (me + shift) // count) + (me - shift + count) // count
    pl.semaphore_wait(barrier, peers)

    out_ref[...] = f_ref[...]
    for k, sends in enumerate(plan):
        send_ref[k] = out_ref[...].astype(send_ref.dtype)
        if k == 0:
            out_ref[...] = jnp.zeros_like(out_ref)
        copies = []
        for i, (shift, power) in enumerate(sends):
            copy = pltpu.make_async_remote_copy(
                src_ref=send_ref.at[k],
                dst_ref=recv_ref.at[k, i],
                send_sem=send_sem.at[k, i],
                recv_sem=recv_sem.at[k, i],
                device_id={"ctx": me + shift},
                device_id_type=pl.DeviceIdType.MESH,
            )
            copies.append((shift, power, copy))

            @pl.when(me + shift < count)
            def _():
                copy.start()

        for i, (shift, power, copy) in enumerate(copies):

            @pl.when(me >= shift)
            def _():
                copy.wait_recv()
                if power == 0:
                    out_ref[...] = out_ref[...] + recv_ref[k, i].astype(jnp.float32)
                else:
                    factor = jnp.exp(r_ref[...] * (-1.0 * rows * power))
                    out_ref[...] = out_ref[...] + factor * recv_ref[k, i].astype(jnp.float32)

        for shift, power, copy in copies:

            @pl.when(me + shift < count)
            def _():
                copy.wait_send()


def scan_call(final_state, decay_rates, count, rows):
    shape = final_state.shape
    rounds = 1
    while (1 << (rounds - 1)) < count:
        rounds += 1
    return pl.pallas_call(
        functools.partial(scan_kernel, count, rows),
        in_specs=[pl.BlockSpec(memory_space=pltpu.VMEM)] * 2,
        out_specs=pl.BlockSpec(memory_space=pltpu.VMEM),
        out_shape=jax.ShapeDtypeStruct(shape, jnp.float32),
        scratch_shapes=[
            pltpu.VMEM((rounds,) + shape, jnp.bfloat16),
            pltpu.VMEM((rounds, 1) + shape, jnp.bfloat16),
            pltpu.SemaphoreType.DMA((rounds, 1)),
            pltpu.SemaphoreType.DMA((rounds, 1)),
        ],
        compiler_params=pltpu.CompilerParams(collective_id=0, has_side_effects=True),
    )(final_state, decay_rates)


def passed_along(value, axis, steps):
    count = lax.axis_size(axis)
    first, last = (max(0, -steps), min(count, count - steps))
    return lax.ppermute(value, axis, [(source, source + steps) for source in range(first, last)])


def short_filter(extended, weights):
    return weights[0] * extended[2:] + weights[1] * extended[1:-1] + weights[2] * extended[:-2]


def medium_conv(extended, taps, row_count):
    tap_count = taps.shape[0]
    total = jnp.zeros((row_count, taps.shape[1]), jnp.float32)
    for offset in range(tap_count):
        start = tap_count - 1 - offset
        total = total + taps[offset] * extended[start : start + row_count]
    return total


def body(
    gate_medium,
    key_medium,
    value_medium,
    short_medium,
    filter_medium,
    skip_medium,
    norm_gain,
    gate_long,
    key_long,
    short_long,
    decay_rates,
    residues,
    skip_long,
):
    row_count = gate_medium.shape[0]
    tap_count = filter_medium.shape[0]
    width_local = gate_medium.shape[1]
    late_product = (
        short_filter(key_medium, short_medium[1]) * short_filter(value_medium, short_medium[2])
    ).astype(jnp.bfloat16)
    halo = tap_count - 1
    rims = passed_along(
        jnp.concatenate(
            [
                late_product[-halo:],
                gate_medium[-2:],
                key_medium[-2:],
                value_medium[-2:],
                gate_long[-2:],
                key_long[-2:],
            ],
            0,
        ),
        "ctx",
        1,
    )
    rim_product = rims[:halo]
    rim_gate, rim_key, rim_value, rim_gate_long, rim_key_long = (
        rims[halo + 2 * i : halo + 2 * i + 2] for i in range(5)
    )
    head_key = short_filter(jnp.concatenate([rim_key, key_medium[:2]], 0), short_medium[1])
    head_value = short_filter(jnp.concatenate([rim_value, value_medium[:2]], 0), short_medium[2])
    head_product = (head_key * head_value).astype(jnp.bfloat16)
    product = jnp.concatenate([rim_product, head_product, late_product], 0)
    gate_feat = short_filter(jnp.concatenate([rim_gate, gate_medium], 0), short_medium[0])
    extended = jnp.concatenate([jnp.zeros((1, width_local), jnp.bfloat16), product], 0)
    mixed_medium, partial_squares = medium_call(
        extended, filter_medium, skip_medium[None, :], gate_feat
    )
    squares = jnp.sum(partial_squares, axis=1)
    ring = lax.axis_size("ch")
    total_squares = squares
    for shift in range(1, ring):
        total_squares = total_squares + lax.ppermute(
            squares, "ch", [(source, (source + shift) % ring) for source in range(ring)]
        )
    inverse = lax.rsqrt(total_squares / D + 1e-06)
    normed = (mixed_medium * norm_gain * inverse[:, None]).astype(jnp.bfloat16)
    rim_normed = passed_along(normed[-2:], "ctx", 1)
    gate_feat_long = short_filter(jnp.concatenate([rim_gate_long, gate_long], 0), short_long[0])
    key_feat_long = short_filter(jnp.concatenate([rim_key_long, key_long], 0), short_long[1])
    value_feat_long = short_filter(jnp.concatenate([rim_normed, normed], 0), short_long[2])
    product_long = (key_feat_long * value_feat_long).astype(jnp.bfloat16)
    mode_weight = residues * jnp.sqrt(-jnp.expm1(-2.0 * decay_rates))
    step_decay = jnp.exp(-decay_rates)
    final_state = modal_end_call(product_long, step_decay)
    incoming = scan_call(final_state, decay_rates, lax.axis_size("ctx"), row_count)
    mixed_long = modal_out_call(
        product_long, step_decay, mode_weight, incoming, skip_long[None, :], gate_feat_long
    )
    return (mixed_medium, mixed_long)


def solution(mesh):
    placed = (
        P("ctx", "ch"),
        P("ctx", "ch"),
        P("ctx", "ch"),
        P(None, None, "ch"),
        P(None, "ch"),
        P("ch"),
        P("ch"),
        P("ctx", "ch"),
        P("ctx", "ch"),
        P(None, None, "ch"),
        P(None, "ch"),
        P(None, "ch"),
        P("ch"),
    )
    return jax.shard_map(
        body,
        mesh=mesh,
        in_specs=placed,
        out_specs=(P("ctx", "ch"), P("ctx", "ch")),
        check_vma=False,
    )
```

```python
import functools
import jax
import jax.numpy as jnp
from jax import lax
from jax.sharding import PartitionSpec as P
from jax.experimental import pallas as pl
from jax.experimental.pallas import tpu as pltpu

TAPS = 128
SUB = 128
RB = 8


def medium_kernel(ext_ref, f_ref, skip_ref, gate_ref, out_ref, ss_ref, q_ref):
    rows = out_ref.shape[0]
    width = out_ref.shape[1]
    span = ext_ref.shape[0]

    @pl.when(pl.program_id(0) == 0)
    def _():
        ss_ref[...] = jnp.zeros_like(ss_ref)

    for h in range(width // SUB):
        lanes = pl.ds(h * SUB, SUB)
        ext = ext_ref[:, lanes].astype(jnp.float32)
        for b in range(8):
            q_ref[b, 8:, :] = ext[8 - b : span - b]

        def block(kb, carry):
            acc = [jnp.zeros((8, SUB), jnp.float32) for _ in range(RB)]
            start = pl.multiple_of(kb * (8 * RB) + 8, 8)
            for b in range(8):
                qv = q_ref[b, pl.ds(start, 8 * (RB + 15)), :]
                for a in range(16):
                    w = jnp.broadcast_to(f_ref[pl.ds(8 * a + b, 1), lanes], (8, SUB))
                    for kk in range(RB):
                        v = kk + 15 - a
                        acc[kk] = acc[kk] + w * qv[8 * v : 8 * v + 8]
            skip = jnp.broadcast_to(skip_ref[:, lanes], (8, SUB))
            for kk in range(RB):
                row = pl.multiple_of(kb * (8 * RB) + 8 * kk, 8)
                own = q_ref[0, pl.ds(row + TAPS, 8), :]
                conv = acc[kk] + skip * own
                mixed = (gate_ref[pl.ds(row, 8), lanes] * conv).astype(jnp.bfloat16)
                out_ref[pl.ds(row, 8), lanes] = mixed
                m = mixed.astype(jnp.float32)
                ss_ref[pl.ds(row, 8), :] += m * m
            return carry

        lax.fori_loop(0, rows // (8 * RB), block, 0)


def medium_call(ext, taps, skip, gate_feat, block=512, interpret=False):
    span, width = ext.shape
    rows = gate_feat.shape[0]
    grid = (width // block,)
    return pl.pallas_call(
        medium_kernel,
        grid=grid,
        in_specs=[
            pl.BlockSpec((span, block), lambda i: (0, i)),
            pl.BlockSpec((TAPS, block), lambda i: (0, i)),
            pl.BlockSpec((1, block), lambda i: (0, i)),
            pl.BlockSpec((rows, block), lambda i: (0, i)),
        ],
        out_specs=[
            pl.BlockSpec((rows, block), lambda i: (0, i)),
            pl.BlockSpec((rows, SUB), lambda i: (0, 0)),
        ],
        out_shape=[
            jax.ShapeDtypeStruct((rows, width), jnp.bfloat16),
            jax.ShapeDtypeStruct((rows, SUB), jnp.float32),
        ],
        scratch_shapes=[pltpu.VMEM((8, span, SUB), jnp.float32)],
        compiler_params=pltpu.CompilerParams(dimension_semantics=("arbitrary",)),
        interpret=interpret,
    )(ext, taps, skip, gate_feat)

D = 8192


LANE = 128
GROUP = 4
MODES_HALF = 8


def _rows_to_f32(p_ref, pf_ref):
    pf_ref[...] = p_ref[...].astype(jnp.float32)


def modal_end_kernel(p_ref, e_ref, out_ref, pf_ref):
    rows = p_ref.shape[0]
    _rows_to_f32(p_ref, pf_ref)
    lanes = [pl.ds(g * LANE, LANE) for g in range(GROUP)]
    e_lo = [e_ref[0:8, ln] for ln in lanes]
    e_hi = [e_ref[8:16, ln] for ln in lanes]

    def step(i, carry):
        lo, hi = carry
        row = pl.multiple_of(i * 8, 8)
        blocks = [pf_ref[pl.ds(row, 8), ln] for ln in lanes]
        for j in range(8):
            new_lo, new_hi = [], []
            for g in range(GROUP):
                pb = jnp.broadcast_to(blocks[g][j : j + 1], (8, LANE))
                new_lo.append(e_lo[g] * lo[g] + pb)
                new_hi.append(e_hi[g] * hi[g] + pb)
            lo, hi = new_lo, new_hi
        return lo, hi

    zero = [jnp.zeros((8, LANE), jnp.float32) for _ in range(GROUP)]
    lo, hi = lax.fori_loop(0, rows // 8, step, (zero, list(zero)))
    for g, ln in enumerate(lanes):
        out_ref[0:8, ln] = lo[g]
        out_ref[8:16, ln] = hi[g]


def modal_end_call(product, decay):
    rows, width = product.shape
    block = LANE * GROUP
    return pl.pallas_call(
        modal_end_kernel,
        grid=(width // block,),
        in_specs=[
            pl.BlockSpec((rows, block), lambda i: (0, i)),
            pl.BlockSpec((16, block), lambda i: (0, i)),
        ],
        out_specs=pl.BlockSpec((16, block), lambda i: (0, i)),
        out_shape=jax.ShapeDtypeStruct((16, width), jnp.float32),
        scratch_shapes=[pltpu.VMEM((rows, block), jnp.float32)],
    )(product, decay)


def modal_out_kernel(p_ref, e_ref, w_ref, s_ref, skip_ref, gate_ref, out_ref, pf_ref, z_ref):
    rows = p_ref.shape[0]
    _rows_to_f32(p_ref, pf_ref)
    lanes = [pl.ds(g * LANE, LANE) for g in range(GROUP)]
    e_lo = [e_ref[0:8, ln] for ln in lanes]
    e_hi = [e_ref[8:16, ln] for ln in lanes]
    w_lo = [w_ref[0:8, ln] for ln in lanes]
    w_hi = [w_ref[8:16, ln] for ln in lanes]

    def step(i, carry):
        lo, hi = carry
        row = pl.multiple_of(i * 8, 8)
        blocks = [pf_ref[pl.ds(row, 8), ln] for ln in lanes]
        for j in range(8):
            new_lo, new_hi = [], []
            for g in range(GROUP):
                pb = jnp.broadcast_to(blocks[g][j : j + 1], (8, LANE))
                a = e_lo[g] * lo[g] + pb
                b = e_hi[g] * hi[g] + pb
                z_ref[g, pl.ds(pl.multiple_of(i * 64 + 8 * j, 8), 8), :] = w_lo[g] * a + w_hi[g] * b
                new_lo.append(a)
                new_hi.append(b)
            lo, hi = new_lo, new_hi
        return lo, hi

    init_lo = [s_ref[0:8, ln] for ln in lanes]
    init_hi = [s_ref[8:16, ln] for ln in lanes]
    lax.fori_loop(0, rows // 8, step, (init_lo, init_hi))

    def reduce(i, carry):
        row = pl.multiple_of(i * 8, 8)
        for g, ln in enumerate(lanes):
            total = z_ref[g, pl.ds(i * 64, 8, stride=8), :]
            for j in range(1, 8):
                total = total + z_ref[g, pl.ds(i * 64 + j, 8, stride=8), :]
            own = pf_ref[pl.ds(row, 8), ln]
            skip = jnp.broadcast_to(skip_ref[:, ln], (8, LANE))
            conv = total + skip * own
            out_ref[pl.ds(row, 8), ln] = (gate_ref[pl.ds(row, 8), ln] * conv).astype(out_ref.dtype)
        return carry

    lax.fori_loop(0, rows // 8, reduce, 0)


def modal_out_call(product, decay, weight, start, skip, gate_feat):
    rows, width = product.shape
    block = LANE * GROUP
    return pl.pallas_call(
        modal_out_kernel,
        grid=(width // block,),
        in_specs=[
            pl.BlockSpec((rows, block), lambda i: (0, i)),
            pl.BlockSpec((16, block), lambda i: (0, i)),
            pl.BlockSpec((16, block), lambda i: (0, i)),
            pl.BlockSpec((16, block), lambda i: (0, i)),
            pl.BlockSpec((1, block), lambda i: (0, i)),
            pl.BlockSpec((rows, block), lambda i: (0, i)),
        ],
        out_specs=pl.BlockSpec((rows, block), lambda i: (0, i)),
        out_shape=jax.ShapeDtypeStruct((rows, width), jnp.bfloat16),
        scratch_shapes=[
            pltpu.VMEM((rows, block), jnp.float32),
            pltpu.VMEM((GROUP, rows * 8, LANE), jnp.float32),
        ],
    )(product, decay, weight, start, skip, gate_feat)


def scan_kernel(count, rows, f_ref, r_ref, out_ref, send_ref, recv_ref, send_sem, recv_sem):
    me = lax.axis_index("ctx")
    plan = []
    span = 1
    while span * 4 < count:
        plan.append([(span * i, span * i) for i in range(1, 4)])
        span *= 4
    plan.append([(1 + span * i, span * i) for i in range(count // span)])
    barrier = pltpu.get_barrier_semaphore()
    partners = sorted({shift for sends in plan for shift, _ in sends})
    for shift in partners:
        for other in (me + shift, me - shift):

            @pl.when(jnp.logical_and(other >= 0, other < count))
            def _():
                pl.semaphore_signal(
                    barrier, 1, device_id={"ctx": other}, device_id_type=pl.DeviceIdType.MESH
                )

    peers = 0
    for shift in partners:
        peers = peers + (1 - (me + shift) // count) + (me - shift + count) // count
    pl.semaphore_wait(barrier, peers)

    out_ref[...] = f_ref[...]
    for k, sends in enumerate(plan):
        send_ref[k] = out_ref[...].astype(send_ref.dtype)
        last = k == len(plan) - 1
        if last:
            out_ref[...] = jnp.zeros_like(out_ref)
        copies = []
        for i, (shift, power) in enumerate(sends):
            copy = pltpu.make_async_remote_copy(
                src_ref=send_ref.at[k],
                dst_ref=recv_ref.at[k, i],
                send_sem=send_sem.at[k, i],
                recv_sem=recv_sem.at[k, i],
                device_id={"ctx": me + shift},
                device_id_type=pl.DeviceIdType.MESH,
            )
            copies.append((shift, power, copy))

            @pl.when(me + shift < count)
            def _():
                copy.start()

        for i, (shift, power, copy) in enumerate(copies):

            @pl.when(me >= shift)
            def _():
                copy.wait_recv()
                if power == 0:
                    out_ref[...] = out_ref[...] + recv_ref[k, i].astype(jnp.float32)
                else:
                    factor = jnp.exp(r_ref[...] * (-1.0 * rows * power))
                    out_ref[...] = out_ref[...] + factor * recv_ref[k, i].astype(jnp.float32)

        for shift, power, copy in copies:

            @pl.when(me + shift < count)
            def _():
                copy.wait_send()


def scan_call(final_state, decay_rates, count, rows):
    shape = final_state.shape
    return pl.pallas_call(
        functools.partial(scan_kernel, count, rows),
        in_specs=[pl.BlockSpec(memory_space=pltpu.VMEM)] * 2,
        out_specs=pl.BlockSpec(memory_space=pltpu.VMEM),
        out_shape=jax.ShapeDtypeStruct(shape, jnp.float32),
        scratch_shapes=[
            pltpu.VMEM((3,) + shape, jnp.bfloat16),
            pltpu.VMEM((3, 4) + shape, jnp.bfloat16),
            pltpu.SemaphoreType.DMA((3, 4)),
            pltpu.SemaphoreType.DMA((3, 4)),
        ],
        compiler_params=pltpu.CompilerParams(collective_id=0, has_side_effects=True),
    )(final_state, decay_rates)


def passed_along(value, axis, steps):
    count = lax.axis_size(axis)
    first, last = (max(0, -steps), min(count, count - steps))
    return lax.ppermute(value, axis, [(source, source + steps) for source in range(first, last)])


def short_filter(extended, weights):
    return weights[0] * extended[2:] + weights[1] * extended[1:-1] + weights[2] * extended[:-2]


def medium_conv(extended, taps, row_count):
    tap_count = taps.shape[0]
    total = jnp.zeros((row_count, taps.shape[1]), jnp.float32)
    for offset in range(tap_count):
        start = tap_count - 1 - offset
        total = total + taps[offset] * extended[start : start + row_count]
    return total


def body(
    gate_medium,
    key_medium,
    value_medium,
    short_medium,
    filter_medium,
    skip_medium,
    norm_gain,
    gate_long,
    key_long,
    short_long,
    decay_rates,
    residues,
    skip_long,
):
    row_count = gate_medium.shape[0]
    tap_count = filter_medium.shape[0]
    width_local = gate_medium.shape[1]
    late_product = (
        short_filter(key_medium, short_medium[1]) * short_filter(value_medium, short_medium[2])
    ).astype(jnp.bfloat16)
    rim_gate, rim_key, rim_value, rim_product = passed_along(
        (gate_medium[-2:], key_medium[-2:], value_medium[-2:], late_product[-(tap_count - 1) :]),
        "ctx",
        1,
    )
    head_key = short_filter(jnp.concatenate([rim_key, key_medium[:2]], 0), short_medium[1])
    head_value = short_filter(jnp.concatenate([rim_value, value_medium[:2]], 0), short_medium[2])
    head_product = (head_key * head_value).astype(jnp.bfloat16)
    product = jnp.concatenate([rim_product, head_product, late_product], 0)
    gate_feat = short_filter(jnp.concatenate([rim_gate, gate_medium], 0), short_medium[0])
    extended = jnp.concatenate([jnp.zeros((1, width_local), jnp.bfloat16), product], 0)
    mixed_medium, partial_squares = medium_call(
        extended, filter_medium, skip_medium[None, :], gate_feat
    )
    squares = jnp.sum(partial_squares, axis=1)
    ring = lax.axis_size("ch")
    total_squares = squares
    for shift in range(1, ring):
        total_squares = total_squares + lax.ppermute(
            squares, "ch", [(source, (source + shift) % ring) for source in range(ring)]
        )
    inverse = lax.rsqrt(total_squares / D + 1e-06)
    normed = (mixed_medium * norm_gain * inverse[:, None]).astype(jnp.bfloat16)
    rim_gate_long, rim_key_long, rim_normed = passed_along(
        (gate_long[-2:], key_long[-2:], normed[-2:]), "ctx", 1
    )
    gate_feat_long = short_filter(jnp.concatenate([rim_gate_long, gate_long], 0), short_long[0])
    key_feat_long = short_filter(jnp.concatenate([rim_key_long, key_long], 0), short_long[1])
    value_feat_long = short_filter(jnp.concatenate([rim_normed, normed], 0), short_long[2])
    product_long = (key_feat_long * value_feat_long).astype(jnp.bfloat16)
    mode_weight = residues * jnp.sqrt(-jnp.expm1(-2.0 * decay_rates))
    step_decay = jnp.exp(-decay_rates)
    final_state = modal_end_call(product_long, step_decay)
    incoming = scan_call(final_state, decay_rates, lax.axis_size("ctx"), row_count)
    mixed_long = modal_out_call(
        product_long, step_decay, mode_weight, incoming, skip_long[None, :], gate_feat_long
    )
    return (mixed_medium, mixed_long)


def solution(mesh):
    placed = (
        P("ctx", "ch"),
        P("ctx", "ch"),
        P("ctx", "ch"),
        P(None, None, "ch"),
        P(None, "ch"),
        P("ch"),
        P("ch"),
        P("ctx", "ch"),
        P("ctx", "ch"),
        P(None, None, "ch"),
        P(None, "ch"),
        P(None, "ch"),
        P("ch"),
    )
    return jax.shard_map(
        body,
        mesh=mesh,
        in_specs=placed,
        out_specs=(P("ctx", "ch"), P("ctx", "ch")),
        check_vma=False,
    )
```

```python
import functools
import jax
import jax.numpy as jnp
from jax import lax
from jax.sharding import PartitionSpec as P
from jax.experimental import pallas as pl
from jax.experimental.pallas import tpu as pltpu

TAPS = 128
SUB = 128
RB = 8


def medium_kernel(ext_ref, f_ref, skip_ref, gate_ref, out_ref, ss_ref, q_ref):
    rows = out_ref.shape[0]
    width = out_ref.shape[1]
    span = ext_ref.shape[0]

    @pl.when(pl.program_id(0) == 0)
    def _():
        ss_ref[...] = jnp.zeros_like(ss_ref)

    for h in range(width // SUB):
        lanes = pl.ds(h * SUB, SUB)
        ext = ext_ref[:, lanes].astype(jnp.float32)
        for b in range(8):
            q_ref[b, 8:, :] = ext[8 - b : span - b]

        def block(kb, carry):
            acc = [jnp.zeros((8, SUB), jnp.float32) for _ in range(RB)]
            start = pl.multiple_of(kb * (8 * RB) + 8, 8)
            for b in range(8):
                qv = q_ref[b, pl.ds(start, 8 * (RB + 15)), :]
                for a in range(16):
                    w = jnp.broadcast_to(f_ref[pl.ds(8 * a + b, 1), lanes], (8, SUB))
                    for kk in range(RB):
                        v = kk + 15 - a
                        acc[kk] = acc[kk] + w * qv[8 * v : 8 * v + 8]
            skip = jnp.broadcast_to(skip_ref[:, lanes], (8, SUB))
            for kk in range(RB):
                row = pl.multiple_of(kb * (8 * RB) + 8 * kk, 8)
                own = q_ref[0, pl.ds(row + TAPS, 8), :]
                conv = acc[kk] + skip * own
                mixed = (gate_ref[pl.ds(row, 8), lanes] * conv).astype(jnp.bfloat16)
                out_ref[pl.ds(row, 8), lanes] = mixed
                m = mixed.astype(jnp.float32)
                ss_ref[pl.ds(row, 8), :] += m * m
            return carry

        lax.fori_loop(0, rows // (8 * RB), block, 0)


def medium_call(ext, taps, skip, gate_feat, block=512, interpret=False):
    span, width = ext.shape
    rows = gate_feat.shape[0]
    grid = (width // block,)
    return pl.pallas_call(
        medium_kernel,
        grid=grid,
        in_specs=[
            pl.BlockSpec((span, block), lambda i: (0, i)),
            pl.BlockSpec((TAPS, block), lambda i: (0, i)),
            pl.BlockSpec((1, block), lambda i: (0, i)),
            pl.BlockSpec((rows, block), lambda i: (0, i)),
        ],
        out_specs=[
            pl.BlockSpec((rows, block), lambda i: (0, i)),
            pl.BlockSpec((rows, SUB), lambda i: (0, 0)),
        ],
        out_shape=[
            jax.ShapeDtypeStruct((rows, width), jnp.bfloat16),
            jax.ShapeDtypeStruct((rows, SUB), jnp.float32),
        ],
        scratch_shapes=[pltpu.VMEM((8, span, SUB), jnp.float32)],
        compiler_params=pltpu.CompilerParams(dimension_semantics=("arbitrary",)),
        interpret=interpret,
    )(ext, taps, skip, gate_feat)

D = 8192


LANE = 128
GROUP = 4
MODES_HALF = 8


def _rows_to_f32(p_ref, pf_ref):
    pf_ref[...] = p_ref[...].astype(jnp.float32)


def modal_end_kernel(p_ref, e_ref, out_ref, pf_ref):
    rows = p_ref.shape[0]
    _rows_to_f32(p_ref, pf_ref)
    lanes = [pl.ds(g * LANE, LANE) for g in range(GROUP)]
    e_lo = [e_ref[0:8, ln] for ln in lanes]
    e_hi = [e_ref[8:16, ln] for ln in lanes]

    def step(i, carry):
        lo, hi = carry
        row = pl.multiple_of(i * 8, 8)
        blocks = [pf_ref[pl.ds(row, 8), ln] for ln in lanes]
        for j in range(8):
            new_lo, new_hi = [], []
            for g in range(GROUP):
                pb = jnp.broadcast_to(blocks[g][j : j + 1], (8, LANE))
                new_lo.append(e_lo[g] * lo[g] + pb)
                new_hi.append(e_hi[g] * hi[g] + pb)
            lo, hi = new_lo, new_hi
        return lo, hi

    zero = [jnp.zeros((8, LANE), jnp.float32) for _ in range(GROUP)]
    lo, hi = lax.fori_loop(0, rows // 8, step, (zero, list(zero)))
    for g, ln in enumerate(lanes):
        out_ref[0:8, ln] = lo[g]
        out_ref[8:16, ln] = hi[g]


def modal_end_call(product, decay):
    rows, width = product.shape
    block = LANE * GROUP
    return pl.pallas_call(
        modal_end_kernel,
        grid=(width // block,),
        in_specs=[
            pl.BlockSpec((rows, block), lambda i: (0, i)),
            pl.BlockSpec((16, block), lambda i: (0, i)),
        ],
        out_specs=pl.BlockSpec((16, block), lambda i: (0, i)),
        out_shape=jax.ShapeDtypeStruct((16, width), jnp.float32),
        scratch_shapes=[pltpu.VMEM((rows, block), jnp.float32)],
    )(product, decay)


def modal_out_kernel(p_ref, e_ref, w_ref, s_ref, skip_ref, gate_ref, out_ref, pf_ref, z_ref):
    rows = p_ref.shape[0]
    _rows_to_f32(p_ref, pf_ref)
    lanes = [pl.ds(g * LANE, LANE) for g in range(GROUP)]
    e_lo = [e_ref[0:8, ln] for ln in lanes]
    e_hi = [e_ref[8:16, ln] for ln in lanes]
    w_lo = [w_ref[0:8, ln] for ln in lanes]
    w_hi = [w_ref[8:16, ln] for ln in lanes]

    def step(i, carry):
        lo, hi = carry
        row = pl.multiple_of(i * 8, 8)
        blocks = [pf_ref[pl.ds(row, 8), ln] for ln in lanes]
        for j in range(8):
            new_lo, new_hi = [], []
            for g in range(GROUP):
                pb = jnp.broadcast_to(blocks[g][j : j + 1], (8, LANE))
                a = e_lo[g] * lo[g] + pb
                b = e_hi[g] * hi[g] + pb
                z_ref[g, pl.ds(pl.multiple_of(i * 64 + 8 * j, 8), 8), :] = w_lo[g] * a + w_hi[g] * b
                new_lo.append(a)
                new_hi.append(b)
            lo, hi = new_lo, new_hi
        return lo, hi

    init_lo = [s_ref[0:8, ln] for ln in lanes]
    init_hi = [s_ref[8:16, ln] for ln in lanes]
    lax.fori_loop(0, rows // 8, step, (init_lo, init_hi))

    def reduce(i, carry):
        row = pl.multiple_of(i * 8, 8)
        for g, ln in enumerate(lanes):
            total = z_ref[g, pl.ds(i * 64, 8, stride=8), :]
            for j in range(1, 8):
                total = total + z_ref[g, pl.ds(i * 64 + j, 8, stride=8), :]
            own = pf_ref[pl.ds(row, 8), ln]
            skip = jnp.broadcast_to(skip_ref[:, ln], (8, LANE))
            conv = total + skip * own
            out_ref[pl.ds(row, 8), ln] = (gate_ref[pl.ds(row, 8), ln] * conv).astype(out_ref.dtype)
        return carry

    lax.fori_loop(0, rows // 8, reduce, 0)


def modal_out_call(product, decay, weight, start, skip, gate_feat):
    rows, width = product.shape
    block = LANE * GROUP
    return pl.pallas_call(
        modal_out_kernel,
        grid=(width // block,),
        in_specs=[
            pl.BlockSpec((rows, block), lambda i: (0, i)),
            pl.BlockSpec((16, block), lambda i: (0, i)),
            pl.BlockSpec((16, block), lambda i: (0, i)),
            pl.BlockSpec((16, block), lambda i: (0, i)),
            pl.BlockSpec((1, block), lambda i: (0, i)),
            pl.BlockSpec((rows, block), lambda i: (0, i)),
        ],
        out_specs=pl.BlockSpec((rows, block), lambda i: (0, i)),
        out_shape=jax.ShapeDtypeStruct((rows, width), jnp.bfloat16),
        scratch_shapes=[
            pltpu.VMEM((rows, block), jnp.float32),
            pltpu.VMEM((GROUP, rows * 8, LANE), jnp.float32),
        ],
    )(product, decay, weight, start, skip, gate_feat)


def scan_kernel(count, rows, f_ref, r_ref, out_ref, send_ref, recv_ref, send_sem, recv_sem):
    me = lax.axis_index("ctx")
    plan = []
    span = 1
    while span * 4 < count:
        plan.append([(span * i, span * i) for i in range(1, 4)])
        span *= 4
    plan.append([(1 + span * i, span * i) for i in range(count // span)])
    barrier = pltpu.get_barrier_semaphore()
    partners = sorted({shift for sends in plan for shift, _ in sends})
    for shift in partners:
        for other in (me + shift, me - shift):

            @pl.when(jnp.logical_and(other >= 0, other < count))
            def _():
                pl.semaphore_signal(
                    barrier, 1, device_id={"ctx": other}, device_id_type=pl.DeviceIdType.MESH
                )

    peers = 0
    for shift in partners:
        peers = peers + (1 - (me + shift) // count) + (me - shift + count) // count
    pl.semaphore_wait(barrier, peers)

    out_ref[...] = f_ref[...]
    for k, sends in enumerate(plan):
        send_ref[k] = out_ref[...].astype(send_ref.dtype)
        last = k == len(plan) - 1
        if last:
            out_ref[...] = jnp.zeros_like(out_ref)
        copies = []
        for i, (shift, power) in enumerate(sends):
            copy = pltpu.make_async_remote_copy(
                src_ref=send_ref.at[k],
                dst_ref=recv_ref.at[k, i],
                send_sem=send_sem.at[k, i],
                recv_sem=recv_sem.at[k, i],
                device_id={"ctx": me + shift},
                device_id_type=pl.DeviceIdType.MESH,
            )
            copies.append((shift, power, copy))

            @pl.when(me + shift < count)
            def _():
                copy.start()

        for i, (shift, power, copy) in enumerate(copies):

            @pl.when(me >= shift)
            def _():
                copy.wait_recv()
                if power == 0:
                    out_ref[...] = out_ref[...] + recv_ref[k, i].astype(jnp.float32)
                else:
                    factor = jnp.exp(r_ref[...] * (-1.0 * rows * power))
                    out_ref[...] = out_ref[...] + factor * recv_ref[k, i].astype(jnp.float32)

        for shift, power, copy in copies:

            @pl.when(me + shift < count)
            def _():
                copy.wait_send()


def scan_call(final_state, decay_rates, count, rows):
    shape = final_state.shape
    return pl.pallas_call(
        functools.partial(scan_kernel, count, rows),
        in_specs=[pl.BlockSpec(memory_space=pltpu.VMEM)] * 2,
        out_specs=pl.BlockSpec(memory_space=pltpu.VMEM),
        out_shape=jax.ShapeDtypeStruct(shape, jnp.float32),
        scratch_shapes=[
            pltpu.VMEM((3,) + shape, jnp.bfloat16),
            pltpu.VMEM((3, 4) + shape, jnp.bfloat16),
            pltpu.SemaphoreType.DMA((3, 4)),
            pltpu.SemaphoreType.DMA((3, 4)),
        ],
        compiler_params=pltpu.CompilerParams(collective_id=0, has_side_effects=True),
    )(final_state, decay_rates)


def channel_sum_kernel(count, x_ref, out_ref, recv_ref, send_sem, recv_sem):
    me = lax.axis_index("ch")
    barrier = pltpu.get_barrier_semaphore()
    for shift in range(1, count):
        pl.semaphore_signal(
            barrier,
            1,
            device_id={"ch": (me + shift) % count},
            device_id_type=pl.DeviceIdType.MESH,
        )
    pl.semaphore_wait(barrier, count - 1)
    copies = []
    for shift in range(1, count):
        copy = pltpu.make_async_remote_copy(
            src_ref=x_ref,
            dst_ref=recv_ref.at[shift],
            send_sem=send_sem.at[shift],
            recv_sem=recv_sem.at[shift],
            device_id={"ch": (me + shift) % count},
            device_id_type=pl.DeviceIdType.MESH,
        )
        copy.start()
        copies.append(copy)
    total = x_ref[...]
    for shift, copy in zip(range(1, count), copies):
        copy.wait_recv()
        total = total + recv_ref[shift]
    out_ref[...] = total
    for copy in copies:
        copy.wait_send()


def channel_sum_call(values, count):
    return pl.pallas_call(
        functools.partial(channel_sum_kernel, count),
        in_specs=[pl.BlockSpec(memory_space=pltpu.VMEM)],
        out_specs=pl.BlockSpec(memory_space=pltpu.VMEM),
        out_shape=jax.ShapeDtypeStruct(values.shape, jnp.float32),
        scratch_shapes=[
            pltpu.VMEM((count,) + values.shape, jnp.float32),
            pltpu.SemaphoreType.DMA((count,)),
            pltpu.SemaphoreType.DMA((count,)),
        ],
        compiler_params=pltpu.CompilerParams(collective_id=1, has_side_effects=True),
    )(values)


def passed_along(value, axis, steps):
    count = lax.axis_size(axis)
    first, last = (max(0, -steps), min(count, count - steps))
    return lax.ppermute(value, axis, [(source, source + steps) for source in range(first, last)])


def short_filter(extended, weights):
    return weights[0] * extended[2:] + weights[1] * extended[1:-1] + weights[2] * extended[:-2]


def medium_conv(extended, taps, row_count):
    tap_count = taps.shape[0]
    total = jnp.zeros((row_count, taps.shape[1]), jnp.float32)
    for offset in range(tap_count):
        start = tap_count - 1 - offset
        total = total + taps[offset] * extended[start : start + row_count]
    return total


def body(
    gate_medium,
    key_medium,
    value_medium,
    short_medium,
    filter_medium,
    skip_medium,
    norm_gain,
    gate_long,
    key_long,
    short_long,
    decay_rates,
    residues,
    skip_long,
):
    row_count = gate_medium.shape[0]
    tap_count = filter_medium.shape[0]
    width_local = gate_medium.shape[1]
    late_product = (
        short_filter(key_medium, short_medium[1]) * short_filter(value_medium, short_medium[2])
    ).astype(jnp.bfloat16)
    rim_gate, rim_key, rim_value, rim_product = passed_along(
        (gate_medium[-2:], key_medium[-2:], value_medium[-2:], late_product[-(tap_count - 1) :]),
        "ctx",
        1,
    )
    head_key = short_filter(jnp.concatenate([rim_key, key_medium[:2]], 0), short_medium[1])
    head_value = short_filter(jnp.concatenate([rim_value, value_medium[:2]], 0), short_medium[2])
    head_product = (head_key * head_value).astype(jnp.bfloat16)
    product = jnp.concatenate([rim_product, head_product, late_product], 0)
    gate_feat = short_filter(jnp.concatenate([rim_gate, gate_medium], 0), short_medium[0])
    extended = jnp.concatenate([jnp.zeros((1, width_local), jnp.bfloat16), product], 0)
    mixed_medium, partial_squares = medium_call(
        extended, filter_medium, skip_medium[None, :], gate_feat
    )
    squares = jnp.sum(partial_squares, axis=1)
    total_squares = channel_sum_call(
        squares.reshape(-1, 128), lax.axis_size("ch")
    ).reshape(squares.shape)
    inverse = lax.rsqrt(total_squares / D + 1e-06)
    normed = (mixed_medium * norm_gain * inverse[:, None]).astype(jnp.bfloat16)
    rim_gate_long, rim_key_long, rim_normed = passed_along(
        (gate_long[-2:], key_long[-2:], normed[-2:]), "ctx", 1
    )
    gate_feat_long = short_filter(jnp.concatenate([rim_gate_long, gate_long], 0), short_long[0])
    key_feat_long = short_filter(jnp.concatenate([rim_key_long, key_long], 0), short_long[1])
    value_feat_long = short_filter(jnp.concatenate([rim_normed, normed], 0), short_long[2])
    product_long = (key_feat_long * value_feat_long).astype(jnp.bfloat16)
    mode_weight = residues * jnp.sqrt(-jnp.expm1(-2.0 * decay_rates))
    step_decay = jnp.exp(-decay_rates)
    final_state = modal_end_call(product_long, step_decay)
    incoming = scan_call(final_state, decay_rates, lax.axis_size("ctx"), row_count)
    mixed_long = modal_out_call(
        product_long, step_decay, mode_weight, incoming, skip_long[None, :], gate_feat_long
    )
    return (mixed_medium, mixed_long)


def solution(mesh):
    placed = (
        P("ctx", "ch"),
        P("ctx", "ch"),
        P("ctx", "ch"),
        P(None, None, "ch"),
        P(None, "ch"),
        P("ch"),
        P("ch"),
        P("ctx", "ch"),
        P("ctx", "ch"),
        P(None, None, "ch"),
        P(None, "ch"),
        P(None, "ch"),
        P("ch"),
    )
    return jax.shard_map(
        body,
        mesh=mesh,
        in_specs=placed,
        out_specs=(P("ctx", "ch"), P("ctx", "ch")),
        check_vma=False,
    )
```

```python
import functools
import jax
import jax.numpy as jnp
from jax import lax
from jax.sharding import PartitionSpec as P
from jax.experimental import pallas as pl
from jax.experimental.pallas import tpu as pltpu

TAPS = 128
SUB = 128
RB = 8


def medium_kernel(ext_ref, f_ref, skip_ref, gate_ref, out_ref, ss_ref, q_ref):
    rows = out_ref.shape[0]
    width = out_ref.shape[1]
    span = ext_ref.shape[0]

    @pl.when(pl.program_id(0) == 0)
    def _():
        ss_ref[...] = jnp.zeros_like(ss_ref)

    for h in range(width // SUB):
        lanes = pl.ds(h * SUB, SUB)
        ext = ext_ref[:, lanes].astype(jnp.float32)
        for b in range(8):
            q_ref[b, 8:, :] = ext[8 - b : span - b]

        def block(kb, carry):
            acc = [jnp.zeros((8, SUB), jnp.float32) for _ in range(RB)]
            start = pl.multiple_of(kb * (8 * RB) + 8, 8)
            for b in range(8):
                qv = q_ref[b, pl.ds(start, 8 * (RB + 15)), :]
                for a in range(16):
                    w = jnp.broadcast_to(f_ref[pl.ds(8 * a + b, 1), lanes], (8, SUB))
                    for kk in range(RB):
                        v = kk + 15 - a
                        acc[kk] = acc[kk] + w * qv[8 * v : 8 * v + 8]
            skip = jnp.broadcast_to(skip_ref[:, lanes], (8, SUB))
            for kk in range(RB):
                row = pl.multiple_of(kb * (8 * RB) + 8 * kk, 8)
                own = q_ref[0, pl.ds(row + TAPS, 8), :]
                conv = acc[kk] + skip * own
                mixed = (gate_ref[pl.ds(row, 8), lanes] * conv).astype(jnp.bfloat16)
                out_ref[pl.ds(row, 8), lanes] = mixed
                m = mixed.astype(jnp.float32)
                ss_ref[pl.ds(row, 8), :] += m * m
            return carry

        lax.fori_loop(0, rows // (8 * RB), block, 0)


def medium_call(ext, taps, skip, gate_feat, block=512, interpret=False):
    span, width = ext.shape
    rows = gate_feat.shape[0]
    grid = (width // block,)
    return pl.pallas_call(
        medium_kernel,
        grid=grid,
        in_specs=[
            pl.BlockSpec((span, block), lambda i: (0, i)),
            pl.BlockSpec((TAPS, block), lambda i: (0, i)),
            pl.BlockSpec((1, block), lambda i: (0, i)),
            pl.BlockSpec((rows, block), lambda i: (0, i)),
        ],
        out_specs=[
            pl.BlockSpec((rows, block), lambda i: (0, i)),
            pl.BlockSpec((rows, SUB), lambda i: (0, 0)),
        ],
        out_shape=[
            jax.ShapeDtypeStruct((rows, width), jnp.bfloat16),
            jax.ShapeDtypeStruct((rows, SUB), jnp.float32),
        ],
        scratch_shapes=[pltpu.VMEM((8, span, SUB), jnp.float32)],
        compiler_params=pltpu.CompilerParams(dimension_semantics=("arbitrary",)),
        interpret=interpret,
    )(ext, taps, skip, gate_feat)

D = 8192


LANE = 128
GROUP = 4
MODES_HALF = 8


def _rows_to_f32(p_ref, pf_ref):
    pf_ref[...] = p_ref[...].astype(jnp.float32)


def modal_end_kernel(p_ref, e_ref, out_ref, pf_ref):
    rows = p_ref.shape[0]
    _rows_to_f32(p_ref, pf_ref)
    lanes = [pl.ds(g * LANE, LANE) for g in range(GROUP)]
    e_lo = [e_ref[0:8, ln] for ln in lanes]
    e_hi = [e_ref[8:16, ln] for ln in lanes]

    def step(i, carry):
        lo, hi = carry
        row = pl.multiple_of(i * 8, 8)
        blocks = [pf_ref[pl.ds(row, 8), ln] for ln in lanes]
        for j in range(8):
            new_lo, new_hi = [], []
            for g in range(GROUP):
                pb = jnp.broadcast_to(blocks[g][j : j + 1], (8, LANE))
                new_lo.append(e_lo[g] * lo[g] + pb)
                new_hi.append(e_hi[g] * hi[g] + pb)
            lo, hi = new_lo, new_hi
        return lo, hi

    zero = [jnp.zeros((8, LANE), jnp.float32) for _ in range(GROUP)]
    lo, hi = lax.fori_loop(0, rows // 8, step, (zero, list(zero)))
    for g, ln in enumerate(lanes):
        out_ref[0:8, ln] = lo[g]
        out_ref[8:16, ln] = hi[g]


def modal_end_call(product, decay):
    rows, width = product.shape
    block = LANE * GROUP
    return pl.pallas_call(
        modal_end_kernel,
        grid=(width // block,),
        in_specs=[
            pl.BlockSpec((rows, block), lambda i: (0, i)),
            pl.BlockSpec((16, block), lambda i: (0, i)),
        ],
        out_specs=pl.BlockSpec((16, block), lambda i: (0, i)),
        out_shape=jax.ShapeDtypeStruct((16, width), jnp.float32),
        scratch_shapes=[pltpu.VMEM((rows, block), jnp.float32)],
    )(product, decay)


def modal_out_kernel(
    p_ref, e_ref, w_ref, s_ref, skip_ref, raw_ref, rim_ref, tap_ref, out_ref, pf_ref, z_ref, gate_ref
):
    rows = p_ref.shape[0]
    _rows_to_f32(p_ref, pf_ref)
    lanes = [pl.ds(g * LANE, LANE) for g in range(GROUP)]
    for ln in lanes:
        extended = jnp.concatenate(
            [rim_ref[:, ln], raw_ref[:, ln].astype(jnp.float32)], 0
        )
        taps = tap_ref[:, ln]
        gate_ref[:, ln] = (
            taps[0:1] * extended[8 : rows + 8]
            + taps[1:2] * extended[7 : rows + 7]
            + taps[2:3] * extended[6 : rows + 6]
        )
    e_lo = [e_ref[0:8, ln] for ln in lanes]
    e_hi = [e_ref[8:16, ln] for ln in lanes]
    w_lo = [w_ref[0:8, ln] for ln in lanes]
    w_hi = [w_ref[8:16, ln] for ln in lanes]

    def step(i, carry):
        lo, hi = carry
        row = pl.multiple_of(i * 8, 8)
        blocks = [pf_ref[pl.ds(row, 8), ln] for ln in lanes]
        for j in range(8):
            new_lo, new_hi = [], []
            for g in range(GROUP):
                pb = jnp.broadcast_to(blocks[g][j : j + 1], (8, LANE))
                a = e_lo[g] * lo[g] + pb
                b = e_hi[g] * hi[g] + pb
                z_ref[g, pl.ds(pl.multiple_of(i * 64 + 8 * j, 8), 8), :] = w_lo[g] * a + w_hi[g] * b
                new_lo.append(a)
                new_hi.append(b)
            lo, hi = new_lo, new_hi
        return lo, hi

    init_lo = [s_ref[0:8, ln] for ln in lanes]
    init_hi = [s_ref[8:16, ln] for ln in lanes]
    lax.fori_loop(0, rows // 8, step, (init_lo, init_hi))

    def reduce(i, carry):
        row = pl.multiple_of(i * 8, 8)
        for g, ln in enumerate(lanes):
            total = z_ref[g, pl.ds(i * 64, 8, stride=8), :]
            for j in range(1, 8):
                total = total + z_ref[g, pl.ds(i * 64 + j, 8, stride=8), :]
            own = pf_ref[pl.ds(row, 8), ln]
            skip = jnp.broadcast_to(skip_ref[:, ln], (8, LANE))
            conv = total + skip * own
            out_ref[pl.ds(row, 8), ln] = (gate_ref[pl.ds(row, 8), ln] * conv).astype(out_ref.dtype)
        return carry

    lax.fori_loop(0, rows // 8, reduce, 0)


def modal_out_call(product, decay, weight, start, skip, gate, rim, taps):
    rows, width = product.shape
    block = LANE * GROUP
    return pl.pallas_call(
        modal_out_kernel,
        grid=(width // block,),
        in_specs=[
            pl.BlockSpec((rows, block), lambda i: (0, i)),
            pl.BlockSpec((16, block), lambda i: (0, i)),
            pl.BlockSpec((16, block), lambda i: (0, i)),
            pl.BlockSpec((16, block), lambda i: (0, i)),
            pl.BlockSpec((1, block), lambda i: (0, i)),
            pl.BlockSpec((rows, block), lambda i: (0, i)),
            pl.BlockSpec((8, block), lambda i: (0, i)),
            pl.BlockSpec((3, block), lambda i: (0, i)),
        ],
        out_specs=pl.BlockSpec((rows, block), lambda i: (0, i)),
        out_shape=jax.ShapeDtypeStruct((rows, width), jnp.bfloat16),
        scratch_shapes=[
            pltpu.VMEM((rows, block), jnp.float32),
            pltpu.VMEM((GROUP, rows * 8, LANE), jnp.float32),
            pltpu.VMEM((rows, block), jnp.float32),
        ],
    )(product, decay, weight, start, skip, gate, rim, taps)


def scan_kernel(count, rows, f_ref, r_ref, out_ref, send_ref, recv_ref, send_sem, recv_sem):
    me = lax.axis_index("ctx")
    plan = []
    span = 1
    while span * 4 < count:
        plan.append([(span * i, span * i) for i in range(1, 4)])
        span *= 4
    plan.append([(1 + span * i, span * i) for i in range(count // span)])
    barrier = pltpu.get_barrier_semaphore()
    partners = sorted({shift for sends in plan for shift, _ in sends})
    for shift in partners:
        for other in (me + shift, me - shift):

            @pl.when(jnp.logical_and(other >= 0, other < count))
            def _():
                pl.semaphore_signal(
                    barrier, 1, device_id={"ctx": other}, device_id_type=pl.DeviceIdType.MESH
                )

    peers = 0
    for shift in partners:
        peers = peers + (1 - (me + shift) // count) + (me - shift + count) // count
    pl.semaphore_wait(barrier, peers)

    out_ref[...] = f_ref[...]
    for k, sends in enumerate(plan):
        send_ref[k] = out_ref[...].astype(send_ref.dtype)
        last = k == len(plan) - 1
        if last:
            out_ref[...] = jnp.zeros_like(out_ref)
        copies = []
        for i, (shift, power) in enumerate(sends):
            copy = pltpu.make_async_remote_copy(
                src_ref=send_ref.at[k],
                dst_ref=recv_ref.at[k, i],
                send_sem=send_sem.at[k, i],
                recv_sem=recv_sem.at[k, i],
                device_id={"ctx": me + shift},
                device_id_type=pl.DeviceIdType.MESH,
            )
            copies.append((shift, power, copy))

            @pl.when(me + shift < count)
            def _():
                copy.start()

        for i, (shift, power, copy) in enumerate(copies):

            @pl.when(me >= shift)
            def _():
                copy.wait_recv()
                if power == 0:
                    out_ref[...] = out_ref[...] + recv_ref[k, i].astype(jnp.float32)
                else:
                    factor = jnp.exp(r_ref[...] * (-1.0 * rows * power))
                    out_ref[...] = out_ref[...] + factor * recv_ref[k, i].astype(jnp.float32)

        for shift, power, copy in copies:

            @pl.when(me + shift < count)
            def _():
                copy.wait_send()


def scan_call(final_state, decay_rates, count, rows):
    shape = final_state.shape
    return pl.pallas_call(
        functools.partial(scan_kernel, count, rows),
        in_specs=[pl.BlockSpec(memory_space=pltpu.VMEM)] * 2,
        out_specs=pl.BlockSpec(memory_space=pltpu.VMEM),
        out_shape=jax.ShapeDtypeStruct(shape, jnp.float32),
        scratch_shapes=[
            pltpu.VMEM((3,) + shape, jnp.bfloat16),
            pltpu.VMEM((3, 4) + shape, jnp.bfloat16),
            pltpu.SemaphoreType.DMA((3, 4)),
            pltpu.SemaphoreType.DMA((3, 4)),
        ],
        compiler_params=pltpu.CompilerParams(collective_id=0, has_side_effects=True),
    )(final_state, decay_rates)


def passed_along(value, axis, steps):
    count = lax.axis_size(axis)
    first, last = (max(0, -steps), min(count, count - steps))
    return lax.ppermute(value, axis, [(source, source + steps) for source in range(first, last)])


def short_filter(extended, weights):
    return weights[0] * extended[2:] + weights[1] * extended[1:-1] + weights[2] * extended[:-2]


def medium_conv(extended, taps, row_count):
    tap_count = taps.shape[0]
    total = jnp.zeros((row_count, taps.shape[1]), jnp.float32)
    for offset in range(tap_count):
        start = tap_count - 1 - offset
        total = total + taps[offset] * extended[start : start + row_count]
    return total


def body(
    gate_medium,
    key_medium,
    value_medium,
    short_medium,
    filter_medium,
    skip_medium,
    norm_gain,
    gate_long,
    key_long,
    short_long,
    decay_rates,
    residues,
    skip_long,
):
    row_count = gate_medium.shape[0]
    tap_count = filter_medium.shape[0]
    width_local = gate_medium.shape[1]
    late_product = (
        short_filter(key_medium, short_medium[1]) * short_filter(value_medium, short_medium[2])
    ).astype(jnp.bfloat16)
    rim_gate, rim_key, rim_value, rim_product = passed_along(
        (gate_medium[-2:], key_medium[-2:], value_medium[-2:], late_product[-(tap_count - 1) :]),
        "ctx",
        1,
    )
    head_key = short_filter(jnp.concatenate([rim_key, key_medium[:2]], 0), short_medium[1])
    head_value = short_filter(jnp.concatenate([rim_value, value_medium[:2]], 0), short_medium[2])
    head_product = (head_key * head_value).astype(jnp.bfloat16)
    product = jnp.concatenate([rim_product, head_product, late_product], 0)
    gate_feat = short_filter(jnp.concatenate([rim_gate, gate_medium], 0), short_medium[0])
    extended = jnp.concatenate([jnp.zeros((1, width_local), jnp.bfloat16), product], 0)
    mixed_medium, partial_squares = medium_call(
        extended, filter_medium, skip_medium[None, :], gate_feat
    )
    squares = jnp.sum(partial_squares, axis=1)
    ring = lax.axis_size("ch")
    total_squares = squares
    for shift in range(1, ring):
        total_squares = total_squares + lax.ppermute(
            squares, "ch", [(source, (source + shift) % ring) for source in range(ring)]
        )
    inverse = lax.rsqrt(total_squares / D + 1e-06)
    normed = (mixed_medium * norm_gain * inverse[:, None]).astype(jnp.bfloat16)
    rim_gate_long, rim_key_long, rim_normed = passed_along(
        (gate_long[-2:], key_long[-2:], normed[-2:]), "ctx", 1
    )
    key_feat_long = short_filter(jnp.concatenate([rim_key_long, key_long], 0), short_long[1])
    value_feat_long = short_filter(jnp.concatenate([rim_normed, normed], 0), short_long[2])
    product_long = (key_feat_long * value_feat_long).astype(jnp.bfloat16)
    mode_weight = residues * jnp.sqrt(-jnp.expm1(-2.0 * decay_rates))
    step_decay = jnp.exp(-decay_rates)
    final_state = modal_end_call(product_long, step_decay)
    incoming = scan_call(final_state, decay_rates, lax.axis_size("ctx"), row_count)
    mixed_long = modal_out_call(
        product_long,
        step_decay,
        mode_weight,
        incoming,
        skip_long[None, :],
        gate_long,
        jnp.pad(rim_gate_long.astype(jnp.float32), ((6, 0), (0, 0))),
        short_long[0],
    )
    return (mixed_medium, mixed_long)


def solution(mesh):
    placed = (
        P("ctx", "ch"),
        P("ctx", "ch"),
        P("ctx", "ch"),
        P(None, None, "ch"),
        P(None, "ch"),
        P("ch"),
        P("ch"),
        P("ctx", "ch"),
        P("ctx", "ch"),
        P(None, None, "ch"),
        P(None, "ch"),
        P(None, "ch"),
        P("ch"),
    )
    return jax.shard_map(
        body,
        mesh=mesh,
        in_specs=placed,
        out_specs=(P("ctx", "ch"), P("ctx", "ch")),
        check_vma=False,
    )
```

```python
import functools
import jax
import jax.numpy as jnp
from jax import lax
from jax.sharding import PartitionSpec as P
from jax.experimental import pallas as pl
from jax.experimental.pallas import tpu as pltpu

TAPS = 128
SUB = 128
RB = 8


def medium_kernel(
    ext_ref, f_ref, skip_ref, raw_ref, rim_ref, tap_ref, out_ref, ss_ref, q_ref, gate_ref
):
    rows = out_ref.shape[0]
    width = out_ref.shape[1]
    span = ext_ref.shape[0]

    @pl.when(pl.program_id(0) == 0)
    def _():
        ss_ref[...] = jnp.zeros_like(ss_ref)

    for h in range(width // SUB):
        lanes = pl.ds(h * SUB, SUB)
        ext = ext_ref[:, lanes].astype(jnp.float32)
        for b in range(8):
            q_ref[b, 8:, :] = ext[8 - b : span - b]
        extended = jnp.concatenate([rim_ref[:, lanes], raw_ref[:, lanes].astype(jnp.float32)], 0)
        taps = tap_ref[:, lanes]
        gate_ref[...] = (
            taps[0:1] * extended[8 : rows + 8]
            + taps[1:2] * extended[7 : rows + 7]
            + taps[2:3] * extended[6 : rows + 6]
        )

        def block(kb, carry):
            acc = [jnp.zeros((8, SUB), jnp.float32) for _ in range(RB)]
            start = pl.multiple_of(kb * (8 * RB) + 8, 8)
            for b in range(8):
                qv = q_ref[b, pl.ds(start, 8 * (RB + 15)), :]
                for a in range(16):
                    w = jnp.broadcast_to(f_ref[pl.ds(8 * a + b, 1), lanes], (8, SUB))
                    for kk in range(RB):
                        v = kk + 15 - a
                        acc[kk] = acc[kk] + w * qv[8 * v : 8 * v + 8]
            skip = jnp.broadcast_to(skip_ref[:, lanes], (8, SUB))
            for kk in range(RB):
                row = pl.multiple_of(kb * (8 * RB) + 8 * kk, 8)
                own = q_ref[0, pl.ds(row + TAPS, 8), :]
                conv = acc[kk] + skip * own
                mixed = (gate_ref[pl.ds(row, 8), :] * conv).astype(jnp.bfloat16)
                out_ref[pl.ds(row, 8), lanes] = mixed
                m = mixed.astype(jnp.float32)
                ss_ref[pl.ds(row, 8), :] += m * m
            return carry

        lax.fori_loop(0, rows // (8 * RB), block, 0)


def medium_call(ext, taps, skip, gate, rim, gate_taps, block=512, interpret=False):
    span, width = ext.shape
    rows = gate.shape[0]
    grid = (width // block,)
    return pl.pallas_call(
        medium_kernel,
        grid=grid,
        in_specs=[
            pl.BlockSpec((span, block), lambda i: (0, i)),
            pl.BlockSpec((TAPS, block), lambda i: (0, i)),
            pl.BlockSpec((1, block), lambda i: (0, i)),
            pl.BlockSpec((rows, block), lambda i: (0, i)),
            pl.BlockSpec((8, block), lambda i: (0, i)),
            pl.BlockSpec((3, block), lambda i: (0, i)),
        ],
        out_specs=[
            pl.BlockSpec((rows, block), lambda i: (0, i)),
            pl.BlockSpec((rows, SUB), lambda i: (0, 0)),
        ],
        out_shape=[
            jax.ShapeDtypeStruct((rows, width), jnp.bfloat16),
            jax.ShapeDtypeStruct((rows, SUB), jnp.float32),
        ],
        scratch_shapes=[
            pltpu.VMEM((8, span, SUB), jnp.float32),
            pltpu.VMEM((rows, SUB), jnp.float32),
        ],
        compiler_params=pltpu.CompilerParams(dimension_semantics=("arbitrary",)),
        interpret=interpret,
    )(ext, taps, skip, gate, rim, gate_taps)

D = 8192


LANE = 128
GROUP = 4
MODES_HALF = 8


def _rows_to_f32(p_ref, pf_ref):
    pf_ref[...] = p_ref[...].astype(jnp.float32)


def modal_end_kernel(p_ref, e_ref, out_ref, pf_ref):
    rows = p_ref.shape[0]
    _rows_to_f32(p_ref, pf_ref)
    lanes = [pl.ds(g * LANE, LANE) for g in range(GROUP)]
    e_lo = [e_ref[0:8, ln] for ln in lanes]
    e_hi = [e_ref[8:16, ln] for ln in lanes]

    def step(i, carry):
        lo, hi = carry
        row = pl.multiple_of(i * 8, 8)
        blocks = [pf_ref[pl.ds(row, 8), ln] for ln in lanes]
        for j in range(8):
            new_lo, new_hi = [], []
            for g in range(GROUP):
                pb = jnp.broadcast_to(blocks[g][j : j + 1], (8, LANE))
                new_lo.append(e_lo[g] * lo[g] + pb)
                new_hi.append(e_hi[g] * hi[g] + pb)
            lo, hi = new_lo, new_hi
        return lo, hi

    zero = [jnp.zeros((8, LANE), jnp.float32) for _ in range(GROUP)]
    lo, hi = lax.fori_loop(0, rows // 8, step, (zero, list(zero)))
    for g, ln in enumerate(lanes):
        out_ref[0:8, ln] = lo[g]
        out_ref[8:16, ln] = hi[g]


def modal_end_call(product, decay):
    rows, width = product.shape
    block = LANE * GROUP
    return pl.pallas_call(
        modal_end_kernel,
        grid=(width // block,),
        in_specs=[
            pl.BlockSpec((rows, block), lambda i: (0, i)),
            pl.BlockSpec((16, block), lambda i: (0, i)),
        ],
        out_specs=pl.BlockSpec((16, block), lambda i: (0, i)),
        out_shape=jax.ShapeDtypeStruct((16, width), jnp.float32),
        scratch_shapes=[pltpu.VMEM((rows, block), jnp.float32)],
    )(product, decay)


def modal_out_kernel(
    p_ref, e_ref, w_ref, s_ref, skip_ref, raw_ref, rim_ref, tap_ref, out_ref, pf_ref, z_ref, gate_ref
):
    rows = p_ref.shape[0]
    _rows_to_f32(p_ref, pf_ref)
    lanes = [pl.ds(g * LANE, LANE) for g in range(GROUP)]
    for ln in lanes:
        extended = jnp.concatenate(
            [rim_ref[:, ln], raw_ref[:, ln].astype(jnp.float32)], 0
        )
        taps = tap_ref[:, ln]
        gate_ref[:, ln] = (
            taps[0:1] * extended[8 : rows + 8]
            + taps[1:2] * extended[7 : rows + 7]
            + taps[2:3] * extended[6 : rows + 6]
        )
    e_lo = [e_ref[0:8, ln] for ln in lanes]
    e_hi = [e_ref[8:16, ln] for ln in lanes]
    w_lo = [w_ref[0:8, ln] for ln in lanes]
    w_hi = [w_ref[8:16, ln] for ln in lanes]

    def step(i, carry):
        lo, hi = carry
        row = pl.multiple_of(i * 8, 8)
        blocks = [pf_ref[pl.ds(row, 8), ln] for ln in lanes]
        for j in range(8):
            new_lo, new_hi = [], []
            for g in range(GROUP):
                pb = jnp.broadcast_to(blocks[g][j : j + 1], (8, LANE))
                a = e_lo[g] * lo[g] + pb
                b = e_hi[g] * hi[g] + pb
                z_ref[g, pl.ds(pl.multiple_of(i * 64 + 8 * j, 8), 8), :] = w_lo[g] * a + w_hi[g] * b
                new_lo.append(a)
                new_hi.append(b)
            lo, hi = new_lo, new_hi
        return lo, hi

    init_lo = [s_ref[0:8, ln] for ln in lanes]
    init_hi = [s_ref[8:16, ln] for ln in lanes]
    lax.fori_loop(0, rows // 8, step, (init_lo, init_hi))

    def reduce(i, carry):
        row = pl.multiple_of(i * 8, 8)
        for g, ln in enumerate(lanes):
            total = z_ref[g, pl.ds(i * 64, 8, stride=8), :]
            for j in range(1, 8):
                total = total + z_ref[g, pl.ds(i * 64 + j, 8, stride=8), :]
            own = pf_ref[pl.ds(row, 8), ln]
            skip = jnp.broadcast_to(skip_ref[:, ln], (8, LANE))
            conv = total + skip * own
            out_ref[pl.ds(row, 8), ln] = (gate_ref[pl.ds(row, 8), ln] * conv).astype(out_ref.dtype)
        return carry

    lax.fori_loop(0, rows // 8, reduce, 0)


def modal_out_call(product, decay, weight, start, skip, gate, rim, taps):
    rows, width = product.shape
    block = LANE * GROUP
    return pl.pallas_call(
        modal_out_kernel,
        grid=(width // block,),
        in_specs=[
            pl.BlockSpec((rows, block), lambda i: (0, i)),
            pl.BlockSpec((16, block), lambda i: (0, i)),
            pl.BlockSpec((16, block), lambda i: (0, i)),
            pl.BlockSpec((16, block), lambda i: (0, i)),
            pl.BlockSpec((1, block), lambda i: (0, i)),
            pl.BlockSpec((rows, block), lambda i: (0, i)),
            pl.BlockSpec((8, block), lambda i: (0, i)),
            pl.BlockSpec((3, block), lambda i: (0, i)),
        ],
        out_specs=pl.BlockSpec((rows, block), lambda i: (0, i)),
        out_shape=jax.ShapeDtypeStruct((rows, width), jnp.bfloat16),
        scratch_shapes=[
            pltpu.VMEM((rows, block), jnp.float32),
            pltpu.VMEM((GROUP, rows * 8, LANE), jnp.float32),
            pltpu.VMEM((rows, block), jnp.float32),
        ],
    )(product, decay, weight, start, skip, gate, rim, taps)


def scan_kernel(count, rows, f_ref, r_ref, out_ref, send_ref, recv_ref, send_sem, recv_sem):
    me = lax.axis_index("ctx")
    plan = []
    span = 1
    while span * 4 < count:
        plan.append([(span * i, span * i) for i in range(1, 4)])
        span *= 4
    plan.append([(1 + span * i, span * i) for i in range(count // span)])
    barrier = pltpu.get_barrier_semaphore()
    partners = sorted({shift for sends in plan for shift, _ in sends})
    for shift in partners:
        for other in (me + shift, me - shift):

            @pl.when(jnp.logical_and(other >= 0, other < count))
            def _():
                pl.semaphore_signal(
                    barrier, 1, device_id={"ctx": other}, device_id_type=pl.DeviceIdType.MESH
                )

    peers = 0
    for shift in partners:
        peers = peers + (1 - (me + shift) // count) + (me - shift + count) // count
    pl.semaphore_wait(barrier, peers)

    out_ref[...] = f_ref[...]
    for k, sends in enumerate(plan):
        send_ref[k] = out_ref[...].astype(send_ref.dtype)
        last = k == len(plan) - 1
        if last:
            out_ref[...] = jnp.zeros_like(out_ref)
        copies = []
        for i, (shift, power) in enumerate(sends):
            copy = pltpu.make_async_remote_copy(
                src_ref=send_ref.at[k],
                dst_ref=recv_ref.at[k, i],
                send_sem=send_sem.at[k, i],
                recv_sem=recv_sem.at[k, i],
                device_id={"ctx": me + shift},
                device_id_type=pl.DeviceIdType.MESH,
            )
            copies.append((shift, power, copy))

            @pl.when(me + shift < count)
            def _():
                copy.start()

        for i, (shift, power, copy) in enumerate(copies):

            @pl.when(me >= shift)
            def _():
                copy.wait_recv()
                if power == 0:
                    out_ref[...] = out_ref[...] + recv_ref[k, i].astype(jnp.float32)
                else:
                    factor = jnp.exp(r_ref[...] * (-1.0 * rows * power))
                    out_ref[...] = out_ref[...] + factor * recv_ref[k, i].astype(jnp.float32)

        for shift, power, copy in copies:

            @pl.when(me + shift < count)
            def _():
                copy.wait_send()


def scan_call(final_state, decay_rates, count, rows):
    shape = final_state.shape
    return pl.pallas_call(
        functools.partial(scan_kernel, count, rows),
        in_specs=[pl.BlockSpec(memory_space=pltpu.VMEM)] * 2,
        out_specs=pl.BlockSpec(memory_space=pltpu.VMEM),
        out_shape=jax.ShapeDtypeStruct(shape, jnp.float32),
        scratch_shapes=[
            pltpu.VMEM((3,) + shape, jnp.bfloat16),
            pltpu.VMEM((3, 4) + shape, jnp.bfloat16),
            pltpu.SemaphoreType.DMA((3, 4)),
            pltpu.SemaphoreType.DMA((3, 4)),
        ],
        compiler_params=pltpu.CompilerParams(collective_id=0, has_side_effects=True),
    )(final_state, decay_rates)


def passed_along(value, axis, steps):
    count = lax.axis_size(axis)
    first, last = (max(0, -steps), min(count, count - steps))
    return lax.ppermute(value, axis, [(source, source + steps) for source in range(first, last)])


def short_filter(extended, weights):
    return weights[0] * extended[2:] + weights[1] * extended[1:-1] + weights[2] * extended[:-2]


def medium_conv(extended, taps, row_count):
    tap_count = taps.shape[0]
    total = jnp.zeros((row_count, taps.shape[1]), jnp.float32)
    for offset in range(tap_count):
        start = tap_count - 1 - offset
        total = total + taps[offset] * extended[start : start + row_count]
    return total


def body(
    gate_medium,
    key_medium,
    value_medium,
    short_medium,
    filter_medium,
    skip_medium,
    norm_gain,
    gate_long,
    key_long,
    short_long,
    decay_rates,
    residues,
    skip_long,
):
    row_count = gate_medium.shape[0]
    tap_count = filter_medium.shape[0]
    width_local = gate_medium.shape[1]
    late_product = (
        short_filter(key_medium, short_medium[1]) * short_filter(value_medium, short_medium[2])
    ).astype(jnp.bfloat16)
    rim_gate, rim_key, rim_value, rim_product = passed_along(
        (gate_medium[-2:], key_medium[-2:], value_medium[-2:], late_product[-(tap_count - 1) :]),
        "ctx",
        1,
    )
    head_key = short_filter(jnp.concatenate([rim_key, key_medium[:2]], 0), short_medium[1])
    head_value = short_filter(jnp.concatenate([rim_value, value_medium[:2]], 0), short_medium[2])
    head_product = (head_key * head_value).astype(jnp.bfloat16)
    product = jnp.concatenate([rim_product, head_product, late_product], 0)
    extended = jnp.concatenate([jnp.zeros((1, width_local), jnp.bfloat16), product], 0)
    mixed_medium, partial_squares = medium_call(
        extended,
        filter_medium,
        skip_medium[None, :],
        gate_medium,
        jnp.pad(rim_gate.astype(jnp.float32), ((6, 0), (0, 0))),
        short_medium[0],
    )
    squares = jnp.sum(partial_squares, axis=1)
    ring = lax.axis_size("ch")
    total_squares = squares
    for shift in range(1, ring):
        total_squares = total_squares + lax.ppermute(
            squares, "ch", [(source, (source + shift) % ring) for source in range(ring)]
        )
    inverse = lax.rsqrt(total_squares / D + 1e-06)
    normed = (mixed_medium * norm_gain * inverse[:, None]).astype(jnp.bfloat16)
    rim_gate_long, rim_key_long, rim_normed = passed_along(
        (gate_long[-2:], key_long[-2:], normed[-2:]), "ctx", 1
    )
    key_feat_long = short_filter(jnp.concatenate([rim_key_long, key_long], 0), short_long[1])
    value_feat_long = short_filter(jnp.concatenate([rim_normed, normed], 0), short_long[2])
    product_long = (key_feat_long * value_feat_long).astype(jnp.bfloat16)
    mode_weight = residues * jnp.sqrt(-jnp.expm1(-2.0 * decay_rates))
    step_decay = jnp.exp(-decay_rates)
    final_state = modal_end_call(product_long, step_decay)
    incoming = scan_call(final_state, decay_rates, lax.axis_size("ctx"), row_count)
    mixed_long = modal_out_call(
        product_long,
        step_decay,
        mode_weight,
        incoming,
        skip_long[None, :],
        gate_long,
        jnp.pad(rim_gate_long.astype(jnp.float32), ((6, 0), (0, 0))),
        short_long[0],
    )
    return (mixed_medium, mixed_long)


def solution(mesh):
    placed = (
        P("ctx", "ch"),
        P("ctx", "ch"),
        P("ctx", "ch"),
        P(None, None, "ch"),
        P(None, "ch"),
        P("ch"),
        P("ch"),
        P("ctx", "ch"),
        P("ctx", "ch"),
        P(None, None, "ch"),
        P(None, "ch"),
        P(None, "ch"),
        P("ch"),
    )
    return jax.shard_map(
        body,
        mesh=mesh,
        in_specs=placed,
        out_specs=(P("ctx", "ch"), P("ctx", "ch")),
        check_vma=False,
    )
```

```python
import functools
import jax
import jax.numpy as jnp
from jax import lax
from jax.sharding import PartitionSpec as P
from jax.experimental import pallas as pl
from jax.experimental.pallas import tpu as pltpu

TAPS = 128
SUB = 128
RB = 8


def medium_kernel(ext_ref, f_ref, skip_ref, gate_ref, out_ref, ss_ref, q_ref):
    rows = out_ref.shape[0]
    width = out_ref.shape[1]
    span = ext_ref.shape[0]

    @pl.when(pl.program_id(0) == 0)
    def _():
        ss_ref[...] = jnp.zeros_like(ss_ref)

    for h in range(width // SUB):
        lanes = pl.ds(h * SUB, SUB)
        ext = ext_ref[:, lanes].astype(jnp.float32)
        for b in range(8):
            q_ref[b, 8:, :] = ext[8 - b : span - b]

        def block(kb, carry):
            acc = [jnp.zeros((8, SUB), jnp.float32) for _ in range(RB)]
            start = pl.multiple_of(kb * (8 * RB) + 8, 8)
            for b in range(8):
                qv = q_ref[b, pl.ds(start, 8 * (RB + 15)), :]
                for a in range(16):
                    w = jnp.broadcast_to(f_ref[pl.ds(8 * a + b, 1), lanes], (8, SUB))
                    for kk in range(RB):
                        v = kk + 15 - a
                        acc[kk] = acc[kk] + w * qv[8 * v : 8 * v + 8]
            skip = jnp.broadcast_to(skip_ref[:, lanes], (8, SUB))
            for kk in range(RB):
                row = pl.multiple_of(kb * (8 * RB) + 8 * kk, 8)
                own = q_ref[0, pl.ds(row + TAPS, 8), :]
                conv = acc[kk] + skip * own
                mixed = (gate_ref[pl.ds(row, 8), lanes] * conv).astype(jnp.bfloat16)
                out_ref[pl.ds(row, 8), lanes] = mixed
                m = mixed.astype(jnp.float32)
                ss_ref[pl.ds(row, 8), :] += m * m
            return carry

        lax.fori_loop(0, rows // (8 * RB), block, 0)


def medium_call(ext, taps, skip, gate_feat, block=512, interpret=False):
    span, width = ext.shape
    rows = gate_feat.shape[0]
    grid = (width // block,)
    return pl.pallas_call(
        medium_kernel,
        grid=grid,
        in_specs=[
            pl.BlockSpec((span, block), lambda i: (0, i)),
            pl.BlockSpec((TAPS, block), lambda i: (0, i)),
            pl.BlockSpec((1, block), lambda i: (0, i)),
            pl.BlockSpec((rows, block), lambda i: (0, i)),
        ],
        out_specs=[
            pl.BlockSpec((rows, block), lambda i: (0, i)),
            pl.BlockSpec((rows, SUB), lambda i: (0, 0)),
        ],
        out_shape=[
            jax.ShapeDtypeStruct((rows, width), jnp.bfloat16),
            jax.ShapeDtypeStruct((rows, SUB), jnp.float32),
        ],
        scratch_shapes=[pltpu.VMEM((8, span, SUB), jnp.float32)],
        compiler_params=pltpu.CompilerParams(dimension_semantics=("arbitrary",)),
        interpret=interpret,
    )(ext, taps, skip, gate_feat)

D = 8192


LANE = 128
GROUP = 8
MODES_HALF = 8


def _rows_to_f32(p_ref, pf_ref):
    pf_ref[...] = p_ref[...].astype(jnp.float32)


def modal_end_kernel(p_ref, e_ref, out_ref, pf_ref):
    rows = p_ref.shape[0]
    _rows_to_f32(p_ref, pf_ref)
    lanes = [pl.ds(g * LANE, LANE) for g in range(GROUP)]
    e_lo = [e_ref[0:8, ln] for ln in lanes]
    e_hi = [e_ref[8:16, ln] for ln in lanes]

    def step(i, carry):
        lo, hi = carry
        row = pl.multiple_of(i * 8, 8)
        blocks = [pf_ref[pl.ds(row, 8), ln] for ln in lanes]
        for j in range(8):
            new_lo, new_hi = [], []
            for g in range(GROUP):
                pb = jnp.broadcast_to(blocks[g][j : j + 1], (8, LANE))
                new_lo.append(e_lo[g] * lo[g] + pb)
                new_hi.append(e_hi[g] * hi[g] + pb)
            lo, hi = new_lo, new_hi
        return lo, hi

    zero = [jnp.zeros((8, LANE), jnp.float32) for _ in range(GROUP)]
    lo, hi = lax.fori_loop(0, rows // 8, step, (zero, list(zero)))
    for g, ln in enumerate(lanes):
        out_ref[0:8, ln] = lo[g]
        out_ref[8:16, ln] = hi[g]


def modal_end_call(product, decay):
    rows, width = product.shape
    block = LANE * GROUP
    return pl.pallas_call(
        modal_end_kernel,
        grid=(width // block,),
        in_specs=[
            pl.BlockSpec((rows, block), lambda i: (0, i)),
            pl.BlockSpec((16, block), lambda i: (0, i)),
        ],
        out_specs=pl.BlockSpec((16, block), lambda i: (0, i)),
        out_shape=jax.ShapeDtypeStruct((16, width), jnp.float32),
        scratch_shapes=[pltpu.VMEM((rows, block), jnp.float32)],
    )(product, decay)


def modal_out_kernel(p_ref, e_ref, w_ref, s_ref, skip_ref, gate_ref, out_ref, pf_ref, z_ref):
    rows = p_ref.shape[0]
    _rows_to_f32(p_ref, pf_ref)
    lanes = [pl.ds(g * LANE, LANE) for g in range(GROUP)]
    e_lo = [e_ref[0:8, ln] for ln in lanes]
    e_hi = [e_ref[8:16, ln] for ln in lanes]
    w_lo = [w_ref[0:8, ln] for ln in lanes]
    w_hi = [w_ref[8:16, ln] for ln in lanes]

    def step(i, carry):
        lo, hi = carry
        row = pl.multiple_of(i * 8, 8)
        blocks = [pf_ref[pl.ds(row, 8), ln] for ln in lanes]
        for j in range(8):
            new_lo, new_hi = [], []
            for g in range(GROUP):
                pb = jnp.broadcast_to(blocks[g][j : j + 1], (8, LANE))
                a = e_lo[g] * lo[g] + pb
                b = e_hi[g] * hi[g] + pb
                z_ref[g, pl.ds(pl.multiple_of(i * 64 + 8 * j, 8), 8), :] = w_lo[g] * a + w_hi[g] * b
                new_lo.append(a)
                new_hi.append(b)
            lo, hi = new_lo, new_hi
        return lo, hi

    init_lo = [s_ref[0:8, ln] for ln in lanes]
    init_hi = [s_ref[8:16, ln] for ln in lanes]
    lax.fori_loop(0, rows // 8, step, (init_lo, init_hi))

    def reduce(i, carry):
        row = pl.multiple_of(i * 8, 8)
        for g, ln in enumerate(lanes):
            total = z_ref[g, pl.ds(i * 64, 8, stride=8), :]
            for j in range(1, 8):
                total = total + z_ref[g, pl.ds(i * 64 + j, 8, stride=8), :]
            own = pf_ref[pl.ds(row, 8), ln]
            skip = jnp.broadcast_to(skip_ref[:, ln], (8, LANE))
            conv = total + skip * own
            out_ref[pl.ds(row, 8), ln] = (gate_ref[pl.ds(row, 8), ln] * conv).astype(out_ref.dtype)
        return carry

    lax.fori_loop(0, rows // 8, reduce, 0)


def modal_out_call(product, decay, weight, start, skip, gate_feat):
    rows, width = product.shape
    block = LANE * GROUP
    return pl.pallas_call(
        modal_out_kernel,
        grid=(width // block,),
        in_specs=[
            pl.BlockSpec((rows, block), lambda i: (0, i)),
            pl.BlockSpec((16, block), lambda i: (0, i)),
            pl.BlockSpec((16, block), lambda i: (0, i)),
            pl.BlockSpec((16, block), lambda i: (0, i)),
            pl.BlockSpec((1, block), lambda i: (0, i)),
            pl.BlockSpec((rows, block), lambda i: (0, i)),
        ],
        out_specs=pl.BlockSpec((rows, block), lambda i: (0, i)),
        out_shape=jax.ShapeDtypeStruct((rows, width), jnp.bfloat16),
        scratch_shapes=[
            pltpu.VMEM((rows, block), jnp.float32),
            pltpu.VMEM((GROUP, rows * 8, LANE), jnp.float32),
        ],
    )(product, decay, weight, start, skip, gate_feat)


def scan_kernel(count, rows, f_ref, r_ref, out_ref, send_ref, recv_ref, send_sem, recv_sem):
    me = lax.axis_index("ctx")
    plan = []
    span = 1
    while span * 4 < count:
        plan.append([(span * i, span * i) for i in range(1, 4)])
        span *= 4
    plan.append([(1 + span * i, span * i) for i in range(count // span)])
    barrier = pltpu.get_barrier_semaphore()
    partners = sorted({shift for sends in plan for shift, _ in sends})
    for shift in partners:
        for other in (me + shift, me - shift):

            @pl.when(jnp.logical_and(other >= 0, other < count))
            def _():
                pl.semaphore_signal(
                    barrier, 1, device_id={"ctx": other}, device_id_type=pl.DeviceIdType.MESH
                )

    peers = 0
    for shift in partners:
        peers = peers + (1 - (me + shift) // count) + (me - shift + count) // count
    pl.semaphore_wait(barrier, peers)

    out_ref[...] = f_ref[...]
    for k, sends in enumerate(plan):
        send_ref[k] = out_ref[...].astype(send_ref.dtype)
        last = k == len(plan) - 1
        if last:
            out_ref[...] = jnp.zeros_like(out_ref)
        copies = []
        for i, (shift, power) in enumerate(sends):
            copy = pltpu.make_async_remote_copy(
                src_ref=send_ref.at[k],
                dst_ref=recv_ref.at[k, i],
                send_sem=send_sem.at[k, i],
                recv_sem=recv_sem.at[k, i],
                device_id={"ctx": me + shift},
                device_id_type=pl.DeviceIdType.MESH,
            )
            copies.append((shift, power, copy))

            @pl.when(me + shift < count)
            def _():
                copy.start()

        for i, (shift, power, copy) in enumerate(copies):

            @pl.when(me >= shift)
            def _():
                copy.wait_recv()
                if power == 0:
                    out_ref[...] = out_ref[...] + recv_ref[k, i].astype(jnp.float32)
                else:
                    factor = jnp.exp(r_ref[...] * (-1.0 * rows * power))
                    out_ref[...] = out_ref[...] + factor * recv_ref[k, i].astype(jnp.float32)

        for shift, power, copy in copies:

            @pl.when(me + shift < count)
            def _():
                copy.wait_send()


def scan_call(final_state, decay_rates, count, rows):
    shape = final_state.shape
    return pl.pallas_call(
        functools.partial(scan_kernel, count, rows),
        in_specs=[pl.BlockSpec(memory_space=pltpu.VMEM)] * 2,
        out_specs=pl.BlockSpec(memory_space=pltpu.VMEM),
        out_shape=jax.ShapeDtypeStruct(shape, jnp.float32),
        scratch_shapes=[
            pltpu.VMEM((3,) + shape, jnp.bfloat16),
            pltpu.VMEM((3, 4) + shape, jnp.bfloat16),
            pltpu.SemaphoreType.DMA((3, 4)),
            pltpu.SemaphoreType.DMA((3, 4)),
        ],
        compiler_params=pltpu.CompilerParams(collective_id=0, has_side_effects=True),
    )(final_state, decay_rates)


def passed_along(value, axis, steps):
    count = lax.axis_size(axis)
    first, last = (max(0, -steps), min(count, count - steps))
    return lax.ppermute(value, axis, [(source, source + steps) for source in range(first, last)])


def short_filter(extended, weights):
    return weights[0] * extended[2:] + weights[1] * extended[1:-1] + weights[2] * extended[:-2]


def medium_conv(extended, taps, row_count):
    tap_count = taps.shape[0]
    total = jnp.zeros((row_count, taps.shape[1]), jnp.float32)
    for offset in range(tap_count):
        start = tap_count - 1 - offset
        total = total + taps[offset] * extended[start : start + row_count]
    return total


def body(
    gate_medium,
    key_medium,
    value_medium,
    short_medium,
    filter_medium,
    skip_medium,
    norm_gain,
    gate_long,
    key_long,
    short_long,
    decay_rates,
    residues,
    skip_long,
):
    row_count = gate_medium.shape[0]
    tap_count = filter_medium.shape[0]
    width_local = gate_medium.shape[1]
    late_product = (
        short_filter(key_medium, short_medium[1]) * short_filter(value_medium, short_medium[2])
    ).astype(jnp.bfloat16)
    rim_gate, rim_key, rim_value, rim_product = passed_along(
        (gate_medium[-2:], key_medium[-2:], value_medium[-2:], late_product[-(tap_count - 1) :]),
        "ctx",
        1,
    )
    head_key = short_filter(jnp.concatenate([rim_key, key_medium[:2]], 0), short_medium[1])
    head_value = short_filter(jnp.concatenate([rim_value, value_medium[:2]], 0), short_medium[2])
    head_product = (head_key * head_value).astype(jnp.bfloat16)
    product = jnp.concatenate([rim_product, head_product, late_product], 0)
    gate_feat = short_filter(jnp.concatenate([rim_gate, gate_medium], 0), short_medium[0])
    extended = jnp.concatenate([jnp.zeros((1, width_local), jnp.bfloat16), product], 0)
    mixed_medium, partial_squares = medium_call(
        extended, filter_medium, skip_medium[None, :], gate_feat
    )
    squares = jnp.sum(partial_squares, axis=1)
    ring = lax.axis_size("ch")
    total_squares = squares
    for shift in range(1, ring):
        total_squares = total_squares + lax.ppermute(
            squares, "ch", [(source, (source + shift) % ring) for source in range(ring)]
        )
    inverse = lax.rsqrt(total_squares / D + 1e-06)
    normed = (mixed_medium * norm_gain * inverse[:, None]).astype(jnp.bfloat16)
    rim_gate_long, rim_key_long, rim_normed = passed_along(
        (gate_long[-2:], key_long[-2:], normed[-2:]), "ctx", 1
    )
    gate_feat_long = short_filter(jnp.concatenate([rim_gate_long, gate_long], 0), short_long[0])
    key_feat_long = short_filter(jnp.concatenate([rim_key_long, key_long], 0), short_long[1])
    value_feat_long = short_filter(jnp.concatenate([rim_normed, normed], 0), short_long[2])
    product_long = (key_feat_long * value_feat_long).astype(jnp.bfloat16)
    mode_weight = residues * jnp.sqrt(-jnp.expm1(-2.0 * decay_rates))
    step_decay = jnp.exp(-decay_rates)
    final_state = modal_end_call(product_long, step_decay)
    incoming = scan_call(final_state, decay_rates, lax.axis_size("ctx"), row_count)
    mixed_long = modal_out_call(
        product_long, step_decay, mode_weight, incoming, skip_long[None, :], gate_feat_long
    )
    return (mixed_medium, mixed_long)


def solution(mesh):
    placed = (
        P("ctx", "ch"),
        P("ctx", "ch"),
        P("ctx", "ch"),
        P(None, None, "ch"),
        P(None, "ch"),
        P("ch"),
        P("ch"),
        P("ctx", "ch"),
        P("ctx", "ch"),
        P(None, None, "ch"),
        P(None, "ch"),
        P(None, "ch"),
        P("ch"),
    )
    return jax.shard_map(
        body,
        mesh=mesh,
        in_specs=placed,
        out_specs=(P("ctx", "ch"), P("ctx", "ch")),
        check_vma=False,
    )
```
